32 devices in a mesh: dp: 8 (over z, x), tensor: 4 (over y, core).
Axes of the slice: x: 2, y: 2, z: 4, core: 2. Of those that a mesh axis runs over, the one named last changes fastest.
Arguments:
- tokens: bfloat16 [4096, 768], P(('dp', 'tensor')), may hold values from -6 to 6
- attn_gain: bfloat16 [768], P('dp'), may hold values from 0.25 to 1.75
- w_qkv: bfloat16 [3, 768, 768], P(None, 'dp', 'tensor'), may hold values from -14.072913 to 14.072913
- w_out: bfloat16 [768, 768], P('tensor', 'dp'), may hold values from -3 to 3
- mlp_gain: bfloat16 [768], P('dp'), may hold values from 0.25 to 1.75
- w_in: bfloat16 [2, 768, 1152], P(None, 'dp', 'tensor'), may hold values from -0.21875 to 0.21875
- w_down: bfloat16 [1152, 768], P('tensor', 'dp'), may hold values from -0.1875 to 0.1875
- cotangent: bfloat16 [4096, 768], P(('dp', 'tensor')), may hold values from -6 to 6
Outputs:
- out: bfloat16 [4096, 768], P(('dp', 'tensor'))
- input_grad: float32 [4096, 768], P(('dp', 'tensor'))
- attn_gain_grad: float32 [768], P('dp')
- w_qkv_grad: float32 [3, 768, 768], P(None, 'dp', 'tensor')
- w_out_grad: float32 [768, 768], P('tensor', 'dp')
- mlp_gain_grad: float32 [768], P('dp')
- w_in_grad: float32 [2, 768, 1152], P(None, 'dp', 'tensor')
- w_down_grad: float32 [1152, 768], P('tensor', 'dp')
The draws below stay inside these ranges and needn't reach their ends.
All inputs are finite; a program needn't handle non-finite values.
Results may differ from the reference program's by a relative error of at most 0.013.
Values may be sent and summed in bfloat16 or wider, within the bound.
A program may use at most 64 MiB of HBM per device.

```python
import jax
import jax.numpy as jnp
from jax import lax

D = 768
H = 12
HD = 64
FF = 1152
L = 512
TOKENS = 4096


def draw_w_qkv(key, part):
    first_key = jax.random.fold_in(key, 0)
    normal_part = jnp.clip(jax.random.normal(first_key, (3, D, D), jnp.float32), -6.0, 6.0) * D ** (-0.5)
    return normal_part.astype(jnp.bfloat16)


def raised(entries, rng, source, target, shards_of, factor):
    owner, partner = [(jnp.arange(entries.shape[dim]) // (entries.shape[dim] // shards_of)).reshape([-1 if axis == dim else 1 for axis in range(entries.ndim)]) for dim in (source, target)]
    chosen = jax.random.permutation(rng, shards_of)[partner]
    strong = (owner == chosen) | (owner == (partner + shards_of // 2) % shards_of)
    return jnp.where(strong, factor * entries, entries)


def level_of(rng, shape, pieces, smallest, largest):
    gain = 1.0
    for dim, parts in pieces:
        draws = jax.random.uniform(jax.random.fold_in(jax.random.fold_in(rng, 6), dim), (parts,), jnp.float32, smallest / len(pieces), largest / len(pieces))
        gain = gain * jnp.repeat(jnp.exp(draws), shape[dim] // parts).reshape((-1,) + (1,) * (len(shape) - 1 - dim))
    return gain


def gaussian(own_key, extent, width, limit, shards=(), dtype=jnp.bfloat16):
    values = width * jax.random.normal(own_key, extent, jnp.float32)
    if shards:
        values = values * level_of(own_key, extent, shards, -0.22, 0.18)
    return jnp.clip(values, -limit, limit).astype(dtype)


def heavy_noise(key, dims, scale, reach, cuts, heavy, kind=jnp.bfloat16):
    drawn = scale * jax.random.normal(key, dims, jnp.float32)
    if cuts:
        drawn = drawn * level_of(key, dims, cuts, -0.22, 0.18)
    return jnp.clip(raised(drawn, jax.random.fold_in(key, 3), *heavy), -reach, reach).astype(kind)


def setup_inputs(seed: int = 0) -> dict:
    key_of = jax.random.split(jax.random.key(seed), 9)
    tokens = heavy_noise(key_of[0], (TOKENS, D), 1.0, 6.0, ((0, 32),), (0, 1, 32, 2.75))
    attn_gain = jnp.clip(1.0 + 0.15 * jax.random.normal(key_of[1], (D,), jnp.float32), 0.25, 1.75).astype(jnp.bfloat16)
    w_qkv = draw_w_qkv(jax.random.fold_in(key_of[8], 71), 0)
    w_out = gaussian(key_of[3], (D, D), (max(D // 192, 1)) ** -0.5, 3.0, ((0, 4), (1, 8)))
    mlp_gain = jnp.clip(1.0 + 0.15 * jax.random.normal(key_of[4], (D,), jnp.float32), 0.25, 1.75).astype(jnp.bfloat16)
    w_in = gaussian(key_of[5], (2, D, FF), D ** -0.5, 0.21875, ((1, 8), (2, 4)))
    w_down = gaussian(key_of[6], (FF, D), FF ** -0.5, 0.1875, ((0, 4), (1, 8)))
    cotangent = heavy_noise(key_of[7], (TOKENS, D), 1.0, 6.0, ((0, 32),), (0, 1, 32, 2.75))
    return {"tokens": tokens, "attn_gain": attn_gain, "w_qkv": w_qkv, "w_out": w_out, "mlp_gain": mlp_gain, "w_in": w_in, "w_down": w_down, "cotangent": cotangent}


NORM_EPS = 1e-05
ROPE_THETA = 160000.0
SQRT_HALF = 0.7071067811865476
GAUSS_NORM = 0.3989422804014327

def widen_float(array):
    return lax.optimization_barrier(array).astype(jnp.float32)

def rope_tables(row_count):
    position = (jnp.arange(row_count) % L).astype(jnp.float32)
    halves = jnp.arange(HD // 2).astype(jnp.float32)
    inverse = ROPE_THETA ** (-2.0 * halves / HD)
    angles = position[:, None] * inverse[None, :]
    angles = jnp.concatenate([angles, angles], axis=1)
    return (jnp.cos(angles)[:, None, :], jnp.sin(angles)[:, None, :])

def rotate(field_rows, cos_table, sin_table):
    first_half = field_rows[..., :HD // 2]
    second_half = field_rows[..., HD // 2:]
    turned = jnp.concatenate([-second_half, first_half], axis=-1)
    return field_rows * cos_table + turned * sin_table

def rotate_back(grad_field, cos_table, sin_table):
    scaled = grad_field * sin_table
    turned = jnp.concatenate([scaled[..., HD // 2:], -scaled[..., :HD // 2]], axis=-1)
    return grad_field * cos_table + turned

def normalize(values):
    centred = values - lax.optimization_barrier(jnp.mean(values, axis=-1, keepdims=True))
    inv_std = lax.rsqrt(lax.optimization_barrier(jnp.mean(centred * centred, axis=-1, keepdims=True)) + NORM_EPS)
    return (centred * inv_std, inv_std)

def normalize_back(grad_norm, normed, inv_std, gain_row):
    gain_part = lax.optimization_barrier(jnp.sum(grad_norm * normed, axis=0))
    scaled = grad_norm * gain_row
    centred = scaled - lax.optimization_barrier(jnp.mean(scaled, axis=-1, keepdims=True))
    grad_in = inv_std * (centred - normed * lax.optimization_barrier(jnp.mean(scaled * normed, axis=-1, keepdims=True)))
    return (grad_in, gain_part)

def gelu_pair(inputs):
    normal_cdf = 0.5 * (1.0 + lax.erf(inputs * SQRT_HALF))
    return (inputs * normal_cdf, normal_cdf + inputs * jnp.exp(-0.5 * inputs * inputs) * GAUSS_NORM)

def attend(queries, key_rows, value_rows):
    score_scale = HD ** (-0.5)
    scores = jnp.einsum('qhd,khd->hqk', widen_float(queries), widen_float(key_rows)) * score_scale
    row_max = lax.optimization_barrier(jnp.max(scores, axis=-1, keepdims=True))
    log_total = row_max + jnp.log(lax.optimization_barrier(jnp.sum(jnp.exp(scores - row_max), axis=-1, keepdims=True)))
    weights = jnp.exp(scores - log_total).astype(jnp.bfloat16)
    attn_mix = jnp.einsum('hqk,khd->qhd', widen_float(weights), widen_float(value_rows)).astype(jnp.bfloat16)
    return (attn_mix, log_total)

def attend_back(queries, key_rows, value_rows, attn_mix, grad_mix, log_total):
    score_scale = HD ** (-0.5)
    scores = jnp.einsum('qhd,khd->hqk', widen_float(queries), widen_float(key_rows)) * score_scale
    probabilities = jnp.exp(scores - log_total)
    grad_probs = jnp.einsum('qhd,khd->hqk', widen_float(grad_mix), widen_float(value_rows))
    row_delta = lax.optimization_barrier(jnp.sum(widen_float(grad_mix) * widen_float(attn_mix), axis=-1))
    grad_scores = (probabilities * (grad_probs - jnp.transpose(row_delta)[:, :, None])).astype(jnp.bfloat16)
    prob_rounded = probabilities.astype(jnp.bfloat16)
    grad_values = jnp.einsum('hqk,qhd->khd', widen_float(prob_rounded), widen_float(grad_mix))
    grad_queries = jnp.einsum('hqk,khd->qhd', widen_float(grad_scores), widen_float(key_rows)) * score_scale
    grad_keys = jnp.einsum('hqk,qhd->khd', widen_float(grad_scores), widen_float(queries)) * score_scale
    return (grad_queries, grad_keys, grad_values)

def one_sequence(params, tok_rows, cot_rows, cos_table, sin_table):
    attn_gain, w_qkv, w_out, mlp_gain, w_in, w_down = params
    head_shape = (L, H, HD)
    residual = tok_rows.astype(jnp.float32)
    normed_one, inv_one = normalize(residual)
    ln_one = (normed_one * attn_gain.astype(jnp.float32)).astype(jnp.bfloat16)
    projections = [jnp.dot(ln_one, w_qkv[which], preferred_element_type=jnp.float32) for which in range(3)]
    queries = rotate(projections[0].reshape(head_shape), cos_table, sin_table).astype(jnp.bfloat16)
    key_rows = rotate(projections[1].reshape(head_shape), cos_table, sin_table).astype(jnp.bfloat16)
    value_rows = projections[2].reshape(head_shape).astype(jnp.bfloat16)
    attn_mix, log_total = attend(queries, key_rows, value_rows)
    mixed_rows = attn_mix.reshape(L, D)
    hidden_res = residual + jnp.dot(mixed_rows, w_out, preferred_element_type=jnp.float32)
    normed_two, inv_two = normalize(hidden_res)
    ln_two = (normed_two * mlp_gain.astype(jnp.float32)).astype(jnp.bfloat16)
    input_part = jnp.dot(ln_two, w_in[0], preferred_element_type=jnp.float32)
    gate_part = jnp.dot(ln_two, w_in[1], preferred_element_type=jnp.float32)
    activated, gelu_slope = gelu_pair(input_part)
    hidden_act = (activated * gate_part).astype(jnp.bfloat16)
    output = (hidden_res + jnp.dot(hidden_act, w_down, preferred_element_type=jnp.float32)).astype(jnp.bfloat16)
    grad_down = jnp.dot(hidden_act.T, cot_rows, preferred_element_type=jnp.float32)
    grad_act = jnp.dot(cot_rows, w_down.T, preferred_element_type=jnp.float32)
    grad_input_part = (grad_act * gate_part * gelu_slope).astype(jnp.bfloat16)
    grad_gate_part = (grad_act * activated).astype(jnp.bfloat16)
    grad_in = jnp.stack([jnp.dot(ln_two.T, grad_input_part, preferred_element_type=jnp.float32), jnp.dot(ln_two.T, grad_gate_part, preferred_element_type=jnp.float32)])
    grad_ln_two = jnp.dot(grad_input_part, w_in[0].T, preferred_element_type=jnp.float32) + jnp.dot(grad_gate_part, w_in[1].T, preferred_element_type=jnp.float32)
    grad_res_two, mlp_gain_part = normalize_back(grad_ln_two, normed_two, inv_two, mlp_gain.astype(jnp.float32))
    grad_hidden = cot_rows.astype(jnp.float32) + grad_res_two
    grad_hidden_bf = grad_hidden.astype(jnp.bfloat16)
    grad_out = jnp.dot(mixed_rows.T, grad_hidden_bf, preferred_element_type=jnp.float32)
    grad_mix = jnp.dot(grad_hidden_bf, w_out.T, preferred_element_type=jnp.float32).astype(jnp.bfloat16).reshape(head_shape)
    grad_q, grad_k, grad_v = attend_back(queries, key_rows, value_rows, attn_mix, grad_mix, log_total)
    grad_proj = [rotate_back(grad_q, cos_table, sin_table).reshape(L, D).astype(jnp.bfloat16), rotate_back(grad_k, cos_table, sin_table).reshape(L, D).astype(jnp.bfloat16), grad_v.reshape(L, D).astype(jnp.bfloat16)]
    grad_qkv = jnp.stack([jnp.dot(ln_one.T, grad_proj[which], preferred_element_type=jnp.float32) for which in range(3)])
    grad_ln_one = jnp.dot(grad_proj[0], w_qkv[0].T, preferred_element_type=jnp.float32)
    grad_ln_one = grad_ln_one + jnp.dot(grad_proj[1], w_qkv[1].T, preferred_element_type=jnp.float32)
    grad_ln_one = grad_ln_one + jnp.dot(grad_proj[2], w_qkv[2].T, preferred_element_type=jnp.float32)
    grad_res_one, attn_gain_part = normalize_back(grad_ln_one, normed_one, inv_one, attn_gain.astype(jnp.float32))
    input_grad = grad_hidden + grad_res_one
    return (output, input_grad, (attn_gain_part, grad_qkv, grad_out, mlp_gain_part, grad_in, grad_down))

def reference(tokens, attn_gain, w_qkv, w_out, mlp_gain, w_in, w_down, cotangent):
    seq_count = tokens.shape[0] // L
    cos_table, sin_table = rope_tables(L)
    params = (attn_gain, w_qkv, w_out, mlp_gain, w_in, w_down)

    def one_step(totals, seq_pair):
        tok_rows, cot_rows = seq_pair
        output, input_grad, seq_grads = one_sequence(params, tok_rows, cot_rows, cos_table, sin_table)
        return (jax.tree.map(lambda left, right: left + right, totals, seq_grads), (output, input_grad))
    zero_grads = (jnp.zeros((D,), jnp.float32), jnp.zeros((3, D, D), jnp.float32), jnp.zeros((D, D), jnp.float32), jnp.zeros((D,), jnp.float32), jnp.zeros((2, D, FF), jnp.float32), jnp.zeros((FF, D), jnp.float32))
    totals, (outputs, input_grads) = lax.scan(one_step, zero_grads, (tokens.reshape(seq_count, L, D), cotangent.reshape(seq_count, L, D)))
    return (outputs.reshape(seq_count * L, D), input_grads.reshape(seq_count * L, D), totals[0], totals[1], totals[2], totals[3], totals[4], totals[5])
```

```python
import functools

import jax
import jax.numpy as jnp
import numpy as np
from jax import lax
from jax.experimental import pallas as pl
from jax.experimental.pallas import tpu as pltpu
from jax.experimental.layout import Layout, with_layout_constraint
from jax.sharding import PartitionSpec as P

HD = 64
L = 512


NORM_EPS = 1e-05
ROPE_THETA = 160000.0
SQRT_HALF = 0.7071067811865476
GAUSS_NORM = 0.3989422804014327


def rope_tables(row_count):
    position = (jnp.arange(row_count) % L).astype(jnp.float32)
    halves = jnp.arange(HD // 2).astype(jnp.float32)
    inverse = ROPE_THETA ** (-2.0 * halves / HD)
    angles = position[:, None] * inverse[None, :]
    angles = jnp.concatenate([angles, angles], axis=1)
    return (jnp.cos(angles)[:, None, :], jnp.sin(angles)[:, None, :])


def rotate(field_rows, cos_table, sin_table):
    first_half = field_rows[..., : HD // 2]
    second_half = field_rows[..., HD // 2 :]
    turned = jnp.concatenate([-second_half, first_half], axis=-1)
    return field_rows * cos_table + turned * sin_table


def rotate_back(grad_field, cos_table, sin_table):
    scaled = grad_field * sin_table
    turned = jnp.concatenate([scaled[..., HD // 2 :], -scaled[..., : HD // 2]], axis=-1)
    return grad_field * cos_table + turned


def normalize(values):
    centred = values - jnp.mean(values, axis=-1, keepdims=True)
    inv_std = lax.rsqrt(jnp.mean(centred * centred, axis=-1, keepdims=True) + NORM_EPS)
    return (centred * inv_std, inv_std)


def normalize_back(grad_norm, normed, inv_std, gain_row):
    gain_part = jnp.sum(grad_norm * normed, axis=0)
    scaled = grad_norm * gain_row
    centred = scaled - jnp.mean(scaled, axis=-1, keepdims=True)
    grad_in = inv_std * (centred - normed * jnp.mean(scaled * normed, axis=-1, keepdims=True))
    return (grad_in, gain_part)


def gelu_pair(inputs):
    normal_cdf = 0.5 * (1.0 + lax.erf(inputs * SQRT_HALF))
    return (inputs * normal_cdf, normal_cdf + inputs * jnp.exp(-0.5 * inputs * inputs) * GAUSS_NORM)


def attend(queries, key_rows, value_rows):
    score_scale = HD ** (-0.5)
    scores = (
        jnp.einsum("qhd,khd->hqk", queries, key_rows, preferred_element_type=jnp.float32)
        * score_scale
    )
    row_max = jnp.max(scores, axis=-1, keepdims=True)
    log_total = row_max + jnp.log(jnp.sum(jnp.exp(scores - row_max), axis=-1, keepdims=True))
    weights = jnp.exp(scores - log_total).astype(jnp.bfloat16)
    attn_mix = jnp.einsum(
        "hqk,khd->qhd", weights, value_rows, preferred_element_type=jnp.float32
    ).astype(jnp.bfloat16)
    return (attn_mix, log_total)


def attend_back(queries, key_rows, value_rows, attn_mix, grad_mix, log_total):
    score_scale = HD ** (-0.5)
    scores = (
        jnp.einsum("qhd,khd->hqk", queries, key_rows, preferred_element_type=jnp.float32)
        * score_scale
    )
    probabilities = jnp.exp(scores - log_total)
    grad_probs = jnp.einsum(
        "qhd,khd->hqk", grad_mix, value_rows, preferred_element_type=jnp.float32
    )
    row_delta = jnp.sum(grad_mix.astype(jnp.float32) * attn_mix.astype(jnp.float32), axis=-1)
    grad_scores = (probabilities * (grad_probs - jnp.transpose(row_delta)[:, :, None])).astype(
        jnp.bfloat16
    )
    prob_rounded = probabilities.astype(jnp.bfloat16)
    grad_values = jnp.einsum(
        "hqk,qhd->khd", prob_rounded, grad_mix, preferred_element_type=jnp.float32
    )
    grad_queries = (
        jnp.einsum("hqk,khd->qhd", grad_scores, key_rows, preferred_element_type=jnp.float32)
        * score_scale
    )
    grad_keys = (
        jnp.einsum("hqk,qhd->khd", grad_scores, queries, preferred_element_type=jnp.float32)
        * score_scale
    )
    return (grad_queries, grad_keys, grad_values)


def exchange_kernel(plan, sizes, *refs):
    count = len(plan)
    sources, targets = refs[:count], refs[count : 2 * count]
    own_sem, send_sem, recv_sem = refs[2 * count :]
    axes = sorted({axis for _, axis, _ in plan})
    barrier = pltpu.get_barrier_semaphore()
    total = 0
    for axis in axes:
        me = lax.axis_index(axis)
        for shift in range(1, sizes[axis]):
            pl.semaphore_signal(
                barrier,
                inc=1,
                device_id={axis: lax.rem(me + shift, sizes[axis])},
                device_id_type=pl.DeviceIdType.MESH,
            )
            total += 1
    pl.semaphore_wait(barrier, total)
    slot = 0
    pending, relays, local = [], [], []

    def remote(source, target, axis, peer, index):
        return pltpu.make_async_remote_copy(
            src_ref=source,
            dst_ref=target,
            send_sem=send_sem.at[index],
            recv_sem=recv_sem.at[index],
            device_id={axis: peer},
            device_id_type=pl.DeviceIdType.MESH,
        )

    for which, (kind, axis, span) in enumerate(plan):
        size = sizes[axis]
        me = lax.axis_index(axis)
        source, target = sources[which], targets[which]
        outer = size // 2
        column = lax.rem(me, 2)
        row = me // 2
        partner = row * 2 + 1 - column
        if kind == "half":
            copy = remote(source.at[:, 1 - column, :, span], target, axis, partner, slot)
            copy.start()
            pending.append(copy)
            slot += 1
            continue
        if kind == "outer":
            for shift in range(1, outer):
                other = lax.rem(row + shift, outer)
                copy = remote(source.at[other], target.at[row], axis, other * 2 + column, slot)
                copy.start()
                pending.append(copy)
                slot += 1
            copy = pltpu.make_async_copy(source.at[row], target.at[row], own_sem.at[which])
            copy.start()
            local.append(copy)
            continue
        if kind == "relay":
            for shift in range(1, outer):
                peer = lax.rem(row + shift, outer) * 2 + column
                copy = remote(source, target.at[me], axis, peer, slot)
                copy.start()
                origin = lax.rem(row + outer - shift, outer) * 2 + column
                relays.append((copy, target, axis, origin, partner, slot + 1))
                slot += 2
            copy = remote(source, target.at[me], axis, partner, slot)
            copy.start()
            pending.append(copy)
            slot += 1
        else:
            for shift in range(1, size):
                peer = lax.rem(me + shift, size)
                piece = source if kind == "gather" else source.at[peer, :, span]
                copy = remote(piece, target.at[me], axis, peer, slot)
                copy.start()
                pending.append(copy)
                slot += 1
        piece = source if kind != "scatter" else source.at[me, :, span]
        copy = pltpu.make_async_copy(piece, target.at[me], own_sem.at[which])
        copy.start()
        local.append(copy)
    for copy, target, axis, origin, partner, index in relays:
        copy.wait_recv()
        onward = remote(target.at[origin], target.at[origin], axis, partner, index)
        onward.start()
        pending.append(onward)
    for copy, *_ in relays:
        copy.wait_send()
    for copy in pending + local:
        copy.wait()


def slots_of(kind, size):
    outer = size // 2
    return {"relay": 2 * outer - 1, "half": 1, "outer": outer - 1}.get(kind, size - 1)


def shape_of(kind, size, shape, wide):
    if kind == "half":
        return (shape[0], shape[2], wide)
    return {"scatter": shape[:-1] + (wide,), "outer": shape}.get(kind, (size,) + shape)


def exchange(sizes, number, *ops):
    arrays = [op[2] for op in ops]
    spans = [slice(*op[3]) if len(op) > 3 else slice(0, op[2].shape[-1]) for op in ops]
    plan = tuple((op[0], op[1], span) for op, span in zip(ops, spans))
    shapes = [
        jax.ShapeDtypeStruct(
            shape_of(kind, sizes[axis], array.shape, span.stop - span.start), array.dtype
        )
        for (kind, axis, span), array in zip(plan, arrays)
    ]
    slots = sum(slots_of(kind, sizes[axis]) for kind, axis, _ in plan)
    return pl.pallas_call(
        functools.partial(exchange_kernel, plan, sizes),
        out_shape=shapes,
        in_specs=[pl.BlockSpec(memory_space=pltpu.VMEM)] * len(arrays),
        out_specs=[pl.BlockSpec(memory_space=pltpu.VMEM)] * len(arrays),
        scratch_shapes=[
            pltpu.SemaphoreType.DMA((len(arrays),)),
            pltpu.SemaphoreType.DMA((slots,)),
            pltpu.SemaphoreType.DMA((slots,)),
        ],
        compiler_params=pltpu.CompilerParams(
            collective_id=number, has_side_effects=True, vmem_limit_bytes=48 << 20
        ),
    )(*arrays)


def pad_columns(array, multiple=128):
    extra = -array.shape[-1] % multiple
    return jnp.pad(array, [(0, 0)] * (array.ndim - 1) + [(0, extra)])


def total_of(pieces):
    return jnp.sum(pieces.astype(jnp.float32), axis=0)


def row_major(array):
    return with_layout_constraint(array, Layout(major_to_minor=(0, 1)))


def dot_f32(left, right, left_dim, right_dim):
    return lax.dot_general(
        left, right, (((left_dim,), (right_dim,)), ((), ())), preferred_element_type=jnp.float32
    )


def feed_forward_kernel(
    hidden, rows_ref, up_ref, gate_ref, down_ref, cot_ref, mlp_ref, back_ref, grads_ref
):
    bf16 = jnp.bfloat16
    rows, cot = rows_ref[...], cot_ref[...]
    inputs = dot_f32(rows, up_ref[...], 1, 0)
    gate_part = dot_f32(rows, gate_ref[...], 1, 0)
    activated, gelu_slope = gelu_pair(inputs)
    hidden_act = (activated * gate_part).astype(bf16)
    mlp_ref[...] = dot_f32(hidden_act, down_ref[...], 1, 1).astype(bf16)
    grad_act = dot_f32(cot, down_ref[...], 1, 0)
    grad_up = (grad_act * gate_part * gelu_slope).astype(bf16)
    grad_gate = (grad_act * activated).astype(bf16)
    back_ref[...] = (
        dot_f32(grad_up, up_ref[...], 1, 1) + dot_f32(grad_gate, gate_ref[...], 1, 1)
    ).astype(bf16)
    grads_ref[:, :hidden] = dot_f32(rows, grad_up, 0, 0).astype(bf16)
    grads_ref[:, hidden : 2 * hidden] = dot_f32(rows, grad_gate, 0, 0).astype(bf16)
    grads_ref[:, 2 * hidden : 3 * hidden] = dot_f32(cot, hidden_act, 0, 0).astype(bf16)
    spare = grads_ref.shape[1] - 3 * hidden
    if spare:
        grads_ref[:, 3 * hidden :] = jnp.zeros((grads_ref.shape[0], spare), bf16)


def feed_forward(hidden, rows, up, gate, down_t, cot):
    row_count, width = rows.shape
    padded = -(-3 * hidden // 128) * 128
    return pl.pallas_call(
        functools.partial(feed_forward_kernel, hidden),
        out_shape=[
            jax.ShapeDtypeStruct((row_count, width), jnp.bfloat16),
            jax.ShapeDtypeStruct((row_count, width), jnp.bfloat16),
            jax.ShapeDtypeStruct((width, padded), jnp.bfloat16),
        ],
        in_specs=[pl.BlockSpec(memory_space=pltpu.VMEM)] * 5,
        out_specs=[pl.BlockSpec(memory_space=pltpu.VMEM)] * 3,
        compiler_params=pltpu.CompilerParams(vmem_limit_bytes=48 << 20),
    )(rows, up, gate, down_t, cot)


def body(sizes, tokens, attn_gain, w_qkv, w_out, mlp_gain, w_in, w_down, cotangent):
    bf16, f32 = jnp.bfloat16, jnp.float32
    groups, members = sizes["dp"], sizes["tensor"]
    block = w_qkv.shape[1]
    width = block * groups
    heads_wide, hidden = w_qkv.shape[2], w_in.shape[2]
    own_rows = tokens.shape[0]
    packed = jnp.concatenate([w_qkv[0], w_qkv[1], w_qkv[2], w_out.T], axis=1)
    gain_tile = jnp.pad(jnp.stack([attn_gain, mlp_gain]), [(0, 14), (0, -block % 128)])
    weights, gain_tiles, token_rows, grad_rows = exchange(
        sizes,
        0,
        ("relay", "dp", packed),
        ("relay", "dp", gain_tile),
        ("relay", "tensor", tokens),
        ("relay", "tensor", cotangent),
    )
    weights = weights.reshape(width, -1)
    qkv_weight = weights[:, : 3 * heads_wide]
    out_weight_t = weights[:, 3 * heads_wide :]
    attn_full = gain_tiles[:, 0, :block].reshape(1, width).astype(f32)
    mlp_full = gain_tiles[:, 1, :block].reshape(1, width).astype(f32)
    outer = groups // 2
    column = lax.rem(lax.axis_index("dp"), 2)

    def quarter(array):
        return array.reshape(outer, 2, block, -1)

    def half_sum(array, received, low, high):
        own = lax.dynamic_index_in_dim(quarter(array)[..., low:high], column, 1, keepdims=False)
        return (own.astype(f32) + received.astype(f32)).astype(bf16)

    row_count = own_rows * members
    grad_rows = grad_rows.reshape(row_count, width)
    residual = tokens.astype(f32)
    normed_one, inv_one = normalize(residual)
    rows_one = (normalize(token_rows.reshape(row_count, width).astype(f32))[0] * attn_full).astype(bf16)
    head_count = heads_wide // HD
    head_shape = (row_count, head_count, HD)
    seq_shape = (row_count // L, L, head_count, HD)
    flat_shape = (row_count, heads_wide)
    cos_table, sin_table = rope_tables(row_count)
    projected = dot_f32(rows_one, qkv_weight, 1, 0)
    pieces = [projected[:, i * heads_wide : (i + 1) * heads_wide].reshape(head_shape) for i in range(3)]
    queries = rotate(pieces[0], cos_table, sin_table).astype(bf16).reshape(seq_shape)
    key_rows = rotate(pieces[1], cos_table, sin_table).astype(bf16).reshape(seq_shape)
    value_rows = pieces[2].astype(bf16).reshape(seq_shape)
    one_seq = row_count == L

    def over_sequences(function, arrays):
        if one_seq:
            results = function(*[array[0] for array in arrays])
            return tuple(result[None] for result in results)
        return lax.map(lambda seq_block: function(*seq_block), arrays)

    attn_mix, log_total = over_sequences(attend, (queries, key_rows, value_rows))
    mixed_rows = attn_mix.reshape(flat_shape)
    attn_part = dot_f32(mixed_rows, out_weight_t, 1, 1).astype(bf16)
    attn_parts, up_weight, down_weight_t = exchange(
        sizes,
        1,
        ("scatter", "tensor", attn_part.reshape(members, own_rows, width)),
        ("relay", "dp", w_in[0]),
        ("relay", "dp", w_down.T),
    )
    up_weight = up_weight.reshape(width, -1)
    down_weight_t = down_weight_t.reshape(width, -1)
    hidden_res = residual + total_of(attn_parts)
    normed_two, inv_two = normalize(hidden_res)
    ln_two = (normed_two * mlp_full).astype(bf16)
    rows_two, gate_weight = exchange(
        sizes, 2, ("relay", "tensor", ln_two), ("relay", "dp", w_in[1])
    )
    gate_weight = gate_weight.reshape(width, -1)
    rows_two = rows_two.reshape(row_count, width)
    mlp_part, ln_two_part, mlp_grads = feed_forward(
        hidden, rows_two, up_weight, gate_weight, down_weight_t, grad_rows
    )
    mlp_wide = mlp_grads.shape[-1]
    first = mlp_wide // 256 * 128
    ln_two_parts, mlp_grads_a = exchange(
        sizes,
        3,
        ("scatter", "tensor", ln_two_part.reshape(members, own_rows, width)),
        ("half", "dp", quarter(mlp_grads), (0, first)),
    )
    grad_res_two, mlp_gain_part = normalize_back(total_of(ln_two_parts), normed_two, inv_two, mlp_full)
    grad_hidden = cotangent.astype(f32) + grad_res_two
    grad_hidden_rows, mlp_grads_b, mlp_sums_a = exchange(
        sizes,
        4,
        ("relay", "tensor", grad_hidden.astype(bf16)),
        ("half", "dp", quarter(mlp_grads), (first, mlp_wide)),
        ("outer", "dp", half_sum(mlp_grads, mlp_grads_a, 0, first)),
    )
    grad_hidden_rows = grad_hidden_rows.reshape(row_count, width)
    grad_out_t = row_major(dot_f32(grad_hidden_rows, mixed_rows, 0, 0).astype(bf16))
    grad_mix = dot_f32(grad_hidden_rows, out_weight_t, 1, 0).astype(bf16).reshape(seq_shape)
    grad_q, grad_k, grad_v = over_sequences(
        attend_back, (queries, key_rows, value_rows, attn_mix, grad_mix, log_total)
    )
    grad_proj = jnp.concatenate(
        [
            rotate_back(grad_q.reshape(head_shape), cos_table, sin_table).reshape(flat_shape),
            rotate_back(grad_k.reshape(head_shape), cos_table, sin_table).reshape(flat_shape),
            grad_v.reshape(flat_shape),
        ],
        axis=1,
    ).astype(bf16)
    grad_qkv = row_major(dot_f32(rows_one, grad_proj, 0, 0).astype(bf16))
    ln_one_part = dot_f32(grad_proj, qkv_weight, 1, 1).astype(bf16)
    ln_one_parts, mlp_sums_b, grad_out_half, qkv_half = exchange(
        sizes,
        5,
        ("scatter", "tensor", ln_one_part.reshape(members, own_rows, width)),
        ("outer", "dp", half_sum(mlp_grads, mlp_grads_b, first, mlp_wide)),
        ("half", "dp", quarter(grad_out_t)),
        ("half", "dp", quarter(grad_qkv)),
    )
    grad_res_one, attn_gain_part = normalize_back(total_of(ln_one_parts), normed_one, inv_one, attn_full)
    input_grad = grad_hidden + grad_res_one
    gain_parts = jnp.stack([attn_gain_part, mlp_gain_part] + [jnp.zeros_like(attn_gain_part)] * 6)
    gain_parts = pad_columns(jnp.swapaxes(gain_parts.reshape(8, groups, block), 0, 1))
    late_parts, gain_parts, mlp_parts, grad_out_parts = exchange(
        sizes,
        6,
        ("outer", "dp", half_sum(grad_qkv, qkv_half, 0, 3 * heads_wide)),
        ("scatter", "dp", gain_parts),
        ("scatter", "tensor", mlp_part.reshape(members, own_rows, width)),
        ("outer", "dp", half_sum(grad_out_t, grad_out_half, 0, heads_wide)),
    )
    output = (hidden_res + total_of(mlp_parts)).astype(bf16)
    (gain_groups,) = exchange(sizes, 7, ("gather", "tensor", total_of(gain_parts)))
    gain_sum = total_of(gain_groups)
    late = total_of(late_parts)
    grad_w_qkv = jnp.stack([late[:, i * heads_wide : (i + 1) * heads_wide] for i in range(3)])
    grad_w_out = total_of(grad_out_parts).T
    mlp_sums = jnp.concatenate(
        [total_of(mlp_sums_a), total_of(mlp_sums_b)], axis=1
    )
    grad_w_in = jnp.stack([mlp_sums[:, :hidden], mlp_sums[:, hidden : 2 * hidden]])
    grad_w_down = mlp_sums[:, 2 * hidden : 3 * hidden].T
    return (
        output,
        input_grad,
        gain_sum[0, :block],
        grad_w_qkv,
        grad_w_out,
        gain_sum[1, :block],
        grad_w_in,
        grad_w_down,
    )


def lanes(shape, dim):
    return lax.broadcasted_iota(jnp.int32, shape, dim)


def spread_matrix(head_count, turned, sign):
    shape = (head_count * HD, head_count * 2 * HD)
    row, column = lanes(shape, 0), lanes(shape, 1)
    head = lax.shift_right_logical(column, 7)
    feature = lax.bitwise_and(column, HD - 1)
    upper = lax.bitwise_and(column, 2 * HD - 1) >= HD
    plain = row == head * HD + feature
    if not turned:
        return jnp.where(plain & jnp.logical_not(upper), 1.0, 0.0).astype(jnp.bfloat16)
    other = row == head * HD + lax.bitwise_and(feature + HD // 2, HD - 1)
    signed = jnp.where(feature < HD // 2, -sign, sign)
    return jnp.where(
        upper, jnp.where(other, signed, 0.0), jnp.where(plain, 1.0, 0.0)
    ).astype(jnp.bfloat16)


def paired_matrix():
    shape = (2 * HD, 2 * HD)
    row, column = lanes(shape, 0), lanes(shape, 1)
    feature = lax.bitwise_and(column, HD - 1)
    upper = column >= HD
    other = row == lax.bitwise_and(feature + HD // 2, HD - 1)
    signed = jnp.where(feature < HD // 2, 1.0, -1.0)
    return jnp.where(
        upper, jnp.where(other, signed, 0.0), jnp.where(row == column, 1.0, 0.0)
    ).astype(jnp.bfloat16)


def layer_kernel(sizes, dims, *refs):
    bf16, f32 = jnp.bfloat16, jnp.float32
    groups, members = sizes["dp"], sizes["tensor"]
    own_rows, width, block, heads_wide, hidden, pad_hidden = dims
    head_count = heads_wide // HD
    spread = 2 * heads_wide
    row_count = own_rows * members
    outer, rings = groups // 2, members // 2
    (
        tok_in, cot_in, qkv_in, out_in, up_in, down_in, attn_in, mlp_in, table_in,
        output_ref, input_grad_ref, gain_ref, qkv_grad_ref, out_grad_ref, mlp_grad_ref,
        tok_buf, cot_buf, qkv_raw, out_raw, up_raw, down_raw, attn_raw, mlp_raw, table,
        w_a, w_b, gain_buf, gain_rows, w_big, w_out_pad, up_w, gate_w, down_w,
        rows_one, probs, q_buf, k_buf, v_buf, mix_t, mix, mix_pack,
        part_one, recv_one, fwd_one, hidden_res, rows_two,
        act_buf, up_grad, gate_grad, part_two, recv_two, fwd_two,
        part_three, recv_three, fwd_three,
        mlp_grads, mlp_half, mlp_sum, mlp_parts,
        grad_hidden, grad_rows, out_grads, out_half, out_sum, out_parts,
        proj_grad, qkv_grads, qkv_half, qkv_sum, qkv_parts,
        part_four, recv_four, fwd_four, gain_send, gain_recv, gain_group,
        load_sem, send_sem, recv_sem,
    ) = refs
    me_d, me_t = lax.axis_index("dp"), lax.axis_index("tensor")
    zrow, col = me_d // 2, lax.rem(me_d, 2)
    x_peer = zrow * 2 + 1 - col
    yrow, core = me_t // 2, lax.rem(me_t, 2)
    c_peer = yrow * 2 + 1 - core
    counter = [0]
    sent = []

    def send(source, target, axis, peer):
        index = counter[0]
        counter[0] += 1
        copy = pltpu.make_async_remote_copy(
            src_ref=source,
            dst_ref=target,
            send_sem=send_sem.at[index],
            recv_sem=recv_sem.at[index],
            device_id={axis: peer},
            device_id_type=pl.DeviceIdType.MESH,
        )
        copy.start()
        sent.append(copy)
        return copy

    loads = [
        pltpu.make_async_copy(source, target, load_sem.at[index])
        for index, (source, target) in enumerate(
            [
                (qkv_in, qkv_raw), (out_in, out_raw), (attn_in, attn_raw), (mlp_in, mlp_raw),
                (tok_in, tok_buf.at[me_t]), (cot_in, cot_buf.at[me_t]),
                (up_in, up_raw), (down_in, down_raw), (table_in, table),
            ]
        )
    ]
    for load in loads:
        load.start()
    barrier = pltpu.get_barrier_semaphore()
    for axis, me in (("dp", me_d), ("tensor", me_t)):
        for shift in range(1, sizes[axis]):
            pl.semaphore_signal(
                barrier,
                inc=1,
                device_id={axis: lax.rem(me + shift, sizes[axis])},
                device_id_type=pl.DeviceIdType.MESH,
            )
    eye_heads = jnp.where(
        lanes((heads_wide, heads_wide), 0) == lanes((heads_wide, heads_wide), 1), 1.0, 0.0
    ).astype(bf16)
    eye_hidden = jnp.where(
        lanes((hidden, hidden), 0) == lanes((hidden, hidden), 1), 1.0, 0.0
    ).astype(bf16)
    for load in loads[:4]:
        load.wait()
    gain_buf[me_d] = jnp.zeros(gain_buf.shape[1:], bf16)
    gain_buf[me_d, 0:1, :block] = attn_raw[...]
    gain_buf[me_d, 8:9, :block] = mlp_raw[...]
    for which in range(3):
        w_a[me_d, :, which * heads_wide : (which + 1) * heads_wide] = qkv_raw[which]
    w_a[me_d, :, 3 * heads_wide :] = dot_f32(out_raw[...], eye_heads, 0, 0).astype(bf16)
    for load in loads[4:]:
        load.wait()
    for which in range(2):
        w_b[me_d, :, which * hidden : (which + 1) * hidden] = up_raw[which]
    w_b[me_d, :, 2 * hidden : 3 * hidden] = dot_f32(down_raw[...], eye_hidden, 0, 0).astype(bf16)
    if pad_hidden > 3 * hidden:
        w_b[me_d, :, 3 * hidden :] = jnp.zeros((block, pad_hidden - 3 * hidden), bf16)
    pl.semaphore_wait(barrier, groups + members - 2)

    def dp_spread(buffer):
        copies = []
        for shift in range(1, outer):
            peer = lax.rem(zrow + shift, outer) * 2 + col
            origin = lax.rem(zrow + outer - shift, outer) * 2 + col
            copies.append((send(buffer.at[me_d], buffer.at[me_d], "dp", peer), origin))
        return copies

    def dp_pair(buffer, origin):
        mirrored = origin // 2 * 2 + 1 - col
        return (send(buffer.at[origin], buffer.at[origin], "dp", x_peer), mirrored)

    def tensor_spread(buffer):
        copies = []
        for shift in range(1, rings):
            peer = lax.rem(yrow + shift, rings) * 2 + core
            origin = lax.rem(yrow + rings - shift, rings) * 2 + core
            copies.append((send(buffer.at[me_t], buffer.at[me_t], "tensor", peer), origin))
        near = send(buffer.at[me_t], buffer.at[me_t], "tensor", c_peer)
        return copies, near

    def tensor_relay(buffer, copies):
        onward = []
        for copy, origin in copies:
            copy.wait_recv()
            onward.append(send(buffer.at[origin], buffer.at[origin], "tensor", c_peer))
        return onward

    gain_z = dp_spread(gain_buf)
    gain_x = [dp_pair(gain_buf, me_d)]
    a_z = dp_spread(w_a)
    a_x = [dp_pair(w_a, me_d)]
    tok_y, tok_near = tensor_spread(tok_buf)
    cot_y, cot_near = tensor_spread(cot_buf)
    b_z = dp_spread(w_b)

    turn = spread_matrix(head_count, True, 1.0)
    plain = spread_matrix(head_count, False, 1.0)

    def expand(index):
        for which, matrix in ((0, turn), (1, turn), (2, plain)):
            piece = w_a[index, :, which * heads_wide : (which + 1) * heads_wide]
            w_big[index, :, which * spread : (which + 1) * spread] = dot_f32(
                piece, matrix, 1, 0
            ).astype(bf16)
        piece = w_a[index, :, 3 * heads_wide :]
        w_out_pad[index] = dot_f32(piece, plain, 1, 0).astype(bf16)

    for copy, origin in gain_z:
        copy.wait_recv()
        gain_x.append(dp_pair(gain_buf, origin))
    expand(me_d)
    tok_far = None
    for number, (copy, origin) in enumerate(a_z):
        copy.wait_recv()
        a_x.append(dp_pair(w_a, origin))
        expand(origin)
        if number == 0:
            tok_far = tensor_relay(tok_buf, tok_y)
            cot_far = tensor_relay(cot_buf, cot_y)
    b_x = [dp_pair(w_b, me_d)]
    for copy, _ in gain_x:
        copy.wait_recv()
    for index in range(groups):
        tile = gain_buf[index].astype(f32)
        gain_rows[0:1, index * block : (index + 1) * block] = tile[0:1, :block]
        gain_rows[8:9, index * block : (index + 1) * block] = tile[8:9, :block]
    attn_gain, mlp_gain = gain_rows[0:1, :], gain_rows[8:9, :]
    tok_near.wait_recv()
    for copy in tok_far:
        copy.wait_recv()
    all_rows = tok_buf[...].reshape(row_count, width).astype(f32)
    rows_one[...] = (normalize(all_rows)[0] * attn_gain).astype(bf16)
    for copy, mirrored in a_x:
        copy.wait_recv()
        expand(mirrored)

    paired = paired_matrix()
    rotary = table[...]
    for which in range(3):
        weight = w_big[:, :, which * spread : (which + 1) * spread].reshape(width, spread)
        projected = dot_f32(rows_one[...], weight, 1, 0)
        for head in range(head_count):
            piece = projected[:, head * 128 : (head + 1) * 128]
            if which == 2:
                v_buf[head] = piece.astype(bf16)
                continue
            turned = piece * rotary
            turned = (turned + pltpu.roll(turned, 64, 1)).astype(bf16)
            (q_buf, k_buf)[which][head] = turned
    for head in range(head_count):
        scores = dot_f32(k_buf[head], q_buf[head], 1, 1) * (0.5 * HD ** (-0.5))
        peak = jnp.max(scores, axis=0, keepdims=True)
        powers = jnp.exp(scores - peak)
        share = powers * (1.0 / jnp.sum(powers, axis=0, keepdims=True))
        probs[head] = share
        mixed_t = dot_f32(v_buf[head], share.astype(bf16), 0, 0).astype(bf16)
        mix_t[head] = mixed_t
        mixed = jnp.transpose(mixed_t.astype(f32)).astype(bf16)
        mix[:, :, head * 128 : (head + 1) * 128] = mixed.reshape(members, own_rows, 128)
        mix_pack[:, head * HD : (head + 1) * HD] = mixed[:, :HD]

    def reduce_start(part, recv):
        first = []
        for shift in range(1, rings):
            far = lax.rem(yrow + shift, rings)
            first.append(send(part.at[far * 2 + 1 - core], recv.at[shift], "tensor", c_peer))
        return first, send(part.at[c_peer], recv.at[0], "tensor", c_peer)

    def reduce_middle(part, recv, fwd, first):
        second = []
        for shift in range(1, rings):
            far = lax.rem(yrow + shift, rings)
            first[shift - 1].wait_recv()
            fwd[shift] = (part[far * 2 + core].astype(f32) + recv[shift].astype(f32)).astype(bf16)
            second.append(
                send(fwd.at[shift], recv.at[rings + shift], "tensor", far * 2 + core)
            )
        return second

    def reduce_finish(part, recv, near, second):
        near.wait_recv()
        total = part[me_t].astype(f32) + recv[0].astype(f32)
        for shift in range(1, rings):
            second[shift - 1].wait_recv()
            total = total + recv[rings + shift].astype(f32)
        return total

    out_weight = w_out_pad[...].reshape(width, spread)
    part_one[...] = (
        dot_f32(mix[...].reshape(row_count, spread), out_weight, 1, 1)
        .astype(bf16)
        .reshape(members, own_rows, width)
    )
    first_one, near_one = reduce_start(part_one, recv_one)
    second_one = reduce_middle(part_one, recv_one, fwd_one, first_one)
    for copy, origin in b_z:
        copy.wait_recv()
        b_x.append(dp_pair(w_b, origin))
    for head in range(head_count):
        q_buf[head] = dot_f32(q_buf[head], paired, 1, 0).astype(bf16)
        k_buf[head] = dot_f32(k_buf[head], paired, 1, 0).astype(bf16)
    residual = tok_buf[me_t].astype(f32)
    hidden_res[...] = residual + reduce_finish(part_one, recv_one, near_one, second_one)
    normed_two, inv_two = normalize(hidden_res[...])
    rows_two[me_t] = (normed_two * mlp_gain).astype(bf16)
    rows_y, rows_near = tensor_spread(rows_two)
    cot_near.wait_recv()
    for copy in cot_far:
        copy.wait_recv()
    for copy, _ in b_x:
        copy.wait_recv()
    up_w[...] = w_b[:, :, :hidden].reshape(width, hidden)
    gate_w[...] = w_b[:, :, hidden : 2 * hidden].reshape(width, hidden)
    down_w[...] = w_b[:, :, 2 * hidden : 3 * hidden].reshape(width, hidden)

    def feed(ring):
        base = 2 * ring
        count = 2 * own_rows
        rows = rows_two[pl.ds(base, 2)].reshape(count, width)
        cot = cot_buf[pl.ds(base, 2)].reshape(count, width)
        inputs = dot_f32(rows, up_w[...], 1, 0)
        gate_part = dot_f32(rows, gate_w[...], 1, 0)
        grad_act = dot_f32(cot, down_w[...], 1, 0)
        activated, slope = gelu_pair(inputs)
        act_buf[ring] = (activated * gate_part).astype(bf16)
        grad_up = (grad_act * gate_part * slope).astype(bf16)
        grad_gate = (grad_act * activated).astype(bf16)
        up_grad[ring] = grad_up
        gate_grad[ring] = grad_gate
        part_two[pl.ds(base, 2)] = (
            (dot_f32(grad_up, up_w[...], 1, 1) + dot_f32(grad_gate, gate_w[...], 1, 1))
            .astype(bf16)
            .reshape(2, own_rows, width)
        )

    rows_near.wait_recv()
    feed(yrow)
    rows_far = tensor_relay(rows_two, rows_y)
    for copy in rows_far:
        copy.wait_recv()
    for shift in range(1, rings):
        feed(lax.rem(yrow + shift, rings))
    first_two, near_two = reduce_start(part_two, recv_two)
    second_two = reduce_middle(part_two, recv_two, fwd_two, first_two)

    def pair_start(grads, half):
        copies = []
        for shift in range(1, outer + 1):
            row = lax.rem(zrow + shift, outer)
            copies.append((send(grads.at[row * 2 + 1 - col], half.at[row], "dp", x_peer), row))
        return copies

    def pair_finish(grads, half, sums, parts, copies):
        across = []
        for number, (copy, row) in enumerate(copies):
            copy.wait_recv()
            value = (grads[row * 2 + col].astype(f32) + half[row].astype(f32)).astype(bf16)
            if number == outer - 1:
                parts[row] = value
                continue
            sums[row] = value
            across.append(send(sums.at[row], parts.at[zrow], "dp", row * 2 + col))
        return across

    full_rows = rows_two[...].reshape(row_count, width)
    full_cot = cot_buf[...].reshape(row_count, width)
    for which, grad in ((0, up_grad), (1, gate_grad)):
        mlp_grads[:, :, which * hidden : (which + 1) * hidden] = (
            dot_f32(full_rows, grad[...].reshape(row_count, hidden), 0, 0)
            .astype(bf16)
            .reshape(groups, block, hidden)
        )
    full_act = act_buf[...].reshape(row_count, hidden)
    mlp_grads[:, :, 2 * hidden : 3 * hidden] = (
        dot_f32(full_cot, full_act, 0, 0).astype(bf16).reshape(groups, block, hidden)
    )
    if pad_hidden > 3 * hidden:
        mlp_grads[:, :, 3 * hidden :] = jnp.zeros(
            (groups, block, pad_hidden - 3 * hidden), bf16
        )
    mlp_pairs = pair_start(mlp_grads, mlp_half)
    part_three[...] = (
        dot_f32(full_act, down_w[...], 1, 1).astype(bf16).reshape(members, own_rows, width)
    )
    normed_two, inv_two = normalize(hidden_res[...])
    back_two = reduce_finish(part_two, recv_two, near_two, second_two)
    grad_res, mlp_gain_part = normalize_back(back_two, normed_two, inv_two, mlp_gain)
    grad_hidden[...] = cot_buf[me_t].astype(f32) + grad_res
    grad_rows[me_t] = grad_hidden[...].astype(bf16)
    grad_y, grad_near = tensor_spread(grad_rows)
    first_three, near_three = reduce_start(part_three, recv_three)
    grad_far = tensor_relay(grad_rows, grad_y)
    second_three = reduce_middle(part_three, recv_three, fwd_three, first_three)
    grad_near.wait_recv()
    for copy in grad_far:
        copy.wait_recv()
    full_grad = grad_rows[...].reshape(row_count, width)
    grad_mix = dot_f32(full_grad, out_weight, 1, 0).astype(bf16)
    out_grads[...] = (
        dot_f32(full_grad, mix_pack[...], 0, 0).astype(bf16).reshape(groups, block, heads_wide)
    )
    mlp_across = pair_finish(mlp_grads, mlp_half, mlp_sum, mlp_parts, mlp_pairs)
    out_pairs = pair_start(out_grads, out_half)
    scale = HD ** (-0.5)
    for head in range(head_count):
        grad_head = grad_mix[:, head * 128 : (head + 1) * 128]
        grad_head_t = jnp.transpose(grad_head.astype(f32))
        delta = jnp.sum(grad_head_t * mix_t[head].astype(f32), axis=0, keepdims=True)
        grad_probs = dot_f32(v_buf[head], grad_head, 1, 1)
        share = probs[head]
        grad_scores = (share * (grad_probs - delta)).astype(bf16)
        grad_v = dot_f32(share.astype(bf16), grad_head, 1, 0)
        grad_k = dot_f32(grad_scores, q_buf[head], 1, 0) * (rotary * scale)
        grad_k = grad_k + pltpu.roll(grad_k, 64, 1)
        grad_q = jnp.transpose(dot_f32(k_buf[head], grad_scores, 0, 0)) * (rotary * scale)
        grad_q = grad_q + pltpu.roll(grad_q, 64, 1)
        for which, value in enumerate((grad_q, grad_k, grad_v)):
            start = which * heads_wide + head * HD
            proj_grad[:, start : start + HD] = value[:, :HD].astype(bf16)
    out_across = pair_finish(out_grads, out_half, out_sum, out_parts, out_pairs)
    qkv_grads[...] = (
        dot_f32(rows_one[...], proj_grad[...], 0, 0)
        .astype(bf16)
        .reshape(groups, block, 3 * heads_wide)
    )
    qkv_pairs = pair_start(qkv_grads, qkv_half)
    qkv_weight = w_a[:, :, : 3 * heads_wide].reshape(width, 3 * heads_wide)
    part_four[...] = (
        dot_f32(proj_grad[...], qkv_weight, 1, 1)
        .astype(bf16)
        .reshape(members, own_rows, width)
    )
    first_four, near_four = reduce_start(part_four, recv_four)
    second_four = reduce_middle(part_four, recv_four, fwd_four, first_four)

    def total(parts, across):
        for copy in across:
            copy.wait_recv()
        return jnp.sum(parts[...].astype(f32), axis=0)

    mlp_out = reduce_finish(part_three, recv_three, near_three, second_three)
    output_ref[...] = (hidden_res[...] + mlp_out).astype(bf16)
    qkv_across = pair_finish(qkv_grads, qkv_half, qkv_sum, qkv_parts, qkv_pairs)
    residual = tok_buf[me_t].astype(f32)
    normed_one, inv_one = normalize(residual)
    back_one = reduce_finish(part_four, recv_four, near_four, second_four)
    grad_res, attn_gain_part = normalize_back(back_one, normed_one, inv_one, attn_gain)
    input_grad_ref[...] = grad_hidden[...] + grad_res
    gain_send[...] = jnp.zeros(gain_send.shape, f32)
    attn_row = attn_gain_part.reshape(1, width)
    mlp_row = mlp_gain_part.reshape(1, width)
    for index in range(groups):
        gain_send[index, 0:1, :block] = attn_row[:, index * block : (index + 1) * block]
        gain_send[index, 1:2, :block] = mlp_row[:, index * block : (index + 1) * block]
    gain_recv[me_d] = gain_send[me_d]
    gain_copies = []
    for shift in range(1, groups):
        peer = lax.rem(me_d + shift, groups)
        gain_copies.append(send(gain_send.at[peer], gain_recv.at[me_d], "dp", peer))
    mlp_grad_ref[...] = total(mlp_parts, mlp_across)
    out_grad_ref[...] = total(out_parts, out_across)
    gain_group[me_t] = total(gain_recv, gain_copies)
    gain_copies = []
    for shift in range(1, members):
        peer = lax.rem(me_t + shift, members)
        gain_copies.append(send(gain_group.at[me_t], gain_group.at[me_t], "tensor", peer))
    qkv_grad_ref[...] = total(qkv_parts, qkv_across)
    gain_ref[...] = total(gain_group, gain_copies)
    for copy in sent:
        copy.wait_send()


def rotary_table(row_count):
    position = (np.arange(row_count) % L).astype(np.float32)
    halves = np.arange(HD // 2).astype(np.float32)
    inverse = np.float32(ROPE_THETA) ** (np.float32(-2.0) * halves / np.float32(HD))
    angles = position[:, None] * inverse[None, :]
    return np.concatenate([np.cos(angles)] * 2 + [np.sin(angles)] * 2, axis=1).astype(np.float32)


def whole_layer(sizes, tokens, attn_gain, w_qkv, w_out, mlp_gain, w_in, w_down, cotangent):
    bf16, f32 = jnp.bfloat16, jnp.float32
    groups, members = sizes["dp"], sizes["tensor"]
    own_rows, width = tokens.shape
    block, heads_wide, hidden = w_qkv.shape[1], w_qkv.shape[2], w_in.shape[2]
    pad_hidden = -(-3 * hidden // 128) * 128
    row_count = own_rows * members
    head_count, spread = heads_wide // HD, 2 * heads_wide
    outer, rings = groups // 2, members // 2
    vmem = pltpu.VMEM
    parts = vmem((members, own_rows, width), bf16)
    arrived = vmem((2 * rings, own_rows, width), bf16)
    passed = vmem((rings, own_rows, width), bf16)
    heads = vmem((head_count, row_count, 128), bf16)
    ringed = vmem((rings, 2 * own_rows, hidden), bf16)

    def exchanged(wide):
        quarter = vmem((outer, block, wide), bf16)
        return [vmem((groups, block, wide), bf16), quarter, quarter, quarter]

    scratch = [
        parts, parts,
        vmem(w_qkv.shape, bf16), vmem(w_out.shape, bf16),
        vmem(w_in.shape, bf16), vmem(w_down.shape, bf16),
        vmem((1, block), bf16), vmem((1, block), bf16), vmem((row_count, 2 * HD), f32),
        vmem((groups, block, 4 * heads_wide), bf16),
        vmem((groups, block, pad_hidden), bf16),
        vmem((groups, 16, 128), bf16),
        vmem((16, width), f32),
        vmem((groups, block, 3 * spread), bf16),
        vmem((groups, block, spread), bf16),
        vmem((width, hidden), bf16), vmem((width, hidden), bf16), vmem((width, hidden), bf16),
        vmem((row_count, width), bf16),
        vmem((head_count, row_count, row_count), f32),
        heads, heads, heads,
        vmem((head_count, 128, row_count), bf16),
        vmem((members, own_rows, spread), bf16),
        vmem((row_count, heads_wide), bf16),
        parts, arrived, passed,
        vmem((own_rows, width), f32),
        parts,
        ringed, ringed, ringed,
        parts, arrived, passed,
        parts, arrived, passed,
        *exchanged(pad_hidden),
        vmem((own_rows, width), f32),
        parts,
        *exchanged(heads_wide),
        vmem((row_count, 3 * heads_wide), bf16),
        *exchanged(3 * heads_wide),
        parts, arrived, passed,
        vmem((groups, 8, 128), f32), vmem((groups, 8, 128), f32), vmem((members, 8, 128), f32),
    ]
    gathers = 3 * (2 * outer - 1) + 4 * (2 * rings - 1)
    reduces = 4 * (2 * rings - 1) + 3 * (2 * outer - 1)
    slots = gathers + reduces + groups + members - 2
    dims = (own_rows, width, block, heads_wide, hidden, pad_hidden)
    output, input_grad, gains, qkv_sum, out_sum, mlp_sums = pl.pallas_call(
        functools.partial(layer_kernel, sizes, dims),
        out_shape=[
            jax.ShapeDtypeStruct((own_rows, width), bf16),
            jax.ShapeDtypeStruct((own_rows, width), f32),
            jax.ShapeDtypeStruct((8, 128), f32),
            jax.ShapeDtypeStruct((block, 3 * heads_wide), f32),
            jax.ShapeDtypeStruct((block, heads_wide), f32),
            jax.ShapeDtypeStruct((block, pad_hidden), f32),
        ],
        in_specs=[pl.BlockSpec(memory_space=pl.ANY)] * 9,
        out_specs=[pl.BlockSpec(memory_space=pltpu.VMEM)] * 6,
        scratch_shapes=scratch
        + [
            pltpu.SemaphoreType.DMA((9,)),
            pltpu.SemaphoreType.DMA((slots,)),
            pltpu.SemaphoreType.DMA((slots,)),
        ],
        compiler_params=pltpu.CompilerParams(
            collective_id=0, has_side_effects=True, vmem_limit_bytes=60 << 20
        ),
    )(
        tokens, cotangent, w_qkv, w_out, w_in, w_down,
        attn_gain.reshape(1, block), mlp_gain.reshape(1, block),
        jnp.asarray(rotary_table(row_count)),
    )
    grad_w_qkv = jnp.stack(
        [qkv_sum[:, i * heads_wide : (i + 1) * heads_wide] for i in range(3)]
    )
    grad_w_in = jnp.stack([mlp_sums[:, :hidden], mlp_sums[:, hidden : 2 * hidden]])
    return (
        output,
        input_grad,
        gains[0, :block],
        grad_w_qkv,
        out_sum.T,
        gains[1, :block],
        grad_w_in,
        mlp_sums[:, 2 * hidden : 3 * hidden].T,
    )


def fits_whole(sizes, tokens, w_qkv):
    row_count = tokens.shape[0] * sizes["tensor"]
    even = sizes["dp"] % 2 == 0 and sizes["tensor"] % 2 == 0
    tiled = w_qkv.shape[1] % 16 == 0 and tokens.shape[0] % 16 == 0
    return even and tiled and row_count == L and w_qkv.shape[1] <= 128


def layer(sizes, tokens, attn_gain, w_qkv, *rest):
    run = whole_layer if fits_whole(sizes, tokens, w_qkv) else body
    return run(sizes, tokens, attn_gain, w_qkv, *rest)


def solution(mesh):
    in_specs = (
        P(("dp", "tensor"), None),
        P("dp"),
        P(None, "dp", "tensor"),
        P("tensor", "dp"),
        P("dp"),
        P(None, "dp", "tensor"),
        P("tensor", "dp"),
        P(("dp", "tensor"), None),
    )
    out_specs = (
        P(("dp", "tensor"), None),
        P(("dp", "tensor"), None),
        P("dp"),
        P(None, "dp", "tensor"),
        P("tensor", "dp"),
        P("dp"),
        P(None, "dp", "tensor"),
        P("tensor", "dp"),
    )
    sizes = {axis: mesh.shape[axis] for axis in ("dp", "tensor")}
    return jax.shard_map(functools.partial(layer, sizes), mesh=mesh, in_specs=in_specs, out_specs=out_specs, check_vma=False)
```

```python
import functools

import jax
import jax.numpy as jnp
import numpy as np
from jax import lax
from jax.experimental import pallas as pl
from jax.experimental.pallas import tpu as pltpu
from jax.experimental.layout import Layout, with_layout_constraint
from jax.sharding import PartitionSpec as P

HD = 64
L = 512


NORM_EPS = 1e-05
ROPE_THETA = 160000.0
SQRT_HALF = 0.7071067811865476
GAUSS_NORM = 0.3989422804014327


def rope_tables(row_count):
    position = (jnp.arange(row_count) % L).astype(jnp.float32)
    halves = jnp.arange(HD // 2).astype(jnp.float32)
    inverse = ROPE_THETA ** (-2.0 * halves / HD)
    angles = position[:, None] * inverse[None, :]
    angles = jnp.concatenate([angles, angles], axis=1)
    return (jnp.cos(angles)[:, None, :], jnp.sin(angles)[:, None, :])


def rotate(field_rows, cos_table, sin_table):
    first_half = field_rows[..., : HD // 2]
    second_half = field_rows[..., HD // 2 :]
    turned = jnp.concatenate([-second_half, first_half], axis=-1)
    return field_rows * cos_table + turned * sin_table


def rotate_back(grad_field, cos_table, sin_table):
    scaled = grad_field * sin_table
    turned = jnp.concatenate([scaled[..., HD // 2 :], -scaled[..., : HD // 2]], axis=-1)
    return grad_field * cos_table + turned


def normalize(values):
    centred = values - jnp.mean(values, axis=-1, keepdims=True)
    inv_std = lax.rsqrt(jnp.mean(centred * centred, axis=-1, keepdims=True) + NORM_EPS)
    return (centred * inv_std, inv_std)


def normalize_back(grad_norm, normed, inv_std, gain_row):
    gain_part = jnp.sum(grad_norm * normed, axis=0)
    scaled = grad_norm * gain_row
    centred = scaled - jnp.mean(scaled, axis=-1, keepdims=True)
    grad_in = inv_std * (centred - normed * jnp.mean(scaled * normed, axis=-1, keepdims=True))
    return (grad_in, gain_part)


def gelu_pair(inputs):
    normal_cdf = 0.5 * (1.0 + lax.erf(inputs * SQRT_HALF))
    return (inputs * normal_cdf, normal_cdf + inputs * jnp.exp(-0.5 * inputs * inputs) * GAUSS_NORM)


def attend(queries, key_rows, value_rows):
    score_scale = HD ** (-0.5)
    scores = (
        jnp.einsum("qhd,khd->hqk", queries, key_rows, preferred_element_type=jnp.float32)
        * score_scale
    )
    row_max = jnp.max(scores, axis=-1, keepdims=True)
    log_total = row_max + jnp.log(jnp.sum(jnp.exp(scores - row_max), axis=-1, keepdims=True))
    weights = jnp.exp(scores - log_total).astype(jnp.bfloat16)
    attn_mix = jnp.einsum(
        "hqk,khd->qhd", weights, value_rows, preferred_element_type=jnp.float32
    ).astype(jnp.bfloat16)
    return (attn_mix, log_total)


def attend_back(queries, key_rows, value_rows, attn_mix, grad_mix, log_total):
    score_scale = HD ** (-0.5)
    scores = (
        jnp.einsum("qhd,khd->hqk", queries, key_rows, preferred_element_type=jnp.float32)
        * score_scale
    )
    probabilities = jnp.exp(scores - log_total)
    grad_probs = jnp.einsum(
        "qhd,khd->hqk", grad_mix, value_rows, preferred_element_type=jnp.float32
    )
    row_delta = jnp.sum(grad_mix.astype(jnp.float32) * attn_mix.astype(jnp.float32), axis=-1)
    grad_scores = (probabilities * (grad_probs - jnp.transpose(row_delta)[:, :, None])).astype(
        jnp.bfloat16
    )
    prob_rounded = probabilities.astype(jnp.bfloat16)
    grad_values = jnp.einsum(
        "hqk,qhd->khd", prob_rounded, grad_mix, preferred_element_type=jnp.float32
    )
    grad_queries = (
        jnp.einsum("hqk,khd->qhd", grad_scores, key_rows, preferred_element_type=jnp.float32)
        * score_scale
    )
    grad_keys = (
        jnp.einsum("hqk,qhd->khd", grad_scores, queries, preferred_element_type=jnp.float32)
        * score_scale
    )
    return (grad_queries, grad_keys, grad_values)


def exchange_kernel(plan, sizes, *refs):
    count = len(plan)
    sources, targets = refs[:count], refs[count : 2 * count]
    own_sem, send_sem, recv_sem = refs[2 * count :]
    axes = sorted({axis for _, axis, _ in plan})
    barrier = pltpu.get_barrier_semaphore()
    total = 0
    for axis in axes:
        me = lax.axis_index(axis)
        for shift in range(1, sizes[axis]):
            pl.semaphore_signal(
                barrier,
                inc=1,
                device_id={axis: lax.rem(me + shift, sizes[axis])},
                device_id_type=pl.DeviceIdType.MESH,
            )
            total += 1
    pl.semaphore_wait(barrier, total)
    slot = 0
    pending, relays, local = [], [], []

    def remote(source, target, axis, peer, index):
        return pltpu.make_async_remote_copy(
            src_ref=source,
            dst_ref=target,
            send_sem=send_sem.at[index],
            recv_sem=recv_sem.at[index],
            device_id={axis: peer},
            device_id_type=pl.DeviceIdType.MESH,
        )

    for which, (kind, axis, span) in enumerate(plan):
        size = sizes[axis]
        me = lax.axis_index(axis)
        source, target = sources[which], targets[which]
        outer = size // 2
        column = lax.rem(me, 2)
        row = me // 2
        partner = row * 2 + 1 - column
        if kind == "half":
            copy = remote(source.at[:, 1 - column, :, span], target, axis, partner, slot)
            copy.start()
            pending.append(copy)
            slot += 1
            continue
        if kind == "outer":
            for shift in range(1, outer):
                other = lax.rem(row + shift, outer)
                copy = remote(source.at[other], target.at[row], axis, other * 2 + column, slot)
                copy.start()
                pending.append(copy)
                slot += 1
            copy = pltpu.make_async_copy(source.at[row], target.at[row], own_sem.at[which])
            copy.start()
            local.append(copy)
            continue
        if kind == "relay":
            for shift in range(1, outer):
                peer = lax.rem(row + shift, outer) * 2 + column
                copy = remote(source, target.at[me], axis, peer, slot)
                copy.start()
                origin = lax.rem(row + outer - shift, outer) * 2 + column
                relays.append((copy, target, axis, origin, partner, slot + 1))
                slot += 2
            copy = remote(source, target.at[me], axis, partner, slot)
            copy.start()
            pending.append(copy)
            slot += 1
        else:
            for shift in range(1, size):
                peer = lax.rem(me + shift, size)
                piece = source if kind == "gather" else source.at[peer, :, span]
                copy = remote(piece, target.at[me], axis, peer, slot)
                copy.start()
                pending.append(copy)
                slot += 1
        piece = source if kind != "scatter" else source.at[me, :, span]
        copy = pltpu.make_async_copy(piece, target.at[me], own_sem.at[which])
        copy.start()
        local.append(copy)
    for copy, target, axis, origin, partner, index in relays:
        copy.wait_recv()
        onward = remote(target.at[origin], target.at[origin], axis, partner, index)
        onward.start()
        pending.append(onward)
    for copy, *_ in relays:
        copy.wait_send()
    for copy in pending + local:
        copy.wait()


def slots_of(kind, size):
    outer = size // 2
    return {"relay": 2 * outer - 1, "half": 1, "outer": outer - 1}.get(kind, size - 1)


def shape_of(kind, size, shape, wide):
    if kind == "half":
        return (shape[0], shape[2], wide)
    return {"scatter": shape[:-1] + (wide,), "outer": shape}.get(kind, (size,) + shape)


def exchange(sizes, number, *ops):
    arrays = [op[2] for op in ops]
    spans = [slice(*op[3]) if len(op) > 3 else slice(0, op[2].shape[-1]) for op in ops]
    plan = tuple((op[0], op[1], span) for op, span in zip(ops, spans))
    shapes = [
        jax.ShapeDtypeStruct(
            shape_of(kind, sizes[axis], array.shape, span.stop - span.start), array.dtype
        )
        for (kind, axis, span), array in zip(plan, arrays)
    ]
    slots = sum(slots_of(kind, sizes[axis]) for kind, axis, _ in plan)
    return pl.pallas_call(
        functools.partial(exchange_kernel, plan, sizes),
        out_shape=shapes,
        in_specs=[pl.BlockSpec(memory_space=pltpu.VMEM)] * len(arrays),
        out_specs=[pl.BlockSpec(memory_space=pltpu.VMEM)] * len(arrays),
        scratch_shapes=[
            pltpu.SemaphoreType.DMA((len(arrays),)),
            pltpu.SemaphoreType.DMA((slots,)),
            pltpu.SemaphoreType.DMA((slots,)),
        ],
        compiler_params=pltpu.CompilerParams(
            collective_id=number, has_side_effects=True, vmem_limit_bytes=48 << 20
        ),
    )(*arrays)


def pad_columns(array, multiple=128):
    extra = -array.shape[-1] % multiple
    return jnp.pad(array, [(0, 0)] * (array.ndim - 1) + [(0, extra)])


def total_of(pieces):
    return jnp.sum(pieces.astype(jnp.float32), axis=0)


def row_major(array):
    return with_layout_constraint(array, Layout(major_to_minor=(0, 1)))


def dot_f32(left, right, left_dim, right_dim):
    return lax.dot_general(
        left, right, (((left_dim,), (right_dim,)), ((), ())), preferred_element_type=jnp.float32
    )


def feed_forward_kernel(
    hidden, rows_ref, up_ref, gate_ref, down_ref, cot_ref, mlp_ref, back_ref, grads_ref
):
    bf16 = jnp.bfloat16
    rows, cot = rows_ref[...], cot_ref[...]
    inputs = dot_f32(rows, up_ref[...], 1, 0)
    gate_part = dot_f32(rows, gate_ref[...], 1, 0)
    activated, gelu_slope = gelu_pair(inputs)
    hidden_act = (activated * gate_part).astype(bf16)
    mlp_ref[...] = dot_f32(hidden_act, down_ref[...], 1, 1).astype(bf16)
    grad_act = dot_f32(cot, down_ref[...], 1, 0)
    grad_up = (grad_act * gate_part * gelu_slope).astype(bf16)
    grad_gate = (grad_act * activated).astype(bf16)
    back_ref[...] = (
        dot_f32(grad_up, up_ref[...], 1, 1) + dot_f32(grad_gate, gate_ref[...], 1, 1)
    ).astype(bf16)
    grads_ref[:, :hidden] = dot_f32(rows, grad_up, 0, 0).astype(bf16)
    grads_ref[:, hidden : 2 * hidden] = dot_f32(rows, grad_gate, 0, 0).astype(bf16)
    grads_ref[:, 2 * hidden : 3 * hidden] = dot_f32(cot, hidden_act, 0, 0).astype(bf16)
    spare = grads_ref.shape[1] - 3 * hidden
    if spare:
        grads_ref[:, 3 * hidden :] = jnp.zeros((grads_ref.shape[0], spare), bf16)


def feed_forward(hidden, rows, up, gate, down_t, cot):
    row_count, width = rows.shape
    padded = -(-3 * hidden // 128) * 128
    return pl.pallas_call(
        functools.partial(feed_forward_kernel, hidden),
        out_shape=[
            jax.ShapeDtypeStruct((row_count, width), jnp.bfloat16),
            jax.ShapeDtypeStruct((row_count, width), jnp.bfloat16),
            jax.ShapeDtypeStruct((width, padded), jnp.bfloat16),
        ],
        in_specs=[pl.BlockSpec(memory_space=pltpu.VMEM)] * 5,
        out_specs=[pl.BlockSpec(memory_space=pltpu.VMEM)] * 3,
        compiler_params=pltpu.CompilerParams(vmem_limit_bytes=48 << 20),
    )(rows, up, gate, down_t, cot)


def body(sizes, tokens, attn_gain, w_qkv, w_out, mlp_gain, w_in, w_down, cotangent):
    bf16, f32 = jnp.bfloat16, jnp.float32
    groups, members = sizes["dp"], sizes["tensor"]
    block = w_qkv.shape[1]
    width = block * groups
    heads_wide, hidden = w_qkv.shape[2], w_in.shape[2]
    own_rows = tokens.shape[0]
    packed = jnp.concatenate([w_qkv[0], w_qkv[1], w_qkv[2], w_out.T], axis=1)
    gain_tile = jnp.pad(jnp.stack([attn_gain, mlp_gain]), [(0, 14), (0, -block % 128)])
    weights, gain_tiles, token_rows, grad_rows = exchange(
        sizes,
        0,
        ("relay", "dp", packed),
        ("relay", "dp", gain_tile),
        ("relay", "tensor", tokens),
        ("relay", "tensor", cotangent),
    )
    weights = weights.reshape(width, -1)
    qkv_weight = weights[:, : 3 * heads_wide]
    out_weight_t = weights[:, 3 * heads_wide :]
    attn_full = gain_tiles[:, 0, :block].reshape(1, width).astype(f32)
    mlp_full = gain_tiles[:, 1, :block].reshape(1, width).astype(f32)
    outer = groups // 2
    column = lax.rem(lax.axis_index("dp"), 2)

    def quarter(array):
        return array.reshape(outer, 2, block, -1)

    def half_sum(array, received, low, high):
        own = lax.dynamic_index_in_dim(quarter(array)[..., low:high], column, 1, keepdims=False)
        return (own.astype(f32) + received.astype(f32)).astype(bf16)

    row_count = own_rows * members
    grad_rows = grad_rows.reshape(row_count, width)
    residual = tokens.astype(f32)
    normed_one, inv_one = normalize(residual)
    rows_one = (normalize(token_rows.reshape(row_count, width).astype(f32))[0] * attn_full).astype(bf16)
    head_count = heads_wide // HD
    head_shape = (row_count, head_count, HD)
    seq_shape = (row_count // L, L, head_count, HD)
    flat_shape = (row_count, heads_wide)
    cos_table, sin_table = rope_tables(row_count)
    projected = dot_f32(rows_one, qkv_weight, 1, 0)
    pieces = [projected[:, i * heads_wide : (i + 1) * heads_wide].reshape(head_shape) for i in range(3)]
    queries = rotate(pieces[0], cos_table, sin_table).astype(bf16).reshape(seq_shape)
    key_rows = rotate(pieces[1], cos_table, sin_table).astype(bf16).reshape(seq_shape)
    value_rows = pieces[2].astype(bf16).reshape(seq_shape)
    one_seq = row_count == L

    def over_sequences(function, arrays):
        if one_seq:
            results = function(*[array[0] for array in arrays])
            return tuple(result[None] for result in results)
        return lax.map(lambda seq_block: function(*seq_block), arrays)

    attn_mix, log_total = over_sequences(attend, (queries, key_rows, value_rows))
    mixed_rows = attn_mix.reshape(flat_shape)
    attn_part = dot_f32(mixed_rows, out_weight_t, 1, 1).astype(bf16)
    attn_parts, up_weight, down_weight_t = exchange(
        sizes,
        1,
        ("scatter", "tensor", attn_part.reshape(members, own_rows, width)),
        ("relay", "dp", w_in[0]),
        ("relay", "dp", w_down.T),
    )
    up_weight = up_weight.reshape(width, -1)
    down_weight_t = down_weight_t.reshape(width, -1)
    hidden_res = residual + total_of(attn_parts)
    normed_two, inv_two = normalize(hidden_res)
    ln_two = (normed_two * mlp_full).astype(bf16)
    rows_two, gate_weight = exchange(
        sizes, 2, ("relay", "tensor", ln_two), ("relay", "dp", w_in[1])
    )
    gate_weight = gate_weight.reshape(width, -1)
    rows_two = rows_two.reshape(row_count, width)
    mlp_part, ln_two_part, mlp_grads = feed_forward(
        hidden, rows_two, up_weight, gate_weight, down_weight_t, grad_rows
    )
    mlp_wide = mlp_grads.shape[-1]
    first = mlp_wide // 256 * 128
    ln_two_parts, mlp_grads_a = exchange(
        sizes,
        3,
        ("scatter", "tensor", ln_two_part.reshape(members, own_rows, width)),
        ("half", "dp", quarter(mlp_grads), (0, first)),
    )
    grad_res_two, mlp_gain_part = normalize_back(total_of(ln_two_parts), normed_two, inv_two, mlp_full)
    grad_hidden = cotangent.astype(f32) + grad_res_two
    grad_hidden_rows, mlp_grads_b, mlp_sums_a = exchange(
        sizes,
        4,
        ("relay", "tensor", grad_hidden.astype(bf16)),
        ("half", "dp", quarter(mlp_grads), (first, mlp_wide)),
        ("outer", "dp", half_sum(mlp_grads, mlp_grads_a, 0, first)),
    )
    grad_hidden_rows = grad_hidden_rows.reshape(row_count, width)
    grad_out_t = row_major(dot_f32(grad_hidden_rows, mixed_rows, 0, 0).astype(bf16))
    grad_mix = dot_f32(grad_hidden_rows, out_weight_t, 1, 0).astype(bf16).reshape(seq_shape)
    grad_q, grad_k, grad_v = over_sequences(
        attend_back, (queries, key_rows, value_rows, attn_mix, grad_mix, log_total)
    )
    grad_proj = jnp.concatenate(
        [
            rotate_back(grad_q.reshape(head_shape), cos_table, sin_table).reshape(flat_shape),
            rotate_back(grad_k.reshape(head_shape), cos_table, sin_table).reshape(flat_shape),
            grad_v.reshape(flat_shape),
        ],
        axis=1,
    ).astype(bf16)
    grad_qkv = row_major(dot_f32(rows_one, grad_proj, 0, 0).astype(bf16))
    ln_one_part = dot_f32(grad_proj, qkv_weight, 1, 1).astype(bf16)
    ln_one_parts, mlp_sums_b, grad_out_half, qkv_half = exchange(
        sizes,
        5,
        ("scatter", "tensor", ln_one_part.reshape(members, own_rows, width)),
        ("outer", "dp", half_sum(mlp_grads, mlp_grads_b, first, mlp_wide)),
        ("half", "dp", quarter(grad_out_t)),
        ("half", "dp", quarter(grad_qkv)),
    )
    grad_res_one, attn_gain_part = normalize_back(total_of(ln_one_parts), normed_one, inv_one, attn_full)
    input_grad = grad_hidden + grad_res_one
    gain_parts = jnp.stack([attn_gain_part, mlp_gain_part] + [jnp.zeros_like(attn_gain_part)] * 6)
    gain_parts = pad_columns(jnp.swapaxes(gain_parts.reshape(8, groups, block), 0, 1))
    late_parts, gain_parts, mlp_parts, grad_out_parts = exchange(
        sizes,
        6,
        ("outer", "dp", half_sum(grad_qkv, qkv_half, 0, 3 * heads_wide)),
        ("scatter", "dp", gain_parts),
        ("scatter", "tensor", mlp_part.reshape(members, own_rows, width)),
        ("outer", "dp", half_sum(grad_out_t, grad_out_half, 0, heads_wide)),
    )
    output = (hidden_res + total_of(mlp_parts)).astype(bf16)
    (gain_groups,) = exchange(sizes, 7, ("gather", "tensor", total_of(gain_parts)))
    gain_sum = total_of(gain_groups)
    late = total_of(late_parts)
    grad_w_qkv = jnp.stack([late[:, i * heads_wide : (i + 1) * heads_wide] for i in range(3)])
    grad_w_out = total_of(grad_out_parts).T
    mlp_sums = jnp.concatenate(
        [total_of(mlp_sums_a), total_of(mlp_sums_b)], axis=1
    )
    grad_w_in = jnp.stack([mlp_sums[:, :hidden], mlp_sums[:, hidden : 2 * hidden]])
    grad_w_down = mlp_sums[:, 2 * hidden : 3 * hidden].T
    return (
        output,
        input_grad,
        gain_sum[0, :block],
        grad_w_qkv,
        grad_w_out,
        gain_sum[1, :block],
        grad_w_in,
        grad_w_down,
    )


def lanes(shape, dim):
    return lax.broadcasted_iota(jnp.int32, shape, dim)


def spread_matrix(head_count, turned, sign):
    shape = (head_count * HD, head_count * 2 * HD)
    row, column = lanes(shape, 0), lanes(shape, 1)
    head = lax.shift_right_logical(column, 7)
    feature = lax.bitwise_and(column, HD - 1)
    upper = lax.bitwise_and(column, 2 * HD - 1) >= HD
    plain = row == head * HD + feature
    if not turned:
        return jnp.where(plain & jnp.logical_not(upper), 1.0, 0.0).astype(jnp.bfloat16)
    other = row == head * HD + lax.bitwise_and(feature + HD // 2, HD - 1)
    signed = jnp.where(feature < HD // 2, -sign, sign)
    return jnp.where(
        upper, jnp.where(other, signed, 0.0), jnp.where(plain, 1.0, 0.0)
    ).astype(jnp.bfloat16)


def paired_matrix():
    shape = (2 * HD, 2 * HD)
    row, column = lanes(shape, 0), lanes(shape, 1)
    feature = lax.bitwise_and(column, HD - 1)
    upper = column >= HD
    other = row == lax.bitwise_and(feature + HD // 2, HD - 1)
    signed = jnp.where(feature < HD // 2, 1.0, -1.0)
    return jnp.where(
        upper, jnp.where(other, signed, 0.0), jnp.where(row == column, 1.0, 0.0)
    ).astype(jnp.bfloat16)


def layer_kernel(sizes, dims, *refs):
    bf16, f32 = jnp.bfloat16, jnp.float32
    groups, members = sizes["dp"], sizes["tensor"]
    own_rows, width, block, heads_wide, hidden, pad_hidden = dims
    head_count = heads_wide // HD
    spread = 2 * heads_wide
    row_count = own_rows * members
    outer, rings = groups // 2, members // 2
    (
        tok_in, cot_in, qkv_in, out_in, up_in, down_in, attn_in, mlp_in, table_in,
        output_ref, input_grad_ref, gain_ref, qkv_grad_ref, out_grad_ref, mlp_grad_ref,
        tok_buf, cot_buf, qkv_raw, out_raw, up_raw, down_raw, attn_raw, mlp_raw, table,
        w_a, w_b, gain_buf, gain_rows, w_big, w_out_pad, up_w, gate_w, down_w,
        rows_one, probs, q_buf, k_buf, v_buf, mix_t, mix, mix_pack,
        part_one, recv_one, fwd_one, hidden_res, rows_two,
        act_buf, up_grad, gate_grad, part_two, recv_two, fwd_two,
        part_three, recv_three, fwd_three,
        mlp_grads, mlp_half, mlp_sum, mlp_parts,
        grad_hidden, grad_rows, out_grads, out_half, out_sum, out_parts,
        proj_grad, qkv_grads, qkv_half, qkv_sum, qkv_parts,
        part_four, recv_four, fwd_four, gain_send, gain_recv, gain_group,
        load_sem, send_sem, recv_sem,
    ) = refs
    me_d, me_t = lax.axis_index("dp"), lax.axis_index("tensor")
    zrow, col = me_d // 2, lax.rem(me_d, 2)
    x_peer = zrow * 2 + 1 - col
    yrow, core = me_t // 2, lax.rem(me_t, 2)
    c_peer = yrow * 2 + 1 - core
    counter = [0]
    sent = []

    def make(source, target, axis, peer):
        index = counter[0]
        counter[0] += 1
        return pltpu.make_async_remote_copy(
            src_ref=source,
            dst_ref=target,
            send_sem=send_sem.at[index],
            recv_sem=recv_sem.at[index],
            device_id={axis: peer},
            device_id_type=pl.DeviceIdType.MESH,
        )

    def send(source, target, axis, peer):
        copy = make(source, target, axis, peer)
        copy.start()
        sent.append((copy, None))
        return copy

    def begin(copy, condition):
        pl.when(condition)(copy.start)
        sent.append((copy, condition))

    cuts = 2 if block % 32 == 0 else 1
    height = block // cuts

    class Chain:
        def __init__(self, buffer):
            self.buffer = buffer
            self.moves = {}
            last = outer - 1
            for step in range(1, outer):
                for side in (0, 1):
                    ahead = 1 if side == 0 else outer - 1
                    target = lax.rem(zrow + ahead, outer) * 2 + col
                    back = step - 1 if side else outer - step + 1
                    carried = lax.rem(zrow + back, outer) * 2 + col
                    origin = lax.rem(zrow + (step if side else outer - step), outer) * 2
                    lands = zrow + step <= last if side else zrow >= step
                    starts = (
                        (zrow >= 1) & (zrow + step - 1 <= last)
                        if side
                        else (zrow < last) & (zrow >= step - 1)
                    )
                    for cut in range(cuts):
                        self.moves[step, side, cut] = (
                            make(self.piece(carried, cut), self.piece(carried, cut), "dp", target),
                            make(
                                self.piece(origin + col, cut),
                                self.piece(origin + col, cut),
                                "dp",
                                x_peer,
                            ),
                            starts,
                            lands,
                            origin,
                        )

        def piece(self, index, cut):
            return self.buffer.at[index, cut * height : (cut + 1) * height]

        def start(self):
            self.own = []
            for cut in range(cuts):
                for side in (0, 1):
                    move, _, starts, _, _ = self.moves[1, side, cut]
                    begin(move, starts)
                piece = self.piece(me_d, cut)
                self.own.append(send(piece, piece, "dp", x_peer))

        def step(self, number):
            for cut in range(cuts):
                for side in (0, 1):
                    move, across, _, lands, _ = self.moves[number, side, cut]
                    pl.when(lands)(move.wait_recv)
                    if number + 1 < outer:
                        onward, _, starts, _, _ = self.moves[number + 1, side, cut]
                        begin(onward, starts)
                    begin(across, lands)

        def paired(self, number, then=None):
            for side in (0, 1):
                lands, origin = self.moves[number, side, 0][3:]

                @pl.when(lands)
                def _():
                    for cut in range(cuts):
                        self.moves[number, side, cut][1].wait_recv()
                    if then is not None:
                        then(origin + 1 - col)

    loads = [
        pltpu.make_async_copy(source, target, load_sem.at[index])
        for index, (source, target) in enumerate(
            [
                (qkv_in, qkv_raw), (out_in, out_raw), (attn_in, attn_raw), (mlp_in, mlp_raw),
                (tok_in, tok_buf.at[me_t]), (cot_in, cot_buf.at[me_t]),
                (up_in, up_raw), (down_in, down_raw), (table_in, table),
            ]
        )
    ]
    for load in loads:
        load.start()
    barrier = pltpu.get_barrier_semaphore()
    for axis, me in (("dp", me_d), ("tensor", me_t)):
        for shift in range(1, sizes[axis]):
            pl.semaphore_signal(
                barrier,
                inc=1,
                device_id={axis: lax.rem(me + shift, sizes[axis])},
                device_id_type=pl.DeviceIdType.MESH,
            )
    eye_heads = jnp.where(
        lanes((heads_wide, heads_wide), 0) == lanes((heads_wide, heads_wide), 1), 1.0, 0.0
    ).astype(bf16)
    for load in loads[:4]:
        load.wait()
    gain_buf[me_d] = jnp.zeros(gain_buf.shape[1:], bf16)
    gain_buf[me_d, 0:1, :block] = attn_raw[...]
    gain_buf[me_d, 8:9, :block] = mlp_raw[...]
    for which in range(3):
        w_a[me_d, :, which * heads_wide : (which + 1) * heads_wide] = qkv_raw[which]
    w_a[me_d, :, 3 * heads_wide :] = dot_f32(out_raw[...], eye_heads, 0, 0).astype(bf16)
    pl.semaphore_wait(barrier, groups + members - 2)

    def dp_spread(buffer):
        copies = []
        for shift in range(1, outer):
            peer = lax.rem(zrow + shift, outer) * 2 + col
            origin = lax.rem(zrow + outer - shift, outer) * 2 + col
            copies.append((send(buffer.at[me_d], buffer.at[me_d], "dp", peer), origin))
        return copies

    def dp_pair(buffer, origin):
        mirrored = origin // 2 * 2 + 1 - col
        return (send(buffer.at[origin], buffer.at[origin], "dp", x_peer), mirrored)

    def tensor_spread(buffer):
        copies = []
        for shift in range(1, rings):
            peer = lax.rem(yrow + shift, rings) * 2 + core
            origin = lax.rem(yrow + rings - shift, rings) * 2 + core
            copies.append((send(buffer.at[me_t], buffer.at[me_t], "tensor", peer), origin))
        near = send(buffer.at[me_t], buffer.at[me_t], "tensor", c_peer)
        return copies, near

    def tensor_relay(buffer, copies):
        onward = []
        for copy, origin in copies:
            copy.wait_recv()
            onward.append(send(buffer.at[origin], buffer.at[origin], "tensor", c_peer))
        return onward

    gain_z = dp_spread(gain_buf)
    gain_x = [dp_pair(gain_buf, me_d)]
    chain_a = Chain(w_a)
    chain_a.start()
    for load in loads[4:6]:
        load.wait()
    tok_y, tok_near = tensor_spread(tok_buf)
    cot_y, cot_near = tensor_spread(cot_buf)
    for load in loads[6:]:
        load.wait()
    eye_hidden = jnp.where(
        lanes((hidden, hidden), 0) == lanes((hidden, hidden), 1), 1.0, 0.0
    ).astype(bf16)
    for which in range(2):
        w_b[me_d, :, which * hidden : (which + 1) * hidden] = up_raw[which]
    w_b[me_d, :, 2 * hidden : 3 * hidden] = dot_f32(down_raw[...], eye_hidden, 0, 0).astype(bf16)
    if pad_hidden > 3 * hidden:
        w_b[me_d, :, 3 * hidden :] = jnp.zeros((block, pad_hidden - 3 * hidden), bf16)
    chain_b = Chain(w_b)

    turn = spread_matrix(head_count, True, 1.0)
    plain = spread_matrix(head_count, False, 1.0)

    def expand(index):
        for which, matrix in ((0, turn), (1, turn), (2, plain)):
            piece = w_a[index, :, which * heads_wide : (which + 1) * heads_wide]
            w_big[index, :, which * spread : (which + 1) * spread] = dot_f32(
                piece, matrix, 1, 0
            ).astype(bf16)
        piece = w_a[index, :, 3 * heads_wide :]
        w_out_pad[index] = dot_f32(piece, plain, 1, 0).astype(bf16)

    expand(me_d)
    chain_a.step(1)
    for copy, origin in gain_z:
        copy.wait_recv()
        gain_x.append(dp_pair(gain_buf, origin))
    tok_far = tensor_relay(tok_buf, tok_y)
    for number in range(2, outer - 1):
        chain_a.step(number)
    for copy, _ in gain_x:
        copy.wait_recv()
    for index in range(groups):
        tile = gain_buf[index].astype(f32)
        gain_rows[0:1, index * block : (index + 1) * block] = tile[0:1, :block]
        gain_rows[8:9, index * block : (index + 1) * block] = tile[8:9, :block]
    attn_gain, mlp_gain = gain_rows[0:1, :], gain_rows[8:9, :]
    tok_near.wait_recv()
    for copy in tok_far:
        copy.wait_recv()
    all_rows = tok_buf[...].reshape(row_count, width).astype(f32)
    rows_one[...] = (normalize(all_rows)[0] * attn_gain).astype(bf16)
    if outer > 2:
        chain_a.step(outer - 1)
    chain_b.start()
    cot_far = tensor_relay(cot_buf, cot_y)
    for shift in range(1, outer):
        expand(lax.rem(zrow + shift, outer) * 2 + col)
    for copy in chain_a.own:
        copy.wait_recv()
    expand(x_peer)
    for number in range(1, outer):
        chain_a.paired(number, expand)

    paired = paired_matrix()
    rotary = table[...]
    for which in range(3):
        weight = w_big[:, :, which * spread : (which + 1) * spread].reshape(width, spread)
        projected = dot_f32(rows_one[...], weight, 1, 0)
        for head in range(head_count):
            piece = projected[:, head * 128 : (head + 1) * 128]
            if which == 2:
                v_buf[head] = piece.astype(bf16)
                continue
            turned = piece * rotary
            turned = (turned + pltpu.roll(turned, 64, 1)).astype(bf16)
            (q_buf, k_buf)[which][head] = turned
    chain_b.step(1)
    for head in range(head_count):
        scores = dot_f32(k_buf[head], q_buf[head], 1, 1) * (0.5 * HD ** (-0.5))
        peak = jnp.max(scores, axis=0, keepdims=True)
        powers = jnp.exp(scores - peak)
        share = powers * (1.0 / jnp.sum(powers, axis=0, keepdims=True))
        probs[head] = share
        mixed_t = dot_f32(v_buf[head], share.astype(bf16), 0, 0).astype(bf16)
        mix_t[head] = mixed_t
        mixed = jnp.transpose(mixed_t.astype(f32)).astype(bf16)
        mix[:, :, head * 128 : (head + 1) * 128] = mixed.reshape(members, own_rows, 128)
        mix_pack[:, head * HD : (head + 1) * HD] = mixed[:, :HD]

    def reduce_start(part, recv):
        first = []
        for shift in range(1, rings):
            far = lax.rem(yrow + shift, rings)
            first.append(send(part.at[far * 2 + 1 - core], recv.at[shift], "tensor", c_peer))
        return first, send(part.at[c_peer], recv.at[0], "tensor", c_peer)

    def reduce_middle(part, recv, fwd, first):
        second = []
        for shift in range(1, rings):
            far = lax.rem(yrow + shift, rings)
            first[shift - 1].wait_recv()
            fwd[shift] = (part[far * 2 + core].astype(f32) + recv[shift].astype(f32)).astype(bf16)
            second.append(
                send(fwd.at[shift], recv.at[rings + shift], "tensor", far * 2 + core)
            )
        return second

    def reduce_finish(part, recv, near, second):
        near.wait_recv()
        total = part[me_t].astype(f32) + recv[0].astype(f32)
        for shift in range(1, rings):
            second[shift - 1].wait_recv()
            total = total + recv[rings + shift].astype(f32)
        return total

    out_weight = w_out_pad[...].reshape(width, spread)
    part_one[...] = (
        dot_f32(mix[...].reshape(row_count, spread), out_weight, 1, 1)
        .astype(bf16)
        .reshape(members, own_rows, width)
    )
    first_one, near_one = reduce_start(part_one, recv_one)
    second_one = reduce_middle(part_one, recv_one, fwd_one, first_one)
    for number in range(2, outer - 1):
        chain_b.step(number)
    for head in range(head_count):
        q_buf[head] = dot_f32(q_buf[head], paired, 1, 0).astype(bf16)
        k_buf[head] = dot_f32(k_buf[head], paired, 1, 0).astype(bf16)
    residual = tok_buf[me_t].astype(f32)
    hidden_res[...] = residual + reduce_finish(part_one, recv_one, near_one, second_one)
    normed_two, inv_two = normalize(hidden_res[...])
    rows_two[me_t] = (normed_two * mlp_gain).astype(bf16)
    rows_y, rows_near = tensor_spread(rows_two)
    if outer > 2:
        chain_b.step(outer - 1)
    cot_near.wait_recv()
    for copy in cot_far:
        copy.wait_recv()
    for copy in chain_b.own:
        copy.wait_recv()
    for number in range(1, outer):
        chain_b.paired(number)
    up_w[...] = w_b[:, :, :hidden].reshape(width, hidden)
    gate_w[...] = w_b[:, :, hidden : 2 * hidden].reshape(width, hidden)
    down_w[...] = w_b[:, :, 2 * hidden : 3 * hidden].reshape(width, hidden)

    def feed(ring):
        base = 2 * ring
        count = 2 * own_rows
        rows = rows_two[pl.ds(base, 2)].reshape(count, width)
        cot = cot_buf[pl.ds(base, 2)].reshape(count, width)
        inputs = dot_f32(rows, up_w[...], 1, 0)
        gate_part = dot_f32(rows, gate_w[...], 1, 0)
        grad_act = dot_f32(cot, down_w[...], 1, 0)
        activated, slope = gelu_pair(inputs)
        act_buf[ring] = (activated * gate_part).astype(bf16)
        grad_up = (grad_act * gate_part * slope).astype(bf16)
        grad_gate = (grad_act * activated).astype(bf16)
        up_grad[ring] = grad_up
        gate_grad[ring] = grad_gate
        part_two[pl.ds(base, 2)] = (
            (dot_f32(grad_up, up_w[...], 1, 1) + dot_f32(grad_gate, gate_w[...], 1, 1))
            .astype(bf16)
            .reshape(2, own_rows, width)
        )

    rows_near.wait_recv()
    rows_far = tensor_relay(rows_two, rows_y)
    feed(yrow)
    for copy in rows_far:
        copy.wait_recv()
    for shift in range(1, rings):
        feed(lax.rem(yrow + shift, rings))
    first_two, near_two = reduce_start(part_two, recv_two)
    second_two = reduce_middle(part_two, recv_two, fwd_two, first_two)

    def pair_start(grads, half):
        copies = []
        for shift in range(1, outer + 1):
            row = lax.rem(zrow + shift, outer)
            copies.append((send(grads.at[row * 2 + 1 - col], half.at[row], "dp", x_peer), row))
        return copies

    def pair_step(grads, half, sums, parts, copies, number):
        copy, row = copies[number]
        copy.wait_recv()
        value = (grads[row * 2 + col].astype(f32) + half[row].astype(f32)).astype(bf16)
        if number == outer - 1:
            parts[row] = value
            return []
        sums[row] = value
        return [send(sums.at[row], parts.at[zrow], "dp", row * 2 + col)]

    full_rows = rows_two[...].reshape(row_count, width)
    full_cot = cot_buf[...].reshape(row_count, width)
    for which, grad in ((0, up_grad), (1, gate_grad)):
        mlp_grads[:, :, which * hidden : (which + 1) * hidden] = (
            dot_f32(full_rows, grad[...].reshape(row_count, hidden), 0, 0)
            .astype(bf16)
            .reshape(groups, block, hidden)
        )
    full_act = act_buf[...].reshape(row_count, hidden)
    mlp_grads[:, :, 2 * hidden : 3 * hidden] = (
        dot_f32(full_cot, full_act, 0, 0).astype(bf16).reshape(groups, block, hidden)
    )
    if pad_hidden > 3 * hidden:
        mlp_grads[:, :, 3 * hidden :] = jnp.zeros(
            (groups, block, pad_hidden - 3 * hidden), bf16
        )
    mlp_pairs = pair_start(mlp_grads, mlp_half)
    part_three[...] = (
        dot_f32(full_act, down_w[...], 1, 1).astype(bf16).reshape(members, own_rows, width)
    )
    normed_two, inv_two = normalize(hidden_res[...])
    back_two = reduce_finish(part_two, recv_two, near_two, second_two)
    grad_res, mlp_gain_part = normalize_back(back_two, normed_two, inv_two, mlp_gain)
    grad_hidden[...] = cot_buf[me_t].astype(f32) + grad_res
    grad_rows[me_t] = grad_hidden[...].astype(bf16)
    grad_y, grad_near = tensor_spread(grad_rows)
    first_three, near_three = reduce_start(part_three, recv_three)
    mlp_state = (mlp_grads, mlp_half, mlp_sum, mlp_parts, mlp_pairs)
    mlp_across = pair_step(*mlp_state, 0)
    grad_far = tensor_relay(grad_rows, grad_y)
    second_three = reduce_middle(part_three, recv_three, fwd_three, first_three)
    grad_near.wait_recv()
    for copy in grad_far:
        copy.wait_recv()
    full_grad = grad_rows[...].reshape(row_count, width)
    grad_mix = dot_f32(full_grad, out_weight, 1, 0).astype(bf16)
    out_grads[...] = (
        dot_f32(full_grad, mix_pack[...], 0, 0).astype(bf16).reshape(groups, block, heads_wide)
    )
    out_pairs = pair_start(out_grads, out_half)
    for number in range(1, outer - 2):
        mlp_across += pair_step(*mlp_state, number)
    scale = HD ** (-0.5)
    for head in range(head_count):
        grad_head = grad_mix[:, head * 128 : (head + 1) * 128]
        grad_head_t = jnp.transpose(grad_head.astype(f32))
        delta = jnp.sum(grad_head_t * mix_t[head].astype(f32), axis=0, keepdims=True)
        grad_probs = dot_f32(v_buf[head], grad_head, 1, 1)
        share = probs[head]
        grad_scores = (share * (grad_probs - delta)).astype(bf16)
        grad_v = dot_f32(share.astype(bf16), grad_head, 1, 0)
        grad_k = dot_f32(grad_scores, q_buf[head], 1, 0) * (rotary * scale)
        grad_k = grad_k + pltpu.roll(grad_k, 64, 1)
        grad_q = jnp.transpose(dot_f32(k_buf[head], grad_scores, 0, 0)) * (rotary * scale)
        grad_q = grad_q + pltpu.roll(grad_q, 64, 1)
        for which, value in enumerate((grad_q, grad_k, grad_v)):
            start = which * heads_wide + head * HD
            proj_grad[:, start : start + HD] = value[:, :HD].astype(bf16)
    qkv_grads[...] = (
        dot_f32(rows_one[...], proj_grad[...], 0, 0)
        .astype(bf16)
        .reshape(groups, block, 3 * heads_wide)
    )
    qkv_pairs = pair_start(qkv_grads, qkv_half)
    qkv_weight = w_a[:, :, : 3 * heads_wide].reshape(width, 3 * heads_wide)
    part_four[...] = (
        dot_f32(proj_grad[...], qkv_weight, 1, 1)
        .astype(bf16)
        .reshape(members, own_rows, width)
    )
    first_four, near_four = reduce_start(part_four, recv_four)
    second_four = reduce_middle(part_four, recv_four, fwd_four, first_four)

    def total(parts, across):
        for copy in across:
            copy.wait_recv()
        return jnp.sum(parts[...].astype(f32), axis=0)

    for number in range(max(outer - 2, 1), outer):
        mlp_across += pair_step(*mlp_state, number)
    mlp_out = reduce_finish(part_three, recv_three, near_three, second_three)
    output_ref[...] = (hidden_res[...] + mlp_out).astype(bf16)
    out_state = (out_grads, out_half, out_sum, out_parts, out_pairs)
    out_across = []
    for number in range(outer):
        out_across += pair_step(*out_state, number)
    qkv_state = (qkv_grads, qkv_half, qkv_sum, qkv_parts, qkv_pairs)
    qkv_across = pair_step(*qkv_state, 0)
    residual = tok_buf[me_t].astype(f32)
    normed_one, inv_one = normalize(residual)
    back_one = reduce_finish(part_four, recv_four, near_four, second_four)
    grad_res, attn_gain_part = normalize_back(back_one, normed_one, inv_one, attn_gain)
    input_grad_ref[...] = grad_hidden[...] + grad_res
    gain_send[...] = jnp.zeros(gain_send.shape, f32)
    attn_row = attn_gain_part.reshape(1, width)
    mlp_row = mlp_gain_part.reshape(1, width)
    for index in range(groups):
        gain_send[index, 0:1, :block] = attn_row[:, index * block : (index + 1) * block]
        gain_send[index, 1:2, :block] = mlp_row[:, index * block : (index + 1) * block]
    gain_recv[me_d] = gain_send[me_d]
    gain_copies = []
    for shift in range(1, groups):
        peer = lax.rem(me_d + shift, groups)
        gain_copies.append(send(gain_send.at[peer], gain_recv.at[me_d], "dp", peer))
    for number in range(1, outer):
        qkv_across += pair_step(*qkv_state, number)
    mlp_grad_ref[...] = total(mlp_parts, mlp_across)
    out_grad_ref[...] = total(out_parts, out_across)
    gain_group[me_t] = total(gain_recv, gain_copies)
    gain_copies = []
    for shift in range(1, members):
        peer = lax.rem(me_t + shift, members)
        gain_copies.append(send(gain_group.at[me_t], gain_group.at[me_t], "tensor", peer))
    qkv_grad_ref[...] = total(qkv_parts, qkv_across)
    gain_ref[...] = total(gain_group, gain_copies)
    for copy, condition in sent:
        if condition is None:
            copy.wait_send()
        else:
            pl.when(condition)(copy.wait_send)


def rotary_table(row_count):
    position = (np.arange(row_count) % L).astype(np.float32)
    halves = np.arange(HD // 2).astype(np.float32)
    inverse = np.float32(ROPE_THETA) ** (np.float32(-2.0) * halves / np.float32(HD))
    angles = position[:, None] * inverse[None, :]
    return np.concatenate([np.cos(angles)] * 2 + [np.sin(angles)] * 2, axis=1).astype(np.float32)


def whole_layer(sizes, tokens, attn_gain, w_qkv, w_out, mlp_gain, w_in, w_down, cotangent):
    bf16, f32 = jnp.bfloat16, jnp.float32
    groups, members = sizes["dp"], sizes["tensor"]
    own_rows, width = tokens.shape
    block, heads_wide, hidden = w_qkv.shape[1], w_qkv.shape[2], w_in.shape[2]
    pad_hidden = -(-3 * hidden // 128) * 128
    row_count = own_rows * members
    head_count, spread = heads_wide // HD, 2 * heads_wide
    outer, rings = groups // 2, members // 2
    vmem = pltpu.VMEM
    parts = vmem((members, own_rows, width), bf16)
    arrived = vmem((2 * rings, own_rows, width), bf16)
    passed = vmem((rings, own_rows, width), bf16)
    heads = vmem((head_count, row_count, 128), bf16)
    ringed = vmem((rings, 2 * own_rows, hidden), bf16)

    def exchanged(wide):
        quarter = vmem((outer, block, wide), bf16)
        return [vmem((groups, block, wide), bf16), quarter, quarter, quarter]

    scratch = [
        parts, parts,
        vmem(w_qkv.shape, bf16), vmem(w_out.shape, bf16),
        vmem(w_in.shape, bf16), vmem(w_down.shape, bf16),
        vmem((1, block), bf16), vmem((1, block), bf16), vmem((row_count, 2 * HD), f32),
        vmem((groups, block, 4 * heads_wide), bf16),
        vmem((groups, block, pad_hidden), bf16),
        vmem((groups, 16, 128), bf16),
        vmem((16, width), f32),
        vmem((groups, block, 3 * spread), bf16),
        vmem((groups, block, spread), bf16),
        vmem((width, hidden), bf16), vmem((width, hidden), bf16), vmem((width, hidden), bf16),
        vmem((row_count, width), bf16),
        vmem((head_count, row_count, row_count), f32),
        heads, heads, heads,
        vmem((head_count, 128, row_count), bf16),
        vmem((members, own_rows, spread), bf16),
        vmem((row_count, heads_wide), bf16),
        parts, arrived, passed,
        vmem((own_rows, width), f32),
        parts,
        ringed, ringed, ringed,
        parts, arrived, passed,
        parts, arrived, passed,
        *exchanged(pad_hidden),
        vmem((own_rows, width), f32),
        parts,
        *exchanged(heads_wide),
        vmem((row_count, 3 * heads_wide), bf16),
        *exchanged(3 * heads_wide),
        parts, arrived, passed,
        vmem((groups, 8, 128), f32), vmem((groups, 8, 128), f32), vmem((members, 8, 128), f32),
    ]
    cuts = 2 if block % 32 == 0 else 1
    chains = 2 * cuts * (4 * (outer - 1) + 1)
    gathers = 2 * outer - 1 + chains + 4 * (2 * rings - 1)
    reduces = 4 * (2 * rings - 1) + 3 * (2 * outer - 1)
    slots = gathers + reduces + groups + members - 2
    dims = (own_rows, width, block, heads_wide, hidden, pad_hidden)
    output, input_grad, gains, qkv_sum, out_sum, mlp_sums = pl.pallas_call(
        functools.partial(layer_kernel, sizes, dims),
        out_shape=[
            jax.ShapeDtypeStruct((own_rows, width), bf16),
            jax.ShapeDtypeStruct((own_rows, width), f32),
            jax.ShapeDtypeStruct((8, 128), f32),
            jax.ShapeDtypeStruct((block, 3 * heads_wide), f32),
            jax.ShapeDtypeStruct((block, heads_wide), f32),
            jax.ShapeDtypeStruct((block, pad_hidden), f32),
        ],
        in_specs=[pl.BlockSpec(memory_space=pl.ANY)] * 9,
        out_specs=[pl.BlockSpec(memory_space=pltpu.VMEM)] * 6,
        scratch_shapes=scratch
        + [
            pltpu.SemaphoreType.DMA((9,)),
            pltpu.SemaphoreType.DMA((slots,)),
            pltpu.SemaphoreType.DMA((slots,)),
        ],
        compiler_params=pltpu.CompilerParams(
            collective_id=0, has_side_effects=True, vmem_limit_bytes=60 << 20
        ),
    )(
        tokens, cotangent, w_qkv, w_out, w_in, w_down,
        attn_gain.reshape(1, block), mlp_gain.reshape(1, block),
        jnp.asarray(rotary_table(row_count)),
    )
    results = pl.pallas_call(
        functools.partial(finish_kernel, hidden),
        out_shape=[
            jax.ShapeDtypeStruct(output.shape, bf16),
            jax.ShapeDtypeStruct(input_grad.shape, f32),
            jax.ShapeDtypeStruct(w_qkv.shape, f32),
            jax.ShapeDtypeStruct(w_out.shape, f32),
            jax.ShapeDtypeStruct(w_in.shape, f32),
            jax.ShapeDtypeStruct(w_down.shape, f32),
        ],
        in_specs=[pl.BlockSpec(memory_space=pltpu.VMEM)] * 5,
        out_specs=[pl.BlockSpec(memory_space=pl.ANY)] * 6,
        scratch_shapes=[
            vmem(w_qkv.shape, f32),
            vmem(w_out.shape, f32),
            vmem(w_in.shape, f32),
            vmem(w_down.shape, f32),
            pltpu.SemaphoreType.DMA((6,)),
        ],
        compiler_params=pltpu.CompilerParams(vmem_limit_bytes=16 << 20),
    )(output, input_grad, qkv_sum, out_sum, mlp_sums)
    output, input_grad, grad_w_qkv, grad_w_out, grad_w_in, grad_w_down = results
    return (
        output,
        input_grad,
        gains[0, :block],
        grad_w_qkv,
        grad_w_out,
        gains[1, :block],
        grad_w_in,
        grad_w_down,
    )


def finish_kernel(hidden, *refs):
    (
        output, input_grad, qkv_sum, out_sum, mlp_sums,
        output_to, input_grad_to, qkv_to, out_to, up_to, down_to,
        qkv_buf, out_buf, up_buf, down_buf, sems,
    ) = refs
    started = []

    def put(source, target):
        copy = pltpu.make_async_copy(source, target, sems.at[len(started)])
        copy.start()
        started.append(copy)

    put(output, output_to)
    put(input_grad, input_grad_to)
    heads_wide = out_sum.shape[1]
    for which in range(3):
        qkv_buf[which] = qkv_sum[:, which * heads_wide : (which + 1) * heads_wide]
    put(qkv_buf, qkv_to)
    for which in range(2):
        up_buf[which] = mlp_sums[:, which * hidden : (which + 1) * hidden]
    put(up_buf, up_to)
    out_buf[...] = jnp.transpose(out_sum[...])
    put(out_buf, out_to)
    down_buf[...] = jnp.transpose(mlp_sums[:, 2 * hidden : 3 * hidden])
    put(down_buf, down_to)
    for copy in started:
        copy.wait()


def fits_whole(sizes, tokens, w_qkv):
    row_count = tokens.shape[0] * sizes["tensor"]
    even = sizes["dp"] % 2 == 0 and sizes["tensor"] % 2 == 0
    tiled = w_qkv.shape[1] % 16 == 0 and tokens.shape[0] % 16 == 0
    return even and tiled and row_count == L and w_qkv.shape[1] <= 128


def layer(sizes, tokens, attn_gain, w_qkv, *rest):
    run = whole_layer if fits_whole(sizes, tokens, w_qkv) else body
    return run(sizes, tokens, attn_gain, w_qkv, *rest)


def solution(mesh):
    in_specs = (
        P(("dp", "tensor"), None),
        P("dp"),
        P(None, "dp", "tensor"),
        P("tensor", "dp"),
        P("dp"),
        P(None, "dp", "tensor"),
        P("tensor", "dp"),
        P(("dp", "tensor"), None),
    )
    out_specs = (
        P(("dp", "tensor"), None),
        P(("dp", "tensor"), None),
        P("dp"),
        P(None, "dp", "tensor"),
        P("tensor", "dp"),
        P("dp"),
        P(None, "dp", "tensor"),
        P("tensor", "dp"),
    )
    sizes = {axis: mesh.shape[axis] for axis in ("dp", "tensor")}
    return jax.shard_map(functools.partial(layer, sizes), mesh=mesh, in_specs=in_specs, out_specs=out_specs, check_vma=False)
```

```python
import functools

import jax
import jax.numpy as jnp
import numpy as np
from jax import lax
from jax.experimental import pallas as pl
from jax.experimental.pallas import tpu as pltpu
from jax.experimental.layout import Layout, with_layout_constraint
from jax.sharding import PartitionSpec as P

HD = 64
L = 512


NORM_EPS = 1e-05
ROPE_THETA = 160000.0
SQRT_HALF = 0.7071067811865476
GAUSS_NORM = 0.3989422804014327


def rope_tables(row_count):
    position = (jnp.arange(row_count) % L).astype(jnp.float32)
    halves = jnp.arange(HD // 2).astype(jnp.float32)
    inverse = ROPE_THETA ** (-2.0 * halves / HD)
    angles = position[:, None] * inverse[None, :]
    angles = jnp.concatenate([angles, angles], axis=1)
    return (jnp.cos(angles)[:, None, :], jnp.sin(angles)[:, None, :])


def rotate(field_rows, cos_table, sin_table):
    first_half = field_rows[..., : HD // 2]
    second_half = field_rows[..., HD // 2 :]
    turned = jnp.concatenate([-second_half, first_half], axis=-1)
    return field_rows * cos_table + turned * sin_table


def rotate_back(grad_field, cos_table, sin_table):
    scaled = grad_field * sin_table
    turned = jnp.concatenate([scaled[..., HD // 2 :], -scaled[..., : HD // 2]], axis=-1)
    return grad_field * cos_table + turned


def normalize(values):
    centred = values - jnp.mean(values, axis=-1, keepdims=True)
    inv_std = lax.rsqrt(jnp.mean(centred * centred, axis=-1, keepdims=True) + NORM_EPS)
    return (centred * inv_std, inv_std)


def normalize_back(grad_norm, normed, inv_std, gain_row):
    gain_part = jnp.sum(grad_norm * normed, axis=0)
    scaled = grad_norm * gain_row
    centred = scaled - jnp.mean(scaled, axis=-1, keepdims=True)
    grad_in = inv_std * (centred - normed * jnp.mean(scaled * normed, axis=-1, keepdims=True))
    return (grad_in, gain_part)


def gelu_pair(inputs):
    normal_cdf = 0.5 * (1.0 + lax.erf(inputs * SQRT_HALF))
    return (inputs * normal_cdf, normal_cdf + inputs * jnp.exp(-0.5 * inputs * inputs) * GAUSS_NORM)


def attend(queries, key_rows, value_rows):
    score_scale = HD ** (-0.5)
    scores = (
        jnp.einsum("qhd,khd->hqk", queries, key_rows, preferred_element_type=jnp.float32)
        * score_scale
    )
    row_max = jnp.max(scores, axis=-1, keepdims=True)
    log_total = row_max + jnp.log(jnp.sum(jnp.exp(scores - row_max), axis=-1, keepdims=True))
    weights = jnp.exp(scores - log_total).astype(jnp.bfloat16)
    attn_mix = jnp.einsum(
        "hqk,khd->qhd", weights, value_rows, preferred_element_type=jnp.float32
    ).astype(jnp.bfloat16)
    return (attn_mix, log_total)


def attend_back(queries, key_rows, value_rows, attn_mix, grad_mix, log_total):
    score_scale = HD ** (-0.5)
    scores = (
        jnp.einsum("qhd,khd->hqk", queries, key_rows, preferred_element_type=jnp.float32)
        * score_scale
    )
    probabilities = jnp.exp(scores - log_total)
    grad_probs = jnp.einsum(
        "qhd,khd->hqk", grad_mix, value_rows, preferred_element_type=jnp.float32
    )
    row_delta = jnp.sum(grad_mix.astype(jnp.float32) * attn_mix.astype(jnp.float32), axis=-1)
    grad_scores = (probabilities * (grad_probs - jnp.transpose(row_delta)[:, :, None])).astype(
        jnp.bfloat16
    )
    prob_rounded = probabilities.astype(jnp.bfloat16)
    grad_values = jnp.einsum(
        "hqk,qhd->khd", prob_rounded, grad_mix, preferred_element_type=jnp.float32
    )
    grad_queries = (
        jnp.einsum("hqk,khd->qhd", grad_scores, key_rows, preferred_element_type=jnp.float32)
        * score_scale
    )
    grad_keys = (
        jnp.einsum("hqk,qhd->khd", grad_scores, queries, preferred_element_type=jnp.float32)
        * score_scale
    )
    return (grad_queries, grad_keys, grad_values)


def exchange_kernel(plan, sizes, *refs):
    count = len(plan)
    sources, targets = refs[:count], refs[count : 2 * count]
    own_sem, send_sem, recv_sem = refs[2 * count :]
    axes = sorted({axis for _, axis, _ in plan})
    barrier = pltpu.get_barrier_semaphore()
    total = 0
    for axis in axes:
        me = lax.axis_index(axis)
        for shift in range(1, sizes[axis]):
            pl.semaphore_signal(
                barrier,
                inc=1,
                device_id={axis: lax.rem(me + shift, sizes[axis])},
                device_id_type=pl.DeviceIdType.MESH,
            )
            total += 1
    pl.semaphore_wait(barrier, total)
    slot = 0
    pending, relays, local = [], [], []

    def remote(source, target, axis, peer, index):
        return pltpu.make_async_remote_copy(
            src_ref=source,
            dst_ref=target,
            send_sem=send_sem.at[index],
            recv_sem=recv_sem.at[index],
            device_id={axis: peer},
            device_id_type=pl.DeviceIdType.MESH,
        )

    for which, (kind, axis, span) in enumerate(plan):
        size = sizes[axis]
        me = lax.axis_index(axis)
        source, target = sources[which], targets[which]
        outer = size // 2
        column = lax.rem(me, 2)
        row = me // 2
        partner = row * 2 + 1 - column
        if kind == "half":
            copy = remote(source.at[:, 1 - column, :, span], target, axis, partner, slot)
            copy.start()
            pending.append(copy)
            slot += 1
            continue
        if kind == "outer":
            for shift in range(1, outer):
                other = lax.rem(row + shift, outer)
                copy = remote(source.at[other], target.at[row], axis, other * 2 + column, slot)
                copy.start()
                pending.append(copy)
                slot += 1
            copy = pltpu.make_async_copy(source.at[row], target.at[row], own_sem.at[which])
            copy.start()
            local.append(copy)
            continue
        if kind == "relay":
            for shift in range(1, outer):
                peer = lax.rem(row + shift, outer) * 2 + column
                copy = remote(source, target.at[me], axis, peer, slot)
                copy.start()
                origin = lax.rem(row + outer - shift, outer) * 2 + column
                relays.append((copy, target, axis, origin, partner, slot + 1))
                slot += 2
            copy = remote(source, target.at[me], axis, partner, slot)
            copy.start()
            pending.append(copy)
            slot += 1
        else:
            for shift in range(1, size):
                peer = lax.rem(me + shift, size)
                piece = source if kind == "gather" else source.at[peer, :, span]
                copy = remote(piece, target.at[me], axis, peer, slot)
                copy.start()
                pending.append(copy)
                slot += 1
        piece = source if kind != "scatter" else source.at[me, :, span]
        copy = pltpu.make_async_copy(piece, target.at[me], own_sem.at[which])
        copy.start()
        local.append(copy)
    for copy, target, axis, origin, partner, index in relays:
        copy.wait_recv()
        onward = remote(target.at[origin], target.at[origin], axis, partner, index)
        onward.start()
        pending.append(onward)
    for copy, *_ in relays:
        copy.wait_send()
    for copy in pending + local:
        copy.wait()


def slots_of(kind, size):
    outer = size // 2
    return {"relay": 2 * outer - 1, "half": 1, "outer": outer - 1}.get(kind, size - 1)


def shape_of(kind, size, shape, wide):
    if kind == "half":
        return (shape[0], shape[2], wide)
    return {"scatter": shape[:-1] + (wide,), "outer": shape}.get(kind, (size,) + shape)


def exchange(sizes, number, *ops):
    arrays = [op[2] for op in ops]
    spans = [slice(*op[3]) if len(op) > 3 else slice(0, op[2].shape[-1]) for op in ops]
    plan = tuple((op[0], op[1], span) for op, span in zip(ops, spans))
    shapes = [
        jax.ShapeDtypeStruct(
            shape_of(kind, sizes[axis], array.shape, span.stop - span.start), array.dtype
        )
        for (kind, axis, span), array in zip(plan, arrays)
    ]
    slots = sum(slots_of(kind, sizes[axis]) for kind, axis, _ in plan)
    return pl.pallas_call(
        functools.partial(exchange_kernel, plan, sizes),
        out_shape=shapes,
        in_specs=[pl.BlockSpec(memory_space=pltpu.VMEM)] * len(arrays),
        out_specs=[pl.BlockSpec(memory_space=pltpu.VMEM)] * len(arrays),
        scratch_shapes=[
            pltpu.SemaphoreType.DMA((len(arrays),)),
            pltpu.SemaphoreType.DMA((slots,)),
            pltpu.SemaphoreType.DMA((slots,)),
        ],
        compiler_params=pltpu.CompilerParams(
            collective_id=number, has_side_effects=True, vmem_limit_bytes=48 << 20
        ),
    )(*arrays)


def pad_columns(array, multiple=128):
    extra = -array.shape[-1] % multiple
    return jnp.pad(array, [(0, 0)] * (array.ndim - 1) + [(0, extra)])


def total_of(pieces):
    return jnp.sum(pieces.astype(jnp.float32), axis=0)


def row_major(array):
    return with_layout_constraint(array, Layout(major_to_minor=(0, 1)))


def dot_f32(left, right, left_dim, right_dim):
    return lax.dot_general(
        left, right, (((left_dim,), (right_dim,)), ((), ())), preferred_element_type=jnp.float32
    )


def feed_forward_kernel(
    hidden, rows_ref, up_ref, gate_ref, down_ref, cot_ref, mlp_ref, back_ref, grads_ref
):
    bf16 = jnp.bfloat16
    rows, cot = rows_ref[...], cot_ref[...]
    inputs = dot_f32(rows, up_ref[...], 1, 0)
    gate_part = dot_f32(rows, gate_ref[...], 1, 0)
    activated, gelu_slope = gelu_pair(inputs)
    hidden_act = (activated * gate_part).astype(bf16)
    mlp_ref[...] = dot_f32(hidden_act, down_ref[...], 1, 1).astype(bf16)
    grad_act = dot_f32(cot, down_ref[...], 1, 0)
    grad_up = (grad_act * gate_part * gelu_slope).astype(bf16)
    grad_gate = (grad_act * activated).astype(bf16)
    back_ref[...] = (
        dot_f32(grad_up, up_ref[...], 1, 1) + dot_f32(grad_gate, gate_ref[...], 1, 1)
    ).astype(bf16)
    grads_ref[:, :hidden] = dot_f32(rows, grad_up, 0, 0).astype(bf16)
    grads_ref[:, hidden : 2 * hidden] = dot_f32(rows, grad_gate, 0, 0).astype(bf16)
    grads_ref[:, 2 * hidden : 3 * hidden] = dot_f32(cot, hidden_act, 0, 0).astype(bf16)
    spare = grads_ref.shape[1] - 3 * hidden
    if spare:
        grads_ref[:, 3 * hidden :] = jnp.zeros((grads_ref.shape[0], spare), bf16)


def feed_forward(hidden, rows, up, gate, down_t, cot):
    row_count, width = rows.shape
    padded = -(-3 * hidden // 128) * 128
    return pl.pallas_call(
        functools.partial(feed_forward_kernel, hidden),
        out_shape=[
            jax.ShapeDtypeStruct((row_count, width), jnp.bfloat16),
            jax.ShapeDtypeStruct((row_count, width), jnp.bfloat16),
            jax.ShapeDtypeStruct((width, padded), jnp.bfloat16),
        ],
        in_specs=[pl.BlockSpec(memory_space=pltpu.VMEM)] * 5,
        out_specs=[pl.BlockSpec(memory_space=pltpu.VMEM)] * 3,
        compiler_params=pltpu.CompilerParams(vmem_limit_bytes=48 << 20),
    )(rows, up, gate, down_t, cot)


def body(sizes, tokens, attn_gain, w_qkv, w_out, mlp_gain, w_in, w_down, cotangent):
    bf16, f32 = jnp.bfloat16, jnp.float32
    groups, members = sizes["dp"], sizes["tensor"]
    block = w_qkv.shape[1]
    width = block * groups
    heads_wide, hidden = w_qkv.shape[2], w_in.shape[2]
    own_rows = tokens.shape[0]
    packed = jnp.concatenate([w_qkv[0], w_qkv[1], w_qkv[2], w_out.T], axis=1)
    gain_tile = jnp.pad(jnp.stack([attn_gain, mlp_gain]), [(0, 14), (0, -block % 128)])
    weights, gain_tiles, token_rows, grad_rows = exchange(
        sizes,
        0,
        ("relay", "dp", packed),
        ("relay", "dp", gain_tile),
        ("relay", "tensor", tokens),
        ("relay", "tensor", cotangent),
    )
    weights = weights.reshape(width, -1)
    qkv_weight = weights[:, : 3 * heads_wide]
    out_weight_t = weights[:, 3 * heads_wide :]
    attn_full = gain_tiles[:, 0, :block].reshape(1, width).astype(f32)
    mlp_full = gain_tiles[:, 1, :block].reshape(1, width).astype(f32)
    outer = groups // 2
    column = lax.rem(lax.axis_index("dp"), 2)

    def quarter(array):
        return array.reshape(outer, 2, block, -1)

    def half_sum(array, received, low, high):
        own = lax.dynamic_index_in_dim(quarter(array)[..., low:high], column, 1, keepdims=False)
        return (own.astype(f32) + received.astype(f32)).astype(bf16)

    row_count = own_rows * members
    grad_rows = grad_rows.reshape(row_count, width)
    residual = tokens.astype(f32)
    normed_one, inv_one = normalize(residual)
    rows_one = (normalize(token_rows.reshape(row_count, width).astype(f32))[0] * attn_full).astype(bf16)
    head_count = heads_wide // HD
    head_shape = (row_count, head_count, HD)
    seq_shape = (row_count // L, L, head_count, HD)
    flat_shape = (row_count, heads_wide)
    cos_table, sin_table = rope_tables(row_count)
    projected = dot_f32(rows_one, qkv_weight, 1, 0)
    pieces = [projected[:, i * heads_wide : (i + 1) * heads_wide].reshape(head_shape) for i in range(3)]
    queries = rotate(pieces[0], cos_table, sin_table).astype(bf16).reshape(seq_shape)
    key_rows = rotate(pieces[1], cos_table, sin_table).astype(bf16).reshape(seq_shape)
    value_rows = pieces[2].astype(bf16).reshape(seq_shape)
    one_seq = row_count == L

    def over_sequences(function, arrays):
        if one_seq:
            results = function(*[array[0] for array in arrays])
            return tuple(result[None] for result in results)
        return lax.map(lambda seq_block: function(*seq_block), arrays)

    attn_mix, log_total = over_sequences(attend, (queries, key_rows, value_rows))
    mixed_rows = attn_mix.reshape(flat_shape)
    attn_part = dot_f32(mixed_rows, out_weight_t, 1, 1).astype(bf16)
    attn_parts, up_weight, down_weight_t = exchange(
        sizes,
        1,
        ("scatter", "tensor", attn_part.reshape(members, own_rows, width)),
        ("relay", "dp", w_in[0]),
        ("relay", "dp", w_down.T),
    )
    up_weight = up_weight.reshape(width, -1)
    down_weight_t = down_weight_t.reshape(width, -1)
    hidden_res = residual + total_of(attn_parts)
    normed_two, inv_two = normalize(hidden_res)
    ln_two = (normed_two * mlp_full).astype(bf16)
    rows_two, gate_weight = exchange(
        sizes, 2, ("relay", "tensor", ln_two), ("relay", "dp", w_in[1])
    )
    gate_weight = gate_weight.reshape(width, -1)
    rows_two = rows_two.reshape(row_count, width)
    mlp_part, ln_two_part, mlp_grads = feed_forward(
        hidden, rows_two, up_weight, gate_weight, down_weight_t, grad_rows
    )
    mlp_wide = mlp_grads.shape[-1]
    first = mlp_wide // 256 * 128
    ln_two_parts, mlp_grads_a = exchange(
        sizes,
        3,
        ("scatter", "tensor", ln_two_part.reshape(members, own_rows, width)),
        ("half", "dp", quarter(mlp_grads), (0, first)),
    )
    grad_res_two, mlp_gain_part = normalize_back(total_of(ln_two_parts), normed_two, inv_two, mlp_full)
    grad_hidden = cotangent.astype(f32) + grad_res_two
    grad_hidden_rows, mlp_grads_b, mlp_sums_a = exchange(
        sizes,
        4,
        ("relay", "tensor", grad_hidden.astype(bf16)),
        ("half", "dp", quarter(mlp_grads), (first, mlp_wide)),
        ("outer", "dp", half_sum(mlp_grads, mlp_grads_a, 0, first)),
    )
    grad_hidden_rows = grad_hidden_rows.reshape(row_count, width)
    grad_out_t = row_major(dot_f32(grad_hidden_rows, mixed_rows, 0, 0).astype(bf16))
    grad_mix = dot_f32(grad_hidden_rows, out_weight_t, 1, 0).astype(bf16).reshape(seq_shape)
    grad_q, grad_k, grad_v = over_sequences(
        attend_back, (queries, key_rows, value_rows, attn_mix, grad_mix, log_total)
    )
    grad_proj = jnp.concatenate(
        [
            rotate_back(grad_q.reshape(head_shape), cos_table, sin_table).reshape(flat_shape),
            rotate_back(grad_k.reshape(head_shape), cos_table, sin_table).reshape(flat_shape),
            grad_v.reshape(flat_shape),
        ],
        axis=1,
    ).astype(bf16)
    grad_qkv = row_major(dot_f32(rows_one, grad_proj, 0, 0).astype(bf16))
    ln_one_part = dot_f32(grad_proj, qkv_weight, 1, 1).astype(bf16)
    ln_one_parts, mlp_sums_b, grad_out_half, qkv_half = exchange(
        sizes,
        5,
        ("scatter", "tensor", ln_one_part.reshape(members, own_rows, width)),
        ("outer", "dp", half_sum(mlp_grads, mlp_grads_b, first, mlp_wide)),
        ("half", "dp", quarter(grad_out_t)),
        ("half", "dp", quarter(grad_qkv)),
    )
    grad_res_one, attn_gain_part = normalize_back(total_of(ln_one_parts), normed_one, inv_one, attn_full)
    input_grad = grad_hidden + grad_res_one
    gain_parts = jnp.stack([attn_gain_part, mlp_gain_part] + [jnp.zeros_like(attn_gain_part)] * 6)
    gain_parts = pad_columns(jnp.swapaxes(gain_parts.reshape(8, groups, block), 0, 1))
    late_parts, gain_parts, mlp_parts, grad_out_parts = exchange(
        sizes,
        6,
        ("outer", "dp", half_sum(grad_qkv, qkv_half, 0, 3 * heads_wide)),
        ("scatter", "dp", gain_parts),
        ("scatter", "tensor", mlp_part.reshape(members, own_rows, width)),
        ("outer", "dp", half_sum(grad_out_t, grad_out_half, 0, heads_wide)),
    )
    output = (hidden_res + total_of(mlp_parts)).astype(bf16)
    (gain_groups,) = exchange(sizes, 7, ("gather", "tensor", total_of(gain_parts)))
    gain_sum = total_of(gain_groups)
    late = total_of(late_parts)
    grad_w_qkv = jnp.stack([late[:, i * heads_wide : (i + 1) * heads_wide] for i in range(3)])
    grad_w_out = total_of(grad_out_parts).T
    mlp_sums = jnp.concatenate(
        [total_of(mlp_sums_a), total_of(mlp_sums_b)], axis=1
    )
    grad_w_in = jnp.stack([mlp_sums[:, :hidden], mlp_sums[:, hidden : 2 * hidden]])
    grad_w_down = mlp_sums[:, 2 * hidden : 3 * hidden].T
    return (
        output,
        input_grad,
        gain_sum[0, :block],
        grad_w_qkv,
        grad_w_out,
        gain_sum[1, :block],
        grad_w_in,
        grad_w_down,
    )


def lanes(shape, dim):
    return lax.broadcasted_iota(jnp.int32, shape, dim)


def spread_matrix(head_count, turned, sign):
    shape = (head_count * HD, head_count * 2 * HD)
    row, column = lanes(shape, 0), lanes(shape, 1)
    head = lax.shift_right_logical(column, 7)
    feature = lax.bitwise_and(column, HD - 1)
    upper = lax.bitwise_and(column, 2 * HD - 1) >= HD
    plain = row == head * HD + feature
    if not turned:
        return jnp.where(plain & jnp.logical_not(upper), 1.0, 0.0).astype(jnp.bfloat16)
    other = row == head * HD + lax.bitwise_and(feature + HD // 2, HD - 1)
    signed = jnp.where(feature < HD // 2, -sign, sign)
    return jnp.where(
        upper, jnp.where(other, signed, 0.0), jnp.where(plain, 1.0, 0.0)
    ).astype(jnp.bfloat16)


def paired_matrix():
    shape = (2 * HD, 2 * HD)
    row, column = lanes(shape, 0), lanes(shape, 1)
    feature = lax.bitwise_and(column, HD - 1)
    upper = column >= HD
    other = row == lax.bitwise_and(feature + HD // 2, HD - 1)
    signed = jnp.where(feature < HD // 2, 1.0, -1.0)
    return jnp.where(
        upper, jnp.where(other, signed, 0.0), jnp.where(row == column, 1.0, 0.0)
    ).astype(jnp.bfloat16)


def layer_kernel(sizes, dims, *refs):
    bf16, f32 = jnp.bfloat16, jnp.float32
    groups, members = sizes["dp"], sizes["tensor"]
    own_rows, width, block, heads_wide, hidden, pad_hidden = dims
    head_count = heads_wide // HD
    spread = 2 * heads_wide
    row_count = own_rows * members
    outer, rings = groups // 2, members // 2
    (
        tok_in, cot_in, qkv_in, out_in, up_in, down_in, attn_in, mlp_in, table_in,
        output_ref, input_grad_ref, gain_ref, qkv_grad_ref, out_grad_ref, mlp_grad_ref,
        tok_buf, cot_buf, qkv_raw, out_raw, up_raw, down_raw, attn_raw, mlp_raw, table,
        w_a, w_b, gain_buf, gain_rows, w_big, w_out_pad, up_w, gate_w, down_w,
        rows_one, probs, q_buf, k_buf, v_buf, mix_t, mix, mix_pack,
        part_one, recv_one, fwd_one, hidden_res, rows_two,
        act_buf, up_grad, gate_grad, part_two, recv_two, fwd_two,
        part_three, recv_three, fwd_three,
        mlp_grads, mlp_half, mlp_sum, mlp_parts,
        grad_hidden, grad_rows, out_grads, out_half, out_sum, out_parts,
        proj_grad, qkv_grads, qkv_half, qkv_sum, qkv_parts,
        part_four, recv_four, fwd_four, gain_send, gain_recv, gain_group,
        load_sem, send_sem, recv_sem,
    ) = refs
    me_d, me_t = lax.axis_index("dp"), lax.axis_index("tensor")
    zrow, col = me_d // 2, lax.rem(me_d, 2)
    x_peer = zrow * 2 + 1 - col
    yrow, core = me_t // 2, lax.rem(me_t, 2)
    c_peer = yrow * 2 + 1 - core
    counter = [0]
    sent = []

    def make(source, target, axis, peer):
        index = counter[0]
        counter[0] += 1
        return pltpu.make_async_remote_copy(
            src_ref=source,
            dst_ref=target,
            send_sem=send_sem.at[index],
            recv_sem=recv_sem.at[index],
            device_id={axis: peer},
            device_id_type=pl.DeviceIdType.MESH,
        )

    def send(source, target, axis, peer):
        copy = make(source, target, axis, peer)
        copy.start()
        sent.append((copy, None))
        return copy

    def begin(copy, condition):
        pl.when(condition)(copy.start)
        sent.append((copy, condition))

    cuts = 2 if block % 32 == 0 else 1
    height = block // cuts

    class Chain:
        def __init__(self, buffer):
            self.buffer = buffer
            self.moves = {}
            last = outer - 1
            for step in range(1, outer):
                for side in (0, 1):
                    ahead = 1 if side == 0 else outer - 1
                    target = lax.rem(zrow + ahead, outer) * 2 + col
                    back = step - 1 if side else outer - step + 1
                    carried = lax.rem(zrow + back, outer) * 2 + col
                    origin = lax.rem(zrow + (step if side else outer - step), outer) * 2
                    lands = zrow + step <= last if side else zrow >= step
                    starts = (
                        (zrow >= 1) & (zrow + step - 1 <= last)
                        if side
                        else (zrow < last) & (zrow >= step - 1)
                    )
                    for cut in range(cuts):
                        self.moves[step, side, cut] = (
                            make(self.piece(carried, cut), self.piece(carried, cut), "dp", target),
                            make(
                                self.piece(origin + col, cut),
                                self.piece(origin + col, cut),
                                "dp",
                                x_peer,
                            ),
                            starts,
                            lands,
                            origin,
                        )

        def piece(self, index, cut):
            return self.buffer.at[index, cut * height : (cut + 1) * height]

        def start(self):
            self.own = []
            for cut in range(cuts):
                for side in (0, 1):
                    move, _, starts, _, _ = self.moves[1, side, cut]
                    begin(move, starts)
                piece = self.piece(me_d, cut)
                self.own.append(send(piece, piece, "dp", x_peer))

        def step(self, number):
            for cut in range(cuts):
                for side in (0, 1):
                    move, across, _, lands, _ = self.moves[number, side, cut]
                    pl.when(lands)(move.wait_recv)
                    if number + 1 < outer:
                        onward, _, starts, _, _ = self.moves[number + 1, side, cut]
                        begin(onward, starts)
                    begin(across, lands)

        def paired(self, number, then=None):
            for side in (0, 1):
                lands, origin = self.moves[number, side, 0][3:]

                @pl.when(lands)
                def _():
                    for cut in range(cuts):
                        self.moves[number, side, cut][1].wait_recv()
                    if then is not None:
                        then(origin + 1 - col)

    loads = [
        pltpu.make_async_copy(source, target, load_sem.at[index])
        for index, (source, target) in enumerate(
            [
                (qkv_in, qkv_raw), (out_in, out_raw), (attn_in, attn_raw), (mlp_in, mlp_raw),
                (tok_in, tok_buf.at[me_t]), (cot_in, cot_buf.at[me_t]),
                (up_in, up_raw), (down_in, down_raw), (table_in, table),
            ]
        )
    ]
    for load in loads:
        load.start()
    barrier = pltpu.get_barrier_semaphore()
    for axis, me in (("dp", me_d), ("tensor", me_t)):
        for shift in range(1, sizes[axis]):
            pl.semaphore_signal(
                barrier,
                inc=1,
                device_id={axis: lax.rem(me + shift, sizes[axis])},
                device_id_type=pl.DeviceIdType.MESH,
            )
    eye_heads = jnp.where(
        lanes((heads_wide, heads_wide), 0) == lanes((heads_wide, heads_wide), 1), 1.0, 0.0
    ).astype(bf16)
    for load in loads[:4]:
        load.wait()
    gain_buf[me_d] = jnp.zeros(gain_buf.shape[1:], bf16)
    gain_buf[me_d, 0:1, :block] = attn_raw[...]
    gain_buf[me_d, 8:9, :block] = mlp_raw[...]
    for which in range(3):
        w_a[me_d, :, which * heads_wide : (which + 1) * heads_wide] = qkv_raw[which]
    w_a[me_d, :, 3 * heads_wide :] = dot_f32(out_raw[...], eye_heads, 0, 0).astype(bf16)
    pl.semaphore_wait(barrier, groups + members - 2)

    def dp_spread(buffer):
        copies = []
        for shift in range(1, outer):
            peer = lax.rem(zrow + shift, outer) * 2 + col
            origin = lax.rem(zrow + outer - shift, outer) * 2 + col
            copies.append((send(buffer.at[me_d], buffer.at[me_d], "dp", peer), origin))
        return copies

    def dp_pair(buffer, origin):
        mirrored = origin // 2 * 2 + 1 - col
        return (send(buffer.at[origin], buffer.at[origin], "dp", x_peer), mirrored)

    def tensor_spread(buffer, span=slice(0, own_rows)):
        copies = []
        own = buffer.at[me_t, span]
        for shift in range(1, rings):
            peer = lax.rem(yrow + shift, rings) * 2 + core
            origin = lax.rem(yrow + rings - shift, rings) * 2 + core
            copies.append((send(own, own, "tensor", peer), origin))
        near = send(own, own, "tensor", c_peer)
        return copies, near

    def tensor_relay(buffer, copies, span=slice(0, own_rows)):
        onward = []
        for copy, origin in copies:
            copy.wait_recv()
            piece = buffer.at[origin, span]
            onward.append(send(piece, piece, "tensor", c_peer))
        return onward

    gain_z = dp_spread(gain_buf)
    gain_x = [dp_pair(gain_buf, me_d)]
    chain_a = Chain(w_a)
    chain_a.start()
    for load in loads[4:6]:
        load.wait()
    tok_y, tok_near = tensor_spread(tok_buf)
    cot_y, cot_near = tensor_spread(cot_buf)
    for load in loads[6:]:
        load.wait()
    eye_hidden = jnp.where(
        lanes((hidden, hidden), 0) == lanes((hidden, hidden), 1), 1.0, 0.0
    ).astype(bf16)
    for which in range(2):
        w_b[me_d, :, which * hidden : (which + 1) * hidden] = up_raw[which]
    w_b[me_d, :, 2 * hidden : 3 * hidden] = dot_f32(down_raw[...], eye_hidden, 0, 0).astype(bf16)
    if pad_hidden > 3 * hidden:
        w_b[me_d, :, 3 * hidden :] = jnp.zeros((block, pad_hidden - 3 * hidden), bf16)
    chain_b = Chain(w_b)

    turn = spread_matrix(head_count, True, 1.0)
    plain = spread_matrix(head_count, False, 1.0)

    def expand(index):
        for which, matrix in ((0, turn), (1, turn), (2, plain)):
            piece = w_a[index, :, which * heads_wide : (which + 1) * heads_wide]
            w_big[index, :, which * spread : (which + 1) * spread] = dot_f32(
                piece, matrix, 1, 0
            ).astype(bf16)
        piece = w_a[index, :, 3 * heads_wide :]
        w_out_pad[index] = dot_f32(piece, plain, 1, 0).astype(bf16)

    expand(me_d)
    chain_a.step(1)
    for copy, origin in gain_z:
        copy.wait_recv()
        gain_x.append(dp_pair(gain_buf, origin))
    tok_far = tensor_relay(tok_buf, tok_y)
    for number in range(2, outer - 1):
        chain_a.step(number)
    for copy, _ in gain_x:
        copy.wait_recv()
    for index in range(groups):
        tile = gain_buf[index].astype(f32)
        gain_rows[0:1, index * block : (index + 1) * block] = tile[0:1, :block]
        gain_rows[8:9, index * block : (index + 1) * block] = tile[8:9, :block]
    attn_gain, mlp_gain = gain_rows[0:1, :], gain_rows[8:9, :]
    tok_near.wait_recv()
    for copy in tok_far:
        copy.wait_recv()
    all_rows = tok_buf[...].reshape(row_count, width).astype(f32)
    rows_one[...] = (normalize(all_rows)[0] * attn_gain).astype(bf16)
    if outer > 2:
        chain_a.step(outer - 1)
    chain_b.start()
    cot_far = tensor_relay(cot_buf, cot_y)
    for shift in range(1, outer):
        expand(lax.rem(zrow + shift, outer) * 2 + col)
    for copy in chain_a.own:
        copy.wait_recv()
    expand(x_peer)
    for number in range(1, outer):
        chain_a.paired(number, expand)

    paired = paired_matrix()
    rotary = table[...]
    for which in range(3):
        weight = w_big[:, :, which * spread : (which + 1) * spread].reshape(width, spread)
        projected = dot_f32(rows_one[...], weight, 1, 0)
        for head in range(head_count):
            piece = projected[:, head * 128 : (head + 1) * 128]
            if which == 2:
                v_buf[head] = piece.astype(bf16)
                continue
            turned = piece * rotary
            turned = (turned + pltpu.roll(turned, 64, 1)).astype(bf16)
            (q_buf, k_buf)[which][head] = turned
    chain_b.step(1)
    for head in range(head_count):
        scores = dot_f32(k_buf[head], q_buf[head], 1, 1) * (0.5 * HD ** (-0.5))
        peak = jnp.max(scores, axis=0, keepdims=True)
        powers = jnp.exp(scores - peak)
        share = powers * (1.0 / jnp.sum(powers, axis=0, keepdims=True))
        probs[head] = share
        mixed_t = dot_f32(v_buf[head], share.astype(bf16), 0, 0).astype(bf16)
        mix_t[head] = mixed_t
        mixed = jnp.transpose(mixed_t.astype(f32)).astype(bf16)
        mix[:, :, head * 128 : (head + 1) * 128] = mixed.reshape(members, own_rows, 128)
        mix_pack[:, head * HD : (head + 1) * HD] = mixed[:, :HD]

    every = slice(0, own_rows)
    if own_rows % 32 == 0:
        spans = (slice(0, own_rows // 2), slice(own_rows // 2, own_rows))
    else:
        spans = (every,)

    def reduce_far(part, recv, span=every):
        first = []
        for shift in range(1, rings):
            far = lax.rem(yrow + shift, rings)
            first.append(
                send(part.at[far * 2 + 1 - core, span], recv.at[shift, span], "tensor", c_peer)
            )
        return first

    def reduce_near(part, recv, span=every):
        return send(part.at[c_peer, span], recv.at[0, span], "tensor", c_peer)

    def reduce_middle(part, recv, fwd, first, span=every):
        second = []
        for shift in range(1, rings):
            far = lax.rem(yrow + shift, rings)
            first[shift - 1].wait_recv()
            fwd[shift, span] = (
                part[far * 2 + core, span].astype(f32) + recv[shift, span].astype(f32)
            ).astype(bf16)
            second.append(
                send(
                    fwd.at[shift, span],
                    recv.at[rings + shift, span],
                    "tensor",
                    far * 2 + core,
                )
            )
        return second

    def reduce_finish(part, recv, near, second, span=every):
        near.wait_recv()
        total = part[me_t, span].astype(f32) + recv[0, span].astype(f32)
        for shift in range(1, rings):
            second[shift - 1].wait_recv()
            total = total + recv[rings + shift, span].astype(f32)
        return total

    def project(part, ring, left, right):
        part[pl.ds(2 * ring, 2)] = (
            dot_f32(left, right, 1, 1).astype(bf16).reshape(2, own_rows, width)
        )

    out_weight = w_out_pad[...].reshape(width, spread)

    def mixed_ring(ring):
        return mix[pl.ds(2 * ring, 2)].reshape(2 * own_rows, spread)

    for shift in range(1, rings):
        far = lax.rem(yrow + shift, rings)
        project(part_one, far, mixed_ring(far), out_weight)
    first_one = [reduce_far(part_one, recv_one, span) for span in spans]
    project(part_one, yrow, mixed_ring(yrow), out_weight)
    near_one = [reduce_near(part_one, recv_one, span) for span in spans]
    second_one = [
        reduce_middle(part_one, recv_one, fwd_one, first, span)
        for first, span in zip(first_one, spans)
    ]
    for number in range(2, outer - 1):
        chain_b.step(number)
    for head in range(head_count):
        q_buf[head] = dot_f32(q_buf[head], paired, 1, 0).astype(bf16)
        k_buf[head] = dot_f32(k_buf[head], paired, 1, 0).astype(bf16)
    if outer > 2:
        chain_b.step(outer - 1)
    rows_y, rows_near = [], []
    for index, span in enumerate(spans):
        residual = tok_buf[me_t, span].astype(f32)
        hidden_res[span] = residual + reduce_finish(
            part_one, recv_one, near_one[index], second_one[index], span
        )
        normed_two = normalize(hidden_res[span])[0]
        rows_two[me_t, span] = (normed_two * mlp_gain).astype(bf16)
        far_copies, near_copy = tensor_spread(rows_two, span)
        rows_y.append(far_copies)
        rows_near.append(near_copy)
    cot_near.wait_recv()
    for copy in cot_far:
        copy.wait_recv()
    for copy in chain_b.own:
        copy.wait_recv()
    for number in range(1, outer):
        chain_b.paired(number)
    up_w[...] = w_b[:, :, :hidden].reshape(width, hidden)
    gate_w[...] = w_b[:, :, hidden : 2 * hidden].reshape(width, hidden)
    down_w[...] = w_b[:, :, 2 * hidden : 3 * hidden].reshape(width, hidden)

    def feed(ring):
        base = 2 * ring
        count = 2 * own_rows
        rows = rows_two[pl.ds(base, 2)].reshape(count, width)
        cot = cot_buf[pl.ds(base, 2)].reshape(count, width)
        inputs = dot_f32(rows, up_w[...], 1, 0)
        gate_part = dot_f32(rows, gate_w[...], 1, 0)
        grad_act = dot_f32(cot, down_w[...], 1, 0)
        activated, slope = gelu_pair(inputs)
        act_buf[ring] = (activated * gate_part).astype(bf16)
        grad_up = (grad_act * gate_part * slope).astype(bf16)
        grad_gate = (grad_act * activated).astype(bf16)
        up_grad[ring] = grad_up
        gate_grad[ring] = grad_gate
        part_two[pl.ds(base, 2)] = (
            (dot_f32(grad_up, up_w[...], 1, 1) + dot_f32(grad_gate, gate_w[...], 1, 1))
            .astype(bf16)
            .reshape(2, own_rows, width)
        )

    for copy in rows_near:
        copy.wait_recv()
    feed(yrow)
    rows_far = []
    for copies, span in zip(rows_y, spans):
        rows_far += tensor_relay(rows_two, copies, span)
    for copy in rows_far:
        copy.wait_recv()
    for shift in range(1, rings):
        feed(lax.rem(yrow + shift, rings))
    first_two = reduce_far(part_two, recv_two)
    near_two = reduce_near(part_two, recv_two)

    shifts = sorted(range(1, outer), key=lambda shift: abs(shift - outer // 2)) + [outer]

    def pair_start(grads, half):
        copies = []
        for shift in shifts:
            row = lax.rem(zrow + shift, outer)
            copies.append((send(grads.at[row * 2 + 1 - col], half.at[row], "dp", x_peer), row))
        return copies

    def pair_step(grads, half, sums, parts, copies, number):
        copy, row = copies[number]
        copy.wait_recv()
        value = (grads[row * 2 + col].astype(f32) + half[row].astype(f32)).astype(bf16)
        if number == outer - 1:
            parts[row] = value
            return []
        sums[row] = value
        return [send(sums.at[row], parts.at[zrow], "dp", row * 2 + col)]

    full_rows = rows_two[...].reshape(row_count, width)
    full_cot = cot_buf[...].reshape(row_count, width)
    for which, grad in ((0, up_grad), (1, gate_grad)):
        mlp_grads[:, :, which * hidden : (which + 1) * hidden] = (
            dot_f32(full_rows, grad[...].reshape(row_count, hidden), 0, 0)
            .astype(bf16)
            .reshape(groups, block, hidden)
        )
    full_act = act_buf[...].reshape(row_count, hidden)
    mlp_grads[:, :, 2 * hidden : 3 * hidden] = (
        dot_f32(full_cot, full_act, 0, 0).astype(bf16).reshape(groups, block, hidden)
    )
    if pad_hidden > 3 * hidden:
        mlp_grads[:, :, 3 * hidden :] = jnp.zeros(
            (groups, block, pad_hidden - 3 * hidden), bf16
        )
    mlp_pairs = pair_start(mlp_grads, mlp_half)
    second_two = reduce_middle(part_two, recv_two, fwd_two, first_two)
    part_three[...] = (
        dot_f32(full_act, down_w[...], 1, 1).astype(bf16).reshape(members, own_rows, width)
    )
    normed_two, inv_two = normalize(hidden_res[...])
    back_two = reduce_finish(part_two, recv_two, near_two, second_two)
    grad_res, mlp_gain_part = normalize_back(back_two, normed_two, inv_two, mlp_gain)
    grad_hidden[...] = cot_buf[me_t].astype(f32) + grad_res
    grad_rows[me_t] = grad_hidden[...].astype(bf16)
    grad_y, grad_near = tensor_spread(grad_rows)
    first_three = reduce_far(part_three, recv_three)
    near_three = reduce_near(part_three, recv_three)
    mlp_state = (mlp_grads, mlp_half, mlp_sum, mlp_parts, mlp_pairs)
    mlp_across = pair_step(*mlp_state, 0)
    for number in range(1, min(2, outer - 1)):
        mlp_across += pair_step(*mlp_state, number)
    grad_far = tensor_relay(grad_rows, grad_y)
    second_three = reduce_middle(part_three, recv_three, fwd_three, first_three)
    grad_near.wait_recv()
    for copy in grad_far:
        copy.wait_recv()
    full_grad = grad_rows[...].reshape(row_count, width)
    grad_mix = dot_f32(full_grad, out_weight, 1, 0).astype(bf16)
    out_grads[...] = (
        dot_f32(full_grad, mix_pack[...], 0, 0).astype(bf16).reshape(groups, block, heads_wide)
    )
    out_pairs = pair_start(out_grads, out_half)
    for number in range(2, outer - 1):
        mlp_across += pair_step(*mlp_state, number)
    scale = HD ** (-0.5)
    for head in range(head_count):
        grad_head = grad_mix[:, head * 128 : (head + 1) * 128]
        grad_head_t = jnp.transpose(grad_head.astype(f32))
        delta = jnp.sum(grad_head_t * mix_t[head].astype(f32), axis=0, keepdims=True)
        grad_probs = dot_f32(v_buf[head], grad_head, 1, 1)
        share = probs[head]
        grad_scores = (share * (grad_probs - delta)).astype(bf16)
        grad_v = dot_f32(share.astype(bf16), grad_head, 1, 0)
        grad_k = dot_f32(grad_scores, q_buf[head], 1, 0) * (rotary * scale)
        grad_k = grad_k + pltpu.roll(grad_k, 64, 1)
        grad_q = jnp.transpose(dot_f32(k_buf[head], grad_scores, 0, 0)) * (rotary * scale)
        grad_q = grad_q + pltpu.roll(grad_q, 64, 1)
        for which, value in enumerate((grad_q, grad_k, grad_v)):
            start = which * heads_wide + head * HD
            proj_grad[:, start : start + HD] = value[:, :HD].astype(bf16)
    qkv_grads[...] = (
        dot_f32(rows_one[...], proj_grad[...], 0, 0)
        .astype(bf16)
        .reshape(groups, block, 3 * heads_wide)
    )
    qkv_pairs = pair_start(qkv_grads, qkv_half)
    qkv_weight = w_a[:, :, : 3 * heads_wide].reshape(width, 3 * heads_wide)

    def grad_ring(ring):
        return proj_grad[pl.ds(pl.multiple_of(ring * 2 * own_rows, 2 * own_rows), 2 * own_rows)]

    for shift in range(1, rings):
        far = lax.rem(yrow + shift, rings)
        project(part_four, far, grad_ring(far), qkv_weight)
    first_four = reduce_far(part_four, recv_four)
    project(part_four, yrow, grad_ring(yrow), qkv_weight)
    near_four = reduce_near(part_four, recv_four)
    second_four = reduce_middle(part_four, recv_four, fwd_four, first_four)

    def total(parts, across):
        for copy in across:
            copy.wait_recv()
        return jnp.sum(parts[...].astype(f32), axis=0)

    mlp_across += pair_step(*mlp_state, outer - 1)
    mlp_out = reduce_finish(part_three, recv_three, near_three, second_three)
    output_ref[...] = (hidden_res[...] + mlp_out).astype(bf16)
    out_state = (out_grads, out_half, out_sum, out_parts, out_pairs)
    out_across = []
    for number in range(outer):
        out_across += pair_step(*out_state, number)
    residual = tok_buf[me_t].astype(f32)
    normed_one, inv_one = normalize(residual)
    back_one = reduce_finish(part_four, recv_four, near_four, second_four)
    grad_res, attn_gain_part = normalize_back(back_one, normed_one, inv_one, attn_gain)
    input_grad_ref[...] = grad_hidden[...] + grad_res
    gain_send[...] = jnp.zeros(gain_send.shape, f32)
    attn_row = attn_gain_part.reshape(1, width)
    mlp_row = mlp_gain_part.reshape(1, width)
    for index in range(groups):
        gain_send[index, 0:1, :block] = attn_row[:, index * block : (index + 1) * block]
        gain_send[index, 1:2, :block] = mlp_row[:, index * block : (index + 1) * block]
    gain_recv[me_d] = gain_send[me_d]
    gain_copies = []
    for shift in range(1, groups):
        peer = lax.rem(me_d + shift, groups)
        gain_copies.append(send(gain_send.at[peer], gain_recv.at[me_d], "dp", peer))
    mlp_grad_ref[...] = total(mlp_parts, mlp_across)
    qkv_state = (qkv_grads, qkv_half, qkv_sum, qkv_parts, qkv_pairs)
    qkv_across = pair_step(*qkv_state, 0)
    for number in range(1, outer - 1):
        qkv_across += pair_step(*qkv_state, number)
    gain_group[me_t] = total(gain_recv, gain_copies)
    gain_copies = []
    for shift in range(1, members):
        peer = lax.rem(me_t + shift, members)
        gain_copies.append(send(gain_group.at[me_t], gain_group.at[me_t], "tensor", peer))
    out_grad_ref[...] = total(out_parts, out_across)
    qkv_across += pair_step(*qkv_state, outer - 1)
    gain_ref[...] = total(gain_group, gain_copies)
    qkv_grad_ref[...] = total(qkv_parts, qkv_across)
    for copy, condition in sent:
        if condition is None:
            copy.wait_send()
        else:
            pl.when(condition)(copy.wait_send)


def rotary_table(row_count):
    position = (np.arange(row_count) % L).astype(np.float32)
    halves = np.arange(HD // 2).astype(np.float32)
    inverse = np.float32(ROPE_THETA) ** (np.float32(-2.0) * halves / np.float32(HD))
    angles = position[:, None] * inverse[None, :]
    return np.concatenate([np.cos(angles)] * 2 + [np.sin(angles)] * 2, axis=1).astype(np.float32)


def whole_layer(sizes, tokens, attn_gain, w_qkv, w_out, mlp_gain, w_in, w_down, cotangent):
    bf16, f32 = jnp.bfloat16, jnp.float32
    groups, members = sizes["dp"], sizes["tensor"]
    own_rows, width = tokens.shape
    block, heads_wide, hidden = w_qkv.shape[1], w_qkv.shape[2], w_in.shape[2]
    pad_hidden = -(-3 * hidden // 128) * 128
    row_count = own_rows * members
    head_count, spread = heads_wide // HD, 2 * heads_wide
    outer, rings = groups // 2, members // 2
    vmem = pltpu.VMEM
    parts = vmem((members, own_rows, width), bf16)
    arrived = vmem((2 * rings, own_rows, width), bf16)
    passed = vmem((rings, own_rows, width), bf16)
    heads = vmem((head_count, row_count, 128), bf16)
    ringed = vmem((rings, 2 * own_rows, hidden), bf16)

    def exchanged(wide):
        quarter = vmem((outer, block, wide), bf16)
        return [vmem((groups, block, wide), bf16), quarter, quarter, quarter]

    scratch = [
        parts, parts,
        vmem(w_qkv.shape, bf16), vmem(w_out.shape, bf16),
        vmem(w_in.shape, bf16), vmem(w_down.shape, bf16),
        vmem((1, block), bf16), vmem((1, block), bf16), vmem((row_count, 2 * HD), f32),
        vmem((groups, block, 4 * heads_wide), bf16),
        vmem((groups, block, pad_hidden), bf16),
        vmem((groups, 16, 128), bf16),
        vmem((16, width), f32),
        vmem((groups, block, 3 * spread), bf16),
        vmem((groups, block, spread), bf16),
        vmem((width, hidden), bf16), vmem((width, hidden), bf16), vmem((width, hidden), bf16),
        vmem((row_count, width), bf16),
        vmem((head_count, row_count, row_count), f32),
        heads, heads, heads,
        vmem((head_count, 128, row_count), bf16),
        vmem((members, own_rows, spread), bf16),
        vmem((row_count, heads_wide), bf16),
        parts, arrived, passed,
        vmem((own_rows, width), f32),
        parts,
        ringed, ringed, ringed,
        parts, arrived, passed,
        parts, arrived, passed,
        *exchanged(pad_hidden),
        vmem((own_rows, width), f32),
        parts,
        *exchanged(heads_wide),
        vmem((row_count, 3 * heads_wide), bf16),
        *exchanged(3 * heads_wide),
        parts, arrived, passed,
        vmem((groups, 8, 128), f32), vmem((groups, 8, 128), f32), vmem((members, 8, 128), f32),
    ]
    cuts = 2 if block % 32 == 0 else 1
    chains = 2 * cuts * (4 * (outer - 1) + 1)
    halves = 2 if own_rows % 32 == 0 else 1
    gathers = 2 * outer - 1 + chains + (3 + halves) * (2 * rings - 1)
    reduces = (3 + halves) * (2 * rings - 1) + 3 * (2 * outer - 1)
    slots = gathers + reduces + groups + members - 2
    dims = (own_rows, width, block, heads_wide, hidden, pad_hidden)
    output, input_grad, gains, qkv_sum, out_sum, mlp_sums = pl.pallas_call(
        functools.partial(layer_kernel, sizes, dims),
        out_shape=[
            jax.ShapeDtypeStruct((own_rows, width), bf16),
            jax.ShapeDtypeStruct((own_rows, width), f32),
            jax.ShapeDtypeStruct((8, 128), f32),
            jax.ShapeDtypeStruct((block, 3 * heads_wide), f32),
            jax.ShapeDtypeStruct((block, heads_wide), f32),
            jax.ShapeDtypeStruct((block, pad_hidden), f32),
        ],
        in_specs=[pl.BlockSpec(memory_space=pltpu.HBM)] * 9,
        out_specs=[pl.BlockSpec(memory_space=pltpu.VMEM)] * 6,
        scratch_shapes=scratch
        + [
            pltpu.SemaphoreType.DMA((9,)),
            pltpu.SemaphoreType.DMA((slots,)),
            pltpu.SemaphoreType.DMA((slots,)),
        ],
        compiler_params=pltpu.CompilerParams(
            collective_id=0, has_side_effects=True, vmem_limit_bytes=44 << 20
        ),
    )(
        *[
            pltpu.with_memory_space_constraint(array, pltpu.HBM)
            for array in (
                tokens, cotangent, w_qkv, w_out, w_in, w_down,
                attn_gain.reshape(1, block), mlp_gain.reshape(1, block),
                jnp.asarray(rotary_table(row_count)),
            )
        ]
    )
    results = pl.pallas_call(
        functools.partial(finish_kernel, hidden),
        out_shape=[
            jax.ShapeDtypeStruct(output.shape, bf16),
            jax.ShapeDtypeStruct(input_grad.shape, f32),
            jax.ShapeDtypeStruct(w_qkv.shape, f32),
            jax.ShapeDtypeStruct(w_out.shape, f32),
            jax.ShapeDtypeStruct(w_in.shape, f32),
            jax.ShapeDtypeStruct(w_down.shape, f32),
            jax.ShapeDtypeStruct((1, block), f32),
            jax.ShapeDtypeStruct((1, block), f32),
        ],
        in_specs=[pl.BlockSpec(memory_space=pltpu.VMEM)] * 6,
        out_specs=[pl.BlockSpec(memory_space=pltpu.HBM)] * 8,
        scratch_shapes=[
            vmem(w_qkv.shape, f32),
            vmem(w_out.shape, f32),
            vmem(w_in.shape, f32),
            vmem(w_down.shape, f32),
            vmem((1, block), f32),
            vmem((1, block), f32),
            pltpu.SemaphoreType.DMA((8,)),
        ],
        compiler_params=pltpu.CompilerParams(vmem_limit_bytes=16 << 20),
    )(output, input_grad, qkv_sum, out_sum, mlp_sums, gains)
    output, input_grad, grad_w_qkv, grad_w_out, grad_w_in, grad_w_down = results[:6]
    return (
        output,
        input_grad,
        results[6].reshape(block),
        grad_w_qkv,
        grad_w_out,
        results[7].reshape(block),
        grad_w_in,
        grad_w_down,
    )


def finish_kernel(hidden, *refs):
    (
        output, input_grad, qkv_sum, out_sum, mlp_sums, gains,
        output_to, input_grad_to, qkv_to, out_to, up_to, down_to, attn_to, mlp_to,
        qkv_buf, out_buf, up_buf, down_buf, attn_buf, mlp_buf, sems,
    ) = refs
    started = []

    def put(source, target):
        copy = pltpu.make_async_copy(source, target, sems.at[len(started)])
        copy.start()
        started.append(copy)

    put(output, output_to)
    put(input_grad, input_grad_to)
    attn_buf[...] = gains[0:1, : attn_buf.shape[1]]
    put(attn_buf, attn_to)
    mlp_buf[...] = gains[1:2, : mlp_buf.shape[1]]
    put(mlp_buf, mlp_to)
    heads_wide = out_sum.shape[1]
    for which in range(3):
        qkv_buf[which] = qkv_sum[:, which * heads_wide : (which + 1) * heads_wide]
    put(qkv_buf, qkv_to)
    for which in range(2):
        up_buf[which] = mlp_sums[:, which * hidden : (which + 1) * hidden]
    put(up_buf, up_to)
    out_buf[...] = jnp.transpose(out_sum[...])
    put(out_buf, out_to)
    down_buf[...] = jnp.transpose(mlp_sums[:, 2 * hidden : 3 * hidden])
    put(down_buf, down_to)
    for copy in started:
        copy.wait()


def fits_whole(sizes, tokens, w_qkv):
    row_count = tokens.shape[0] * sizes["tensor"]
    even = sizes["dp"] % 2 == 0 and sizes["tensor"] % 2 == 0
    tiled = w_qkv.shape[1] % 16 == 0 and tokens.shape[0] % 16 == 0
    return even and tiled and row_count == L and w_qkv.shape[1] <= 128


def layer(sizes, tokens, attn_gain, w_qkv, *rest):
    run = whole_layer if fits_whole(sizes, tokens, w_qkv) else body
    return run(sizes, tokens, attn_gain, w_qkv, *rest)


def solution(mesh):
    in_specs = (
        P(("dp", "tensor"), None),
        P("dp"),
        P(None, "dp", "tensor"),
        P("tensor", "dp"),
        P("dp"),
        P(None, "dp", "tensor"),
        P("tensor", "dp"),
        P(("dp", "tensor"), None),
    )
    out_specs = (
        P(("dp", "tensor"), None),
        P(("dp", "tensor"), None),
        P("dp"),
        P(None, "dp", "tensor"),
        P("tensor", "dp"),
        P("dp"),
        P(None, "dp", "tensor"),
        P("tensor", "dp"),
    )
    sizes = {axis: mesh.shape[axis] for axis in ("dp", "tensor")}
    return jax.shard_map(functools.partial(layer, sizes), mesh=mesh, in_specs=in_specs, out_specs=out_specs, check_vma=False)
```

```python
import functools

import jax
import jax.numpy as jnp
import numpy as np
from jax import lax
from jax.experimental import pallas as pl
from jax.experimental.pallas import tpu as pltpu
from jax.experimental.layout import Layout, with_layout_constraint
from jax.sharding import PartitionSpec as P

HD = 64
L = 512


NORM_EPS = 1e-05
ROPE_THETA = 160000.0
SQRT_HALF = 0.7071067811865476
GAUSS_NORM = 0.3989422804014327


def rope_tables(row_count):
    position = (jnp.arange(row_count) % L).astype(jnp.float32)
    halves = jnp.arange(HD // 2).astype(jnp.float32)
    inverse = ROPE_THETA ** (-2.0 * halves / HD)
    angles = position[:, None] * inverse[None, :]
    angles = jnp.concatenate([angles, angles], axis=1)
    return (jnp.cos(angles)[:, None, :], jnp.sin(angles)[:, None, :])


def rotate(field_rows, cos_table, sin_table):
    first_half = field_rows[..., : HD // 2]
    second_half = field_rows[..., HD // 2 :]
    turned = jnp.concatenate([-second_half, first_half], axis=-1)
    return field_rows * cos_table + turned * sin_table


def rotate_back(grad_field, cos_table, sin_table):
    scaled = grad_field * sin_table
    turned = jnp.concatenate([scaled[..., HD // 2 :], -scaled[..., : HD // 2]], axis=-1)
    return grad_field * cos_table + turned


def normalize(values):
    centred = values - jnp.mean(values, axis=-1, keepdims=True)
    inv_std = lax.rsqrt(jnp.mean(centred * centred, axis=-1, keepdims=True) + NORM_EPS)
    return (centred * inv_std, inv_std)


def normalize_back(grad_norm, normed, inv_std, gain_row):
    gain_part = jnp.sum(grad_norm * normed, axis=0)
    scaled = grad_norm * gain_row
    centred = scaled - jnp.mean(scaled, axis=-1, keepdims=True)
    grad_in = inv_std * (centred - normed * jnp.mean(scaled * normed, axis=-1, keepdims=True))
    return (grad_in, gain_part)


def gelu_pair(inputs):
    normal_cdf = 0.5 * (1.0 + lax.erf(inputs * SQRT_HALF))
    return (inputs * normal_cdf, normal_cdf + inputs * jnp.exp(-0.5 * inputs * inputs) * GAUSS_NORM)


def attend(queries, key_rows, value_rows):
    score_scale = HD ** (-0.5)
    scores = (
        jnp.einsum("qhd,khd->hqk", queries, key_rows, preferred_element_type=jnp.float32)
        * score_scale
    )
    row_max = jnp.max(scores, axis=-1, keepdims=True)
    log_total = row_max + jnp.log(jnp.sum(jnp.exp(scores - row_max), axis=-1, keepdims=True))
    weights = jnp.exp(scores - log_total).astype(jnp.bfloat16)
    attn_mix = jnp.einsum(
        "hqk,khd->qhd", weights, value_rows, preferred_element_type=jnp.float32
    ).astype(jnp.bfloat16)
    return (attn_mix, log_total)


def attend_back(queries, key_rows, value_rows, attn_mix, grad_mix, log_total):
    score_scale = HD ** (-0.5)
    scores = (
        jnp.einsum("qhd,khd->hqk", queries, key_rows, preferred_element_type=jnp.float32)
        * score_scale
    )
    probabilities = jnp.exp(scores - log_total)
    grad_probs = jnp.einsum(
        "qhd,khd->hqk", grad_mix, value_rows, preferred_element_type=jnp.float32
    )
    row_delta = jnp.sum(grad_mix.astype(jnp.float32) * attn_mix.astype(jnp.float32), axis=-1)
    grad_scores = (probabilities * (grad_probs - jnp.transpose(row_delta)[:, :, None])).astype(
        jnp.bfloat16
    )
    prob_rounded = probabilities.astype(jnp.bfloat16)
    grad_values = jnp.einsum(
        "hqk,qhd->khd", prob_rounded, grad_mix, preferred_element_type=jnp.float32
    )
    grad_queries = (
        jnp.einsum("hqk,khd->qhd", grad_scores, key_rows, preferred_element_type=jnp.float32)
        * score_scale
    )
    grad_keys = (
        jnp.einsum("hqk,qhd->khd", grad_scores, queries, preferred_element_type=jnp.float32)
        * score_scale
    )
    return (grad_queries, grad_keys, grad_values)


def exchange_kernel(plan, sizes, *refs):
    count = len(plan)
    sources, targets = refs[:count], refs[count : 2 * count]
    own_sem, send_sem, recv_sem = refs[2 * count :]
    axes = sorted({axis for _, axis, _ in plan})
    barrier = pltpu.get_barrier_semaphore()
    total = 0
    for axis in axes:
        me = lax.axis_index(axis)
        for shift in range(1, sizes[axis]):
            pl.semaphore_signal(
                barrier,
                inc=1,
                device_id={axis: lax.rem(me + shift, sizes[axis])},
                device_id_type=pl.DeviceIdType.MESH,
            )
            total += 1
    pl.semaphore_wait(barrier, total)
    slot = 0
    pending, relays, local = [], [], []

    def remote(source, target, axis, peer, index):
        return pltpu.make_async_remote_copy(
            src_ref=source,
            dst_ref=target,
            send_sem=send_sem.at[index],
            recv_sem=recv_sem.at[index],
            device_id={axis: peer},
            device_id_type=pl.DeviceIdType.MESH,
        )

    for which, (kind, axis, span) in enumerate(plan):
        size = sizes[axis]
        me = lax.axis_index(axis)
        source, target = sources[which], targets[which]
        outer = size // 2
        column = lax.rem(me, 2)
        row = me // 2
        partner = row * 2 + 1 - column
        if kind == "half":
            copy = remote(source.at[:, 1 - column, :, span], target, axis, partner, slot)
            copy.start()
            pending.append(copy)
            slot += 1
            continue
        if kind == "outer":
            for shift in range(1, outer):
                other = lax.rem(row + shift, outer)
                copy = remote(source.at[other], target.at[row], axis, other * 2 + column, slot)
                copy.start()
                pending.append(copy)
                slot += 1
            copy = pltpu.make_async_copy(source.at[row], target.at[row], own_sem.at[which])
            copy.start()
            local.append(copy)
            continue
        if kind == "relay":
            for shift in range(1, outer):
                peer = lax.rem(row + shift, outer) * 2 + column
                copy = remote(source, target.at[me], axis, peer, slot)
                copy.start()
                origin = lax.rem(row + outer - shift, outer) * 2 + column
                relays.append((copy, target, axis, origin, partner, slot + 1))
                slot += 2
            copy = remote(source, target.at[me], axis, partner, slot)
            copy.start()
            pending.append(copy)
            slot += 1
        else:
            for shift in range(1, size):
                peer = lax.rem(me + shift, size)
                piece = source if kind == "gather" else source.at[peer, :, span]
                copy = remote(piece, target.at[me], axis, peer, slot)
                copy.start()
                pending.append(copy)
                slot += 1
        piece = source if kind != "scatter" else source.at[me, :, span]
        copy = pltpu.make_async_copy(piece, target.at[me], own_sem.at[which])
        copy.start()
        local.append(copy)
    for copy, target, axis, origin, partner, index in relays:
        copy.wait_recv()
        onward = remote(target.at[origin], target.at[origin], axis, partner, index)
        onward.start()
        pending.append(onward)
    for copy, *_ in relays:
        copy.wait_send()
    for copy in pending + local:
        copy.wait()


def slots_of(kind, size):
    outer = size // 2
    return {"relay": 2 * outer - 1, "half": 1, "outer": outer - 1}.get(kind, size - 1)


def shape_of(kind, size, shape, wide):
    if kind == "half":
        return (shape[0], shape[2], wide)
    return {"scatter": shape[:-1] + (wide,), "outer": shape}.get(kind, (size,) + shape)


def exchange(sizes, number, *ops):
    arrays = [op[2] for op in ops]
    spans = [slice(*op[3]) if len(op) > 3 else slice(0, op[2].shape[-1]) for op in ops]
    plan = tuple((op[0], op[1], span) for op, span in zip(ops, spans))
    shapes = [
        jax.ShapeDtypeStruct(
            shape_of(kind, sizes[axis], array.shape, span.stop - span.start), array.dtype
        )
        for (kind, axis, span), array in zip(plan, arrays)
    ]
    slots = sum(slots_of(kind, sizes[axis]) for kind, axis, _ in plan)
    return pl.pallas_call(
        functools.partial(exchange_kernel, plan, sizes),
        out_shape=shapes,
        in_specs=[pl.BlockSpec(memory_space=pltpu.VMEM)] * len(arrays),
        out_specs=[pl.BlockSpec(memory_space=pltpu.VMEM)] * len(arrays),
        scratch_shapes=[
            pltpu.SemaphoreType.DMA((len(arrays),)),
            pltpu.SemaphoreType.DMA((slots,)),
            pltpu.SemaphoreType.DMA((slots,)),
        ],
        compiler_params=pltpu.CompilerParams(
            collective_id=number, has_side_effects=True, vmem_limit_bytes=48 << 20
        ),
    )(*arrays)


def pad_columns(array, multiple=128):
    extra = -array.shape[-1] % multiple
    return jnp.pad(array, [(0, 0)] * (array.ndim - 1) + [(0, extra)])


def total_of(pieces):
    return jnp.sum(pieces.astype(jnp.float32), axis=0)


def row_major(array):
    return with_layout_constraint(array, Layout(major_to_minor=(0, 1)))


def dot_f32(left, right, left_dim, right_dim):
    return lax.dot_general(
        left, right, (((left_dim,), (right_dim,)), ((), ())), preferred_element_type=jnp.float32
    )


def feed_forward_kernel(
    hidden, rows_ref, up_ref, gate_ref, down_ref, cot_ref, mlp_ref, back_ref, grads_ref
):
    bf16 = jnp.bfloat16
    rows, cot = rows_ref[...], cot_ref[...]
    inputs = dot_f32(rows, up_ref[...], 1, 0)
    gate_part = dot_f32(rows, gate_ref[...], 1, 0)
    activated, gelu_slope = gelu_pair(inputs)
    hidden_act = (activated * gate_part).astype(bf16)
    mlp_ref[...] = dot_f32(hidden_act, down_ref[...], 1, 1).astype(bf16)
    grad_act = dot_f32(cot, down_ref[...], 1, 0)
    grad_up = (grad_act * gate_part * gelu_slope).astype(bf16)
    grad_gate = (grad_act * activated).astype(bf16)
    back_ref[...] = (
        dot_f32(grad_up, up_ref[...], 1, 1) + dot_f32(grad_gate, gate_ref[...], 1, 1)
    ).astype(bf16)
    grads_ref[:, :hidden] = dot_f32(rows, grad_up, 0, 0).astype(bf16)
    grads_ref[:, hidden : 2 * hidden] = dot_f32(rows, grad_gate, 0, 0).astype(bf16)
    grads_ref[:, 2 * hidden : 3 * hidden] = dot_f32(cot, hidden_act, 0, 0).astype(bf16)
    spare = grads_ref.shape[1] - 3 * hidden
    if spare:
        grads_ref[:, 3 * hidden :] = jnp.zeros((grads_ref.shape[0], spare), bf16)


def feed_forward(hidden, rows, up, gate, down_t, cot):
    row_count, width = rows.shape
    padded = -(-3 * hidden // 128) * 128
    return pl.pallas_call(
        functools.partial(feed_forward_kernel, hidden),
        out_shape=[
            jax.ShapeDtypeStruct((row_count, width), jnp.bfloat16),
            jax.ShapeDtypeStruct((row_count, width), jnp.bfloat16),
            jax.ShapeDtypeStruct((width, padded), jnp.bfloat16),
        ],
        in_specs=[pl.BlockSpec(memory_space=pltpu.VMEM)] * 5,
        out_specs=[pl.BlockSpec(memory_space=pltpu.VMEM)] * 3,
        compiler_params=pltpu.CompilerParams(vmem_limit_bytes=48 << 20),
    )(rows, up, gate, down_t, cot)


def body(sizes, tokens, attn_gain, w_qkv, w_out, mlp_gain, w_in, w_down, cotangent):
    bf16, f32 = jnp.bfloat16, jnp.float32
    groups, members = sizes["dp"], sizes["tensor"]
    block = w_qkv.shape[1]
    width = block * groups
    heads_wide, hidden = w_qkv.shape[2], w_in.shape[2]
    own_rows = tokens.shape[0]
    packed = jnp.concatenate([w_qkv[0], w_qkv[1], w_qkv[2], w_out.T], axis=1)
    gain_tile = jnp.pad(jnp.stack([attn_gain, mlp_gain]), [(0, 14), (0, -block % 128)])
    weights, gain_tiles, token_rows, grad_rows = exchange(
        sizes,
        0,
        ("relay", "dp", packed),
        ("relay", "dp", gain_tile),
        ("relay", "tensor", tokens),
        ("relay", "tensor", cotangent),
    )
    weights = weights.reshape(width, -1)
    qkv_weight = weights[:, : 3 * heads_wide]
    out_weight_t = weights[:, 3 * heads_wide :]
    attn_full = gain_tiles[:, 0, :block].reshape(1, width).astype(f32)
    mlp_full = gain_tiles[:, 1, :block].reshape(1, width).astype(f32)
    outer = groups // 2
    column = lax.rem(lax.axis_index("dp"), 2)

    def quarter(array):
        return array.reshape(outer, 2, block, -1)

    def half_sum(array, received, low, high):
        own = lax.dynamic_index_in_dim(quarter(array)[..., low:high], column, 1, keepdims=False)
        return (own.astype(f32) + received.astype(f32)).astype(bf16)

    row_count = own_rows * members
    grad_rows = grad_rows.reshape(row_count, width)
    residual = tokens.astype(f32)
    normed_one, inv_one = normalize(residual)
    rows_one = (normalize(token_rows.reshape(row_count, width).astype(f32))[0] * attn_full).astype(bf16)
    head_count = heads_wide // HD
    head_shape = (row_count, head_count, HD)
    seq_shape = (row_count // L, L, head_count, HD)
    flat_shape = (row_count, heads_wide)
    cos_table, sin_table = rope_tables(row_count)
    projected = dot_f32(rows_one, qkv_weight, 1, 0)
    pieces = [projected[:, i * heads_wide : (i + 1) * heads_wide].reshape(head_shape) for i in range(3)]
    queries = rotate(pieces[0], cos_table, sin_table).astype(bf16).reshape(seq_shape)
    key_rows = rotate(pieces[1], cos_table, sin_table).astype(bf16).reshape(seq_shape)
    value_rows = pieces[2].astype(bf16).reshape(seq_shape)
    one_seq = row_count == L

    def over_sequences(function, arrays):
        if one_seq:
            results = function(*[array[0] for array in arrays])
            return tuple(result[None] for result in results)
        return lax.map(lambda seq_block: function(*seq_block), arrays)

    attn_mix, log_total = over_sequences(attend, (queries, key_rows, value_rows))
    mixed_rows = attn_mix.reshape(flat_shape)
    attn_part = dot_f32(mixed_rows, out_weight_t, 1, 1).astype(bf16)
    attn_parts, up_weight, down_weight_t = exchange(
        sizes,
        1,
        ("scatter", "tensor", attn_part.reshape(members, own_rows, width)),
        ("relay", "dp", w_in[0]),
        ("relay", "dp", w_down.T),
    )
    up_weight = up_weight.reshape(width, -1)
    down_weight_t = down_weight_t.reshape(width, -1)
    hidden_res = residual + total_of(attn_parts)
    normed_two, inv_two = normalize(hidden_res)
    ln_two = (normed_two * mlp_full).astype(bf16)
    rows_two, gate_weight = exchange(
        sizes, 2, ("relay", "tensor", ln_two), ("relay", "dp", w_in[1])
    )
    gate_weight = gate_weight.reshape(width, -1)
    rows_two = rows_two.reshape(row_count, width)
    mlp_part, ln_two_part, mlp_grads = feed_forward(
        hidden, rows_two, up_weight, gate_weight, down_weight_t, grad_rows
    )
    mlp_wide = mlp_grads.shape[-1]
    first = mlp_wide // 256 * 128
    ln_two_parts, mlp_grads_a = exchange(
        sizes,
        3,
        ("scatter", "tensor", ln_two_part.reshape(members, own_rows, width)),
        ("half", "dp", quarter(mlp_grads), (0, first)),
    )
    grad_res_two, mlp_gain_part = normalize_back(total_of(ln_two_parts), normed_two, inv_two, mlp_full)
    grad_hidden = cotangent.astype(f32) + grad_res_two
    grad_hidden_rows, mlp_grads_b, mlp_sums_a = exchange(
        sizes,
        4,
        ("relay", "tensor", grad_hidden.astype(bf16)),
        ("half", "dp", quarter(mlp_grads), (first, mlp_wide)),
        ("outer", "dp", half_sum(mlp_grads, mlp_grads_a, 0, first)),
    )
    grad_hidden_rows = grad_hidden_rows.reshape(row_count, width)
    grad_out_t = row_major(dot_f32(grad_hidden_rows, mixed_rows, 0, 0).astype(bf16))
    grad_mix = dot_f32(grad_hidden_rows, out_weight_t, 1, 0).astype(bf16).reshape(seq_shape)
    grad_q, grad_k, grad_v = over_sequences(
        attend_back, (queries, key_rows, value_rows, attn_mix, grad_mix, log_total)
    )
    grad_proj = jnp.concatenate(
        [
            rotate_back(grad_q.reshape(head_shape), cos_table, sin_table).reshape(flat_shape),
            rotate_back(grad_k.reshape(head_shape), cos_table, sin_table).reshape(flat_shape),
            grad_v.reshape(flat_shape),
        ],
        axis=1,
    ).astype(bf16)
    grad_qkv = row_major(dot_f32(rows_one, grad_proj, 0, 0).astype(bf16))
    ln_one_part = dot_f32(grad_proj, qkv_weight, 1, 1).astype(bf16)
    ln_one_parts, mlp_sums_b, grad_out_half, qkv_half = exchange(
        sizes,
        5,
        ("scatter", "tensor", ln_one_part.reshape(members, own_rows, width)),
        ("outer", "dp", half_sum(mlp_grads, mlp_grads_b, first, mlp_wide)),
        ("half", "dp", quarter(grad_out_t)),
        ("half", "dp", quarter(grad_qkv)),
    )
    grad_res_one, attn_gain_part = normalize_back(total_of(ln_one_parts), normed_one, inv_one, attn_full)
    input_grad = grad_hidden + grad_res_one
    gain_parts = jnp.stack([attn_gain_part, mlp_gain_part] + [jnp.zeros_like(attn_gain_part)] * 6)
    gain_parts = pad_columns(jnp.swapaxes(gain_parts.reshape(8, groups, block), 0, 1))
    late_parts, gain_parts, mlp_parts, grad_out_parts = exchange(
        sizes,
        6,
        ("outer", "dp", half_sum(grad_qkv, qkv_half, 0, 3 * heads_wide)),
        ("scatter", "dp", gain_parts),
        ("scatter", "tensor", mlp_part.reshape(members, own_rows, width)),
        ("outer", "dp", half_sum(grad_out_t, grad_out_half, 0, heads_wide)),
    )
    output = (hidden_res + total_of(mlp_parts)).astype(bf16)
    (gain_groups,) = exchange(sizes, 7, ("gather", "tensor", total_of(gain_parts)))
    gain_sum = total_of(gain_groups)
    late = total_of(late_parts)
    grad_w_qkv = jnp.stack([late[:, i * heads_wide : (i + 1) * heads_wide] for i in range(3)])
    grad_w_out = total_of(grad_out_parts).T
    mlp_sums = jnp.concatenate(
        [total_of(mlp_sums_a), total_of(mlp_sums_b)], axis=1
    )
    grad_w_in = jnp.stack([mlp_sums[:, :hidden], mlp_sums[:, hidden : 2 * hidden]])
    grad_w_down = mlp_sums[:, 2 * hidden : 3 * hidden].T
    return (
        output,
        input_grad,
        gain_sum[0, :block],
        grad_w_qkv,
        grad_w_out,
        gain_sum[1, :block],
        grad_w_in,
        grad_w_down,
    )


def lanes(shape, dim):
    return lax.broadcasted_iota(jnp.int32, shape, dim)


def spread_matrix(head_count, turned, sign):
    shape = (head_count * HD, head_count * 2 * HD)
    row, column = lanes(shape, 0), lanes(shape, 1)
    head = lax.shift_right_logical(column, 7)
    feature = lax.bitwise_and(column, HD - 1)
    upper = lax.bitwise_and(column, 2 * HD - 1) >= HD
    plain = row == head * HD + feature
    if not turned:
        return jnp.where(plain & jnp.logical_not(upper), 1.0, 0.0).astype(jnp.bfloat16)
    other = row == head * HD + lax.bitwise_and(feature + HD // 2, HD - 1)
    signed = jnp.where(feature < HD // 2, -sign, sign)
    return jnp.where(
        upper, jnp.where(other, signed, 0.0), jnp.where(plain, 1.0, 0.0)
    ).astype(jnp.bfloat16)


def paired_matrix():
    shape = (2 * HD, 2 * HD)
    row, column = lanes(shape, 0), lanes(shape, 1)
    feature = lax.bitwise_and(column, HD - 1)
    upper = column >= HD
    other = row == lax.bitwise_and(feature + HD // 2, HD - 1)
    signed = jnp.where(feature < HD // 2, 1.0, -1.0)
    return jnp.where(
        upper, jnp.where(other, signed, 0.0), jnp.where(row == column, 1.0, 0.0)
    ).astype(jnp.bfloat16)


def layer_kernel(sizes, dims, *refs):
    bf16, f32 = jnp.bfloat16, jnp.float32
    groups, members = sizes["dp"], sizes["tensor"]
    own_rows, width, block, heads_wide, hidden, pad_hidden = dims
    head_count = heads_wide // HD
    spread = 2 * heads_wide
    side = -3 * heads_wide % 128
    row_count = own_rows * members
    outer, rings = groups // 2, members // 2
    (
        tok_in, cot_in, qkv_in, out_in, up_in, down_in, attn_in, mlp_in, table_in,
        output_ref, input_grad_ref, gain_ref, qkv_grad_ref, out_grad_ref, mlp_grad_ref,
        tok_buf, cot_buf, qkv_raw, out_raw, up_raw, down_raw, attn_raw, mlp_raw, table,
        w_a, w_b, w_c, gain_buf, gain_rows, w_big, w_out_pad, up_w, gate_w, down_w,
        rows_one, probs, q_buf, k_buf, v_buf, mix_t, mix, mix_pack,
        part_one, recv_one, fwd_one, hidden_res, rows_two,
        act_buf, up_grad, gate_grad, part_two, recv_two, fwd_two,
        part_three, recv_three, fwd_three,
        mlp_grads, mlp_half, mlp_sum, mlp_parts,
        grad_hidden, grad_rows, out_grads, out_half, out_sum, out_parts,
        proj_grad, qk_grads, qk_half, qk_sum, qk_parts,
        vo_grads, vo_half, vo_sum, vo_parts,
        part_four, recv_four, fwd_four, gain_send, gain_recv, gain_group,
        load_sem, send_sem, recv_sem,
    ) = refs
    me_d, me_t = lax.axis_index("dp"), lax.axis_index("tensor")
    zrow, col = me_d // 2, lax.rem(me_d, 2)
    x_peer = zrow * 2 + 1 - col
    yrow, core = me_t // 2, lax.rem(me_t, 2)
    c_peer = yrow * 2 + 1 - core
    counter = [0]
    sent = []

    def make(source, target, axis, peer):
        index = counter[0]
        counter[0] += 1
        return pltpu.make_async_remote_copy(
            src_ref=source,
            dst_ref=target,
            send_sem=send_sem.at[index],
            recv_sem=recv_sem.at[index],
            device_id={axis: peer},
            device_id_type=pl.DeviceIdType.MESH,
        )

    def send(source, target, axis, peer):
        copy = make(source, target, axis, peer)
        copy.start()
        sent.append((copy, None))
        return copy

    def begin(copy, condition):
        pl.when(condition)(copy.start)
        sent.append((copy, condition))

    cuts = 2 if block % 32 == 0 else 1
    height = block // cuts

    class Chain:
        def __init__(self, buffer):
            self.buffer = buffer
            self.moves = {}
            last = outer - 1
            for step in range(1, outer):
                for way in (0, 1):
                    ahead = 1 if way == 0 else outer - 1
                    target = lax.rem(zrow + ahead, outer) * 2 + col
                    back = step - 1 if way else outer - step + 1
                    carried = lax.rem(zrow + back, outer) * 2 + col
                    origin = lax.rem(zrow + (step if way else outer - step), outer) * 2
                    lands = zrow + step <= last if way else zrow >= step
                    starts = (
                        (zrow >= 1) & (zrow + step - 1 <= last)
                        if way
                        else (zrow < last) & (zrow >= step - 1)
                    )
                    for cut in range(cuts):
                        self.moves[step, way, cut] = (
                            make(self.piece(carried, cut), self.piece(carried, cut), "dp", target),
                            make(
                                self.piece(origin + col, cut),
                                self.piece(origin + col, cut),
                                "dp",
                                x_peer,
                            ),
                            starts,
                            lands,
                            origin,
                        )

        def piece(self, index, cut):
            return self.buffer.at[index, cut * height : (cut + 1) * height]

        def start(self):
            for cut in range(cuts):
                for way in (0, 1):
                    move, _, starts, _, _ = self.moves[1, way, cut]
                    begin(move, starts)

        def start_pair(self):
            self.own = []
            for cut in range(cuts):
                piece = self.piece(me_d, cut)
                self.own.append(send(piece, piece, "dp", x_peer))

        def step(self, number):
            for cut in range(cuts):
                for way in (0, 1):
                    move, across, _, lands, _ = self.moves[number, way, cut]
                    pl.when(lands)(move.wait_recv)
                    if number + 1 < outer:
                        onward, _, starts, _, _ = self.moves[number + 1, way, cut]
                        begin(onward, starts)
                    begin(across, lands)

        def paired(self, number, then=None):
            for way in (0, 1):
                lands, origin = self.moves[number, way, 0][3:]

                @pl.when(lands)
                def _():
                    for cut in range(cuts):
                        self.moves[number, way, cut][1].wait_recv()
                    if then is not None:
                        then(origin + 1 - col)

    loads = [
        pltpu.make_async_copy(source, target, load_sem.at[index])
        for index, (source, target) in enumerate(
            [
                (qkv_in, qkv_raw), (out_in, out_raw), (attn_in, attn_raw), (mlp_in, mlp_raw),
                (tok_in, tok_buf.at[me_t]), (cot_in, cot_buf.at[me_t]),
                (up_in, up_raw), (down_in, down_raw), (table_in, table),
            ]
        )
    ]
    for load in loads:
        load.start()
    barrier = pltpu.get_barrier_semaphore()
    for axis, me in (("dp", me_d), ("tensor", me_t)):
        for shift in range(1, sizes[axis]):
            pl.semaphore_signal(
                barrier,
                inc=1,
                device_id={axis: lax.rem(me + shift, sizes[axis])},
                device_id_type=pl.DeviceIdType.MESH,
            )
    eye_heads = jnp.where(
        lanes((heads_wide, heads_wide), 0) == lanes((heads_wide, heads_wide), 1), 1.0, 0.0
    ).astype(bf16)
    for load in loads[:4]:
        load.wait()
    gain_buf[me_d] = jnp.zeros(gain_buf.shape[1:], bf16)
    gain_buf[me_d, 0:1, :block] = attn_raw[...]
    gain_buf[me_d, 8:9, :block] = mlp_raw[...]
    for which in range(3):
        w_a[me_d, :, which * heads_wide : (which + 1) * heads_wide] = qkv_raw[which]
    out_turned = dot_f32(out_raw[...], eye_heads, 0, 0).astype(bf16)
    if side:
        w_a[me_d, :, 3 * heads_wide :] = out_turned[:, :side]
    w_c[me_d] = out_turned[:, side:]
    pl.semaphore_wait(barrier, groups + members - 2)

    def dp_spread(buffer):
        copies = []
        for shift in range(1, outer):
            peer = lax.rem(zrow + shift, outer) * 2 + col
            origin = lax.rem(zrow + outer - shift, outer) * 2 + col
            copies.append((send(buffer.at[me_d], buffer.at[me_d], "dp", peer), origin))
        return copies

    def dp_pair(buffer, origin):
        mirrored = origin // 2 * 2 + 1 - col
        return (send(buffer.at[origin], buffer.at[origin], "dp", x_peer), mirrored)

    def tensor_spread(buffer, span=slice(0, own_rows)):
        copies = []
        own = buffer.at[me_t, span]
        for shift in range(1, rings):
            peer = lax.rem(yrow + shift, rings) * 2 + core
            origin = lax.rem(yrow + rings - shift, rings) * 2 + core
            copies.append((send(own, own, "tensor", peer), origin))
        near = send(own, own, "tensor", c_peer)
        return copies, near

    def tensor_relay(buffer, copies, span=slice(0, own_rows)):
        onward = []
        for copy, origin in copies:
            copy.wait_recv()
            piece = buffer.at[origin, span]
            onward.append(send(piece, piece, "tensor", c_peer))
        return onward

    gain_z = dp_spread(gain_buf)
    gain_x = [dp_pair(gain_buf, me_d)]
    chain_a = Chain(w_a)
    chain_a.start()
    chain_a.start_pair()
    for load in loads[4:6]:
        load.wait()
    tok_y, tok_near = tensor_spread(tok_buf)
    cot_y, cot_near = tensor_spread(cot_buf)
    for load in loads[6:]:
        load.wait()
    eye_hidden = jnp.where(
        lanes((hidden, hidden), 0) == lanes((hidden, hidden), 1), 1.0, 0.0
    ).astype(bf16)
    for which in range(2):
        w_b[me_d, :, which * hidden : (which + 1) * hidden] = up_raw[which]
    w_b[me_d, :, 2 * hidden : 3 * hidden] = dot_f32(down_raw[...], eye_hidden, 0, 0).astype(bf16)
    if pad_hidden > 3 * hidden:
        w_b[me_d, :, 3 * hidden :] = jnp.zeros((block, pad_hidden - 3 * hidden), bf16)
    chain_b = Chain(w_b)

    turn = spread_matrix(head_count, True, 1.0)
    plain = spread_matrix(head_count, False, 1.0)

    def expand(index):
        for which, matrix in ((0, turn), (1, turn), (2, plain)):
            piece = w_a[index, :, which * heads_wide : (which + 1) * heads_wide]
            w_big[index, :, which * spread : (which + 1) * spread] = dot_f32(
                piece, matrix, 1, 0
            ).astype(bf16)

    def expand_out():
        value = dot_f32(
            w_c[...].reshape(width, heads_wide - side), plain[side:], 1, 0
        )
        if side:
            head_piece = w_a[:, :, 3 * heads_wide :].reshape(width, side)
            value = value + dot_f32(head_piece, plain[:side], 1, 0)
        w_out_pad[...] = value.astype(bf16).reshape(groups, block, spread)

    expand(me_d)
    chain_a.step(1)
    for copy, origin in gain_z:
        copy.wait_recv()
        gain_x.append(dp_pair(gain_buf, origin))
    tok_far = tensor_relay(tok_buf, tok_y)
    for number in range(2, outer - 1):
        chain_a.step(number)
    c_z = dp_spread(w_c)
    chain_b.start()
    for copy, _ in gain_x:
        copy.wait_recv()
    for index in range(groups):
        tile = gain_buf[index].astype(f32)
        gain_rows[0:1, index * block : (index + 1) * block] = tile[0:1, :block]
        gain_rows[8:9, index * block : (index + 1) * block] = tile[8:9, :block]
    attn_gain, mlp_gain = gain_rows[0:1, :], gain_rows[8:9, :]
    tok_near.wait_recv()
    for copy in tok_far:
        copy.wait_recv()
    all_rows = tok_buf[...].reshape(row_count, width).astype(f32)
    rows_one[...] = (normalize(all_rows)[0] * attn_gain).astype(bf16)
    if outer > 2:
        chain_a.step(outer - 1)
    c_x = [dp_pair(w_c, me_d)]
    cot_far = tensor_relay(cot_buf, cot_y)
    for shift in range(1, outer):
        expand(lax.rem(zrow + shift, outer) * 2 + col)
    for copy, origin in c_z:
        copy.wait_recv()
        c_x.append(dp_pair(w_c, origin))
    chain_b.start_pair()
    for copy in chain_a.own:
        copy.wait_recv()
    expand(x_peer)
    chain_b.step(1)
    for number in range(1, outer):
        chain_a.paired(number, expand)

    paired = paired_matrix()
    rotary = table[...]
    for which in range(3):
        weight = w_big[:, :, which * spread : (which + 1) * spread].reshape(width, spread)
        projected = dot_f32(rows_one[...], weight, 1, 0)
        for head in range(head_count):
            piece = projected[:, head * 128 : (head + 1) * 128]
            if which == 2:
                v_buf[head] = piece.astype(bf16)
                continue
            turned = piece * rotary
            turned = (turned + pltpu.roll(turned, 64, 1)).astype(bf16)
            (q_buf, k_buf)[which][head] = turned
    for head in range(head_count):
        scores = dot_f32(k_buf[head], q_buf[head], 1, 1) * (0.5 * HD ** (-0.5))
        peak = jnp.max(scores, axis=0, keepdims=True)
        powers = jnp.exp(scores - peak)
        share = powers * (1.0 / jnp.sum(powers, axis=0, keepdims=True))
        probs[head] = share
        mixed_t = dot_f32(v_buf[head], share.astype(bf16), 0, 0).astype(bf16)
        mix_t[head] = mixed_t
        mixed = jnp.transpose(mixed_t.astype(f32)).astype(bf16)
        mix[:, :, head * 128 : (head + 1) * 128] = mixed.reshape(members, own_rows, 128)
        mix_pack[:, head * HD : (head + 1) * HD] = mixed[:, :HD]

    every = slice(0, own_rows)
    if own_rows % 32 == 0:
        spans = (slice(0, own_rows // 2), slice(own_rows // 2, own_rows))
    else:
        spans = (every,)

    def reduce_far(part, recv, span=every):
        first = []
        for shift in range(1, rings):
            far = lax.rem(yrow + shift, rings)
            first.append(
                send(part.at[far * 2 + 1 - core, span], recv.at[shift, span], "tensor", c_peer)
            )
        return first

    def reduce_near(part, recv, span=every):
        return send(part.at[c_peer, span], recv.at[0, span], "tensor", c_peer)

    def reduce_middle(part, recv, fwd, first, span=every):
        second = []
        for shift in range(1, rings):
            far = lax.rem(yrow + shift, rings)
            first[shift - 1].wait_recv()
            fwd[shift, span] = (
                part[far * 2 + core, span].astype(f32) + recv[shift, span].astype(f32)
            ).astype(bf16)
            second.append(
                send(
                    fwd.at[shift, span],
                    recv.at[rings + shift, span],
                    "tensor",
                    far * 2 + core,
                )
            )
        return second

    def reduce_finish(part, recv, near, second, span=every):
        near.wait_recv()
        total = part[me_t, span].astype(f32) + recv[0, span].astype(f32)
        for shift in range(1, rings):
            second[shift - 1].wait_recv()
            total = total + recv[rings + shift, span].astype(f32)
        return total

    def project(part, ring, left, right):
        part[pl.ds(2 * ring, 2)] = (
            dot_f32(left, right, 1, 1).astype(bf16).reshape(2, own_rows, width)
        )

    for copy, _ in c_x:
        copy.wait_recv()
    expand_out()
    out_weight = w_out_pad[...].reshape(width, spread)

    def mixed_ring(ring):
        return mix[pl.ds(2 * ring, 2)].reshape(2 * own_rows, spread)

    for shift in range(1, rings):
        far = lax.rem(yrow + shift, rings)
        project(part_one, far, mixed_ring(far), out_weight)
    first_one = [reduce_far(part_one, recv_one, span) for span in spans]
    project(part_one, yrow, mixed_ring(yrow), out_weight)
    near_one = [reduce_near(part_one, recv_one, span) for span in spans]
    second_one = [
        reduce_middle(part_one, recv_one, fwd_one, first, span)
        for first, span in zip(first_one, spans)
    ]
    for number in range(2, outer - 1):
        chain_b.step(number)
    for head in range(head_count):
        q_buf[head] = dot_f32(q_buf[head], paired, 1, 0).astype(bf16)
        k_buf[head] = dot_f32(k_buf[head], paired, 1, 0).astype(bf16)
    if outer > 2:
        chain_b.step(outer - 1)
    rows_y, rows_near = [], []
    for index, span in enumerate(spans):
        residual = tok_buf[me_t, span].astype(f32)
        hidden_res[span] = residual + reduce_finish(
            part_one, recv_one, near_one[index], second_one[index], span
        )
        normed_two = normalize(hidden_res[span])[0]
        rows_two[me_t, span] = (normed_two * mlp_gain).astype(bf16)
        far_copies, near_copy = tensor_spread(rows_two, span)
        rows_y.append(far_copies)
        rows_near.append(near_copy)
    cot_near.wait_recv()
    for copy in cot_far:
        copy.wait_recv()
    for copy in chain_b.own:
        copy.wait_recv()
    for number in range(1, outer):
        chain_b.paired(number)
    up_w[...] = w_b[:, :, :hidden].reshape(width, hidden)
    gate_w[...] = w_b[:, :, hidden : 2 * hidden].reshape(width, hidden)
    down_w[...] = w_b[:, :, 2 * hidden : 3 * hidden].reshape(width, hidden)

    def feed(ring):
        base = 2 * ring
        count = 2 * own_rows
        rows = rows_two[pl.ds(base, 2)].reshape(count, width)
        cot = cot_buf[pl.ds(base, 2)].reshape(count, width)
        inputs = dot_f32(rows, up_w[...], 1, 0)
        gate_part = dot_f32(rows, gate_w[...], 1, 0)
        grad_act = dot_f32(cot, down_w[...], 1, 0)
        activated, slope = gelu_pair(inputs)
        act_buf[ring] = (activated * gate_part).astype(bf16)
        grad_up = (grad_act * gate_part * slope).astype(bf16)
        grad_gate = (grad_act * activated).astype(bf16)
        up_grad[ring] = grad_up
        gate_grad[ring] = grad_gate
        part_two[pl.ds(base, 2)] = (
            (dot_f32(grad_up, up_w[...], 1, 1) + dot_f32(grad_gate, gate_w[...], 1, 1))
            .astype(bf16)
            .reshape(2, own_rows, width)
        )

    for copy in rows_near:
        copy.wait_recv()
    feed(yrow)
    rows_far = []
    for copies, span in zip(rows_y, spans):
        rows_far += tensor_relay(rows_two, copies, span)
    for copy in rows_far:
        copy.wait_recv()
    for shift in range(1, rings):
        feed(lax.rem(yrow + shift, rings))
    first_two = reduce_far(part_two, recv_two)
    near_two = reduce_near(part_two, recv_two)

    staged = outer == 4
    beside = zrow // 2 * 2 + 1 - lax.rem(zrow, 2)
    if staged:
        across_z = lax.rem(zrow + 2, outer)
        targets = [lax.rem(beside + 2, outer), across_z, beside, zrow]
    else:
        targets = [lax.rem(zrow + shift, outer) for shift in range(1, outer + 1)]

    def pair_start(grads, half):
        return [
            (send(grads.at[row * 2 + 1 - col], half.at[row], "dp", x_peer), row)
            for row in targets
        ]

    def pair_step(state, number):
        grads, half, sums, parts, copies, moved = state
        copy, row = copies[number]
        copy.wait_recv()
        value = grads[row * 2 + col].astype(f32) + half[row].astype(f32)
        if number == outer - 1:
            for copy in moved[1:] if staged else moved:
                copy.wait_recv()
            if not staged:
                parts[zrow] = jnp.zeros(parts.shape[1:], bf16)
            arrived = parts[1 : outer - 1] if staged else parts[...]
            return value + jnp.sum(arrived.astype(f32), axis=0)
        if not staged:
            sums[row] = value.astype(bf16)
            moved.append(send(sums.at[row], parts.at[zrow], "dp", row * 2 + col))
            return None
        if number == 1:
            moved[0].wait_recv()
            value = value + parts[0].astype(f32)
        sums[number] = value.astype(bf16)
        target, place = ((beside, 0), (across_z, 1), (beside, 2))[number]
        moved.append(send(sums.at[number], parts.at[place], "dp", target * 2 + col))
        return None

    full_rows = rows_two[...].reshape(row_count, width)
    full_cot = cot_buf[...].reshape(row_count, width)
    for which, grad in ((0, up_grad), (1, gate_grad)):
        mlp_grads[:, :, which * hidden : (which + 1) * hidden] = (
            dot_f32(full_rows, grad[...].reshape(row_count, hidden), 0, 0)
            .astype(bf16)
            .reshape(groups, block, hidden)
        )
    full_act = act_buf[...].reshape(row_count, hidden)
    mlp_grads[:, :, 2 * hidden : 3 * hidden] = (
        dot_f32(full_cot, full_act, 0, 0).astype(bf16).reshape(groups, block, hidden)
    )
    if pad_hidden > 3 * hidden:
        mlp_grads[:, :, 3 * hidden :] = jnp.zeros(
            (groups, block, pad_hidden - 3 * hidden), bf16
        )
    mlp_pairs = pair_start(mlp_grads, mlp_half)
    second_two = reduce_middle(part_two, recv_two, fwd_two, first_two)
    part_three[...] = (
        dot_f32(full_act, down_w[...], 1, 1).astype(bf16).reshape(members, own_rows, width)
    )
    normed_two, inv_two = normalize(hidden_res[...])
    mlp_state = (mlp_grads, mlp_half, mlp_sum, mlp_parts, mlp_pairs, [])
    pair_step(mlp_state, 0)
    back_two = reduce_finish(part_two, recv_two, near_two, second_two)
    grad_res, mlp_gain_part = normalize_back(back_two, normed_two, inv_two, mlp_gain)
    grad_hidden[...] = cot_buf[me_t].astype(f32) + grad_res
    grad_rows[me_t] = grad_hidden[...].astype(bf16)
    grad_y, grad_near = tensor_spread(grad_rows)
    first_three = reduce_far(part_three, recv_three)
    near_three = reduce_near(part_three, recv_three)
    for number in range(1, min(2, outer - 1)):
        pair_step(mlp_state, number)
    grad_far = tensor_relay(grad_rows, grad_y)
    second_three = reduce_middle(part_three, recv_three, fwd_three, first_three)
    grad_near.wait_recv()
    for copy in grad_far:
        copy.wait_recv()
    full_grad = grad_rows[...].reshape(row_count, width)
    grad_mix = dot_f32(full_grad, out_weight, 1, 0).astype(bf16)
    out_product = dot_f32(full_grad, mix_pack[...], 0, 0).astype(bf16)
    if side:
        vo_grads[:, :, heads_wide:] = out_product[:, :side].reshape(groups, block, side)
    out_grads[...] = out_product[:, side:].reshape(groups, block, heads_wide - side)
    out_pairs = pair_start(out_grads, out_half)
    for number in range(2, outer - 1):
        pair_step(mlp_state, number)
    scale = HD ** (-0.5)
    for head in range(head_count):
        grad_head = grad_mix[:, head * 128 : (head + 1) * 128]
        grad_head_t = jnp.transpose(grad_head.astype(f32))
        delta = jnp.sum(grad_head_t * mix_t[head].astype(f32), axis=0, keepdims=True)
        grad_probs = dot_f32(v_buf[head], grad_head, 1, 1)
        share = probs[head]
        grad_scores = (share * (grad_probs - delta)).astype(bf16)
        grad_v = dot_f32(share.astype(bf16), grad_head, 1, 0)
        grad_k = dot_f32(grad_scores, q_buf[head], 1, 0) * (rotary * scale)
        grad_k = grad_k + pltpu.roll(grad_k, 64, 1)
        grad_q = jnp.transpose(dot_f32(k_buf[head], grad_scores, 0, 0)) * (rotary * scale)
        grad_q = grad_q + pltpu.roll(grad_q, 64, 1)
        for which, value in enumerate((grad_q, grad_k, grad_v)):
            start = which * heads_wide + head * HD
            proj_grad[:, start : start + HD] = value[:, :HD].astype(bf16)
    qk_grads[...] = (
        dot_f32(rows_one[...], proj_grad[:, : 2 * heads_wide], 0, 0)
        .astype(bf16)
        .reshape(groups, block, 2 * heads_wide)
    )
    qk_pairs = pair_start(qk_grads, qk_half)
    vo_grads[:, :, :heads_wide] = (
        dot_f32(rows_one[...], proj_grad[:, 2 * heads_wide :], 0, 0)
        .astype(bf16)
        .reshape(groups, block, heads_wide)
    )
    vo_pairs = pair_start(vo_grads, vo_half)
    qkv_weight = w_a[:, :, : 3 * heads_wide].reshape(width, 3 * heads_wide)

    def grad_ring(ring):
        return proj_grad[pl.ds(pl.multiple_of(ring * 2 * own_rows, 2 * own_rows), 2 * own_rows)]

    for shift in range(1, rings):
        far = lax.rem(yrow + shift, rings)
        project(part_four, far, grad_ring(far), qkv_weight)
    first_four = reduce_far(part_four, recv_four)
    project(part_four, yrow, grad_ring(yrow), qkv_weight)
    near_four = reduce_near(part_four, recv_four)
    second_four = reduce_middle(part_four, recv_four, fwd_four, first_four)

    def total(parts, across):
        for copy in across:
            copy.wait_recv()
        return jnp.sum(parts[...].astype(f32), axis=0)

    mlp_out = reduce_finish(part_three, recv_three, near_three, second_three)
    output_ref[...] = (hidden_res[...] + mlp_out).astype(bf16)
    out_state = (out_grads, out_half, out_sum, out_parts, out_pairs, [])
    for number in range(outer - 1):
        pair_step(out_state, number)
    mlp_grad_ref[...] = pair_step(mlp_state, outer - 1)
    qk_state = (qk_grads, qk_half, qk_sum, qk_parts, qk_pairs, [])
    vo_state = (vo_grads, vo_half, vo_sum, vo_parts, vo_pairs, [])
    pair_step(qk_state, 0)
    residual = tok_buf[me_t].astype(f32)
    normed_one, inv_one = normalize(residual)
    back_one = reduce_finish(part_four, recv_four, near_four, second_four)
    grad_res, attn_gain_part = normalize_back(back_one, normed_one, inv_one, attn_gain)
    input_grad_ref[...] = grad_hidden[...] + grad_res
    gain_send[...] = jnp.zeros(gain_send.shape, f32)
    attn_row = attn_gain_part.reshape(1, width)
    mlp_row = mlp_gain_part.reshape(1, width)
    for index in range(groups):
        gain_send[index, 0:1, :block] = attn_row[:, index * block : (index + 1) * block]
        gain_send[index, 1:2, :block] = mlp_row[:, index * block : (index + 1) * block]
    gain_recv[me_d] = gain_send[me_d]
    gain_copies = []
    for shift in range(1, groups):
        peer = lax.rem(me_d + shift, groups)
        gain_copies.append(send(gain_send.at[peer], gain_recv.at[me_d], "dp", peer))
    for number in range(1, outer - 1):
        pair_step(qk_state, number)
    pair_step(vo_state, 0)
    gain_group[me_t] = total(gain_recv, gain_copies)
    gain_copies = []
    for shift in range(1, members):
        peer = lax.rem(me_t + shift, members)
        gain_copies.append(send(gain_group.at[me_t], gain_group.at[me_t], "tensor", peer))
    for number in range(1, outer - 1):
        pair_step(vo_state, number)
    out_grad_ref[...] = pair_step(out_state, outer - 1)
    qkv_grad_ref[:, : 2 * heads_wide] = pair_step(qk_state, outer - 1)
    qkv_grad_ref[:, 2 * heads_wide :] = pair_step(vo_state, outer - 1)
    gain_ref[...] = total(gain_group, gain_copies)
    for copy, condition in sent:
        if condition is None:
            copy.wait_send()
        else:
            pl.when(condition)(copy.wait_send)


def rotary_table(row_count):
    position = (np.arange(row_count) % L).astype(np.float32)
    halves = np.arange(HD // 2).astype(np.float32)
    inverse = np.float32(ROPE_THETA) ** (np.float32(-2.0) * halves / np.float32(HD))
    angles = position[:, None] * inverse[None, :]
    return np.concatenate([np.cos(angles)] * 2 + [np.sin(angles)] * 2, axis=1).astype(np.float32)


def whole_layer(sizes, tokens, attn_gain, w_qkv, w_out, mlp_gain, w_in, w_down, cotangent):
    bf16, f32 = jnp.bfloat16, jnp.float32
    groups, members = sizes["dp"], sizes["tensor"]
    own_rows, width = tokens.shape
    block, heads_wide, hidden = w_qkv.shape[1], w_qkv.shape[2], w_in.shape[2]
    pad_hidden = -(-3 * hidden // 128) * 128
    row_count = own_rows * members
    head_count, spread = heads_wide // HD, 2 * heads_wide
    side = -3 * heads_wide % 128
    outer, rings = groups // 2, members // 2
    vmem = pltpu.VMEM
    parts = vmem((members, own_rows, width), bf16)
    arrived = vmem((2 * rings, own_rows, width), bf16)
    passed = vmem((rings, own_rows, width), bf16)
    heads = vmem((head_count, row_count, 128), bf16)
    ringed = vmem((rings, 2 * own_rows, hidden), bf16)

    def exchanged(wide):
        quarter = vmem((outer, block, wide), bf16)
        return [vmem((groups, block, wide), bf16), quarter, quarter, quarter]

    scratch = [
        parts, parts,
        vmem(w_qkv.shape, bf16), vmem(w_out.shape, bf16),
        vmem(w_in.shape, bf16), vmem(w_down.shape, bf16),
        vmem((1, block), bf16), vmem((1, block), bf16), vmem((row_count, 2 * HD), f32),
        vmem((groups, block, 3 * heads_wide + side), bf16),
        vmem((groups, block, pad_hidden), bf16),
        vmem((groups, block, heads_wide - side), bf16),
        vmem((groups, 16, 128), bf16),
        vmem((16, width), f32),
        vmem((groups, block, 3 * spread), bf16),
        vmem((groups, block, spread), bf16),
        vmem((width, hidden), bf16), vmem((width, hidden), bf16), vmem((width, hidden), bf16),
        vmem((row_count, width), bf16),
        vmem((head_count, row_count, row_count), f32),
        heads, heads, heads,
        vmem((head_count, 128, row_count), bf16),
        vmem((members, own_rows, spread), bf16),
        vmem((row_count, heads_wide), bf16),
        parts, arrived, passed,
        vmem((own_rows, width), f32),
        parts,
        ringed, ringed, ringed,
        parts, arrived, passed,
        parts, arrived, passed,
        *exchanged(pad_hidden),
        vmem((own_rows, width), f32),
        parts,
        *exchanged(heads_wide - side),
        vmem((row_count, 3 * heads_wide), bf16),
        *exchanged(2 * heads_wide),
        *exchanged(heads_wide + side),
        parts, arrived, passed,
        vmem((groups, 8, 128), f32), vmem((groups, 8, 128), f32), vmem((members, 8, 128), f32),
    ]
    cuts = 2 if block % 32 == 0 else 1
    chains = 2 * cuts * (4 * (outer - 1) + 1)
    halves = 2 if own_rows % 32 == 0 else 1
    gathers = 2 * (2 * outer - 1) + chains + (3 + halves) * (2 * rings - 1)
    reduces = (3 + halves) * (2 * rings - 1) + 4 * (2 * outer - 1)
    slots = gathers + reduces + groups + members - 2
    dims = (own_rows, width, block, heads_wide, hidden, pad_hidden)
    output, input_grad, gains, qkv_sum, out_sum, mlp_sums = pl.pallas_call(
        functools.partial(layer_kernel, sizes, dims),
        out_shape=[
            jax.ShapeDtypeStruct((own_rows, width), bf16),
            jax.ShapeDtypeStruct((own_rows, width), f32),
            jax.ShapeDtypeStruct((8, 128), f32),
            jax.ShapeDtypeStruct((block, 3 * heads_wide + side), f32),
            jax.ShapeDtypeStruct((block, heads_wide - side), f32),
            jax.ShapeDtypeStruct((block, pad_hidden), f32),
        ],
        in_specs=[pl.BlockSpec(memory_space=pltpu.HBM)] * 9,
        out_specs=[pl.BlockSpec(memory_space=pltpu.VMEM)] * 6,
        scratch_shapes=scratch
        + [
            pltpu.SemaphoreType.DMA((9,)),
            pltpu.SemaphoreType.DMA((slots,)),
            pltpu.SemaphoreType.DMA((slots,)),
        ],
        compiler_params=pltpu.CompilerParams(
            collective_id=0, has_side_effects=True, vmem_limit_bytes=44 << 20
        ),
    )(
        *[
            pltpu.with_memory_space_constraint(array, pltpu.HBM)
            for array in (
                tokens, cotangent, w_qkv, w_out, w_in, w_down,
                attn_gain.reshape(1, block), mlp_gain.reshape(1, block),
                jnp.asarray(rotary_table(row_count)),
            )
        ]
    )
    results = pl.pallas_call(
        functools.partial(finish_kernel, hidden),
        out_shape=[
            jax.ShapeDtypeStruct(output.shape, bf16),
            jax.ShapeDtypeStruct(input_grad.shape, f32),
            jax.ShapeDtypeStruct(w_qkv.shape, f32),
            jax.ShapeDtypeStruct(w_out.shape, f32),
            jax.ShapeDtypeStruct(w_in.shape, f32),
            jax.ShapeDtypeStruct(w_down.shape, f32),
            jax.ShapeDtypeStruct((1, block), f32),
            jax.ShapeDtypeStruct((1, block), f32),
        ],
        in_specs=[pl.BlockSpec(memory_space=pltpu.VMEM)] * 6,
        out_specs=[pl.BlockSpec(memory_space=pltpu.HBM)] * 8,
        scratch_shapes=[
            vmem(w_qkv.shape, f32),
            vmem(w_out.shape, f32),
            vmem(w_in.shape, f32),
            vmem(w_down.shape, f32),
            vmem((1, block), f32),
            vmem((1, block), f32),
            pltpu.SemaphoreType.DMA((8,)),
        ],
        compiler_params=pltpu.CompilerParams(vmem_limit_bytes=16 << 20),
    )(output, input_grad, qkv_sum, out_sum, mlp_sums, gains)
    output, input_grad, grad_w_qkv, grad_w_out, grad_w_in, grad_w_down = results[:6]
    return (
        output,
        input_grad,
        results[6].reshape(block),
        grad_w_qkv,
        grad_w_out,
        results[7].reshape(block),
        grad_w_in,
        grad_w_down,
    )


def finish_kernel(hidden, *refs):
    (
        output, input_grad, qkv_sum, out_sum, mlp_sums, gains,
        output_to, input_grad_to, qkv_to, out_to, up_to, down_to, attn_to, mlp_to,
        qkv_buf, out_buf, up_buf, down_buf, attn_buf, mlp_buf, sems,
    ) = refs
    started = []

    def put(source, target):
        copy = pltpu.make_async_copy(source, target, sems.at[len(started)])
        copy.start()
        started.append(copy)

    put(output, output_to)
    put(input_grad, input_grad_to)
    attn_buf[...] = gains[0:1, : attn_buf.shape[1]]
    put(attn_buf, attn_to)
    mlp_buf[...] = gains[1:2, : mlp_buf.shape[1]]
    put(mlp_buf, mlp_to)
    heads_wide = out_buf.shape[0]
    side = heads_wide - out_sum.shape[1]
    for which in range(3):
        qkv_buf[which] = qkv_sum[:, which * heads_wide : (which + 1) * heads_wide]
    put(qkv_buf, qkv_to)
    for which in range(2):
        up_buf[which] = mlp_sums[:, which * hidden : (which + 1) * hidden]
    put(up_buf, up_to)
    if side:
        out_buf[:side] = jnp.transpose(qkv_sum[:, 3 * heads_wide :])
    out_buf[side:] = jnp.transpose(out_sum[...])
    put(out_buf, out_to)
    down_buf[...] = jnp.transpose(mlp_sums[:, 2 * hidden : 3 * hidden])
    put(down_buf, down_to)
    for copy in started:
        copy.wait()


def fits_whole(sizes, tokens, w_qkv):
    row_count = tokens.shape[0] * sizes["tensor"]
    even = sizes["dp"] % 2 == 0 and sizes["tensor"] % 2 == 0
    tiled = w_qkv.shape[1] % 16 == 0 and tokens.shape[0] % 16 == 0
    narrow = -3 * w_qkv.shape[2] % 128 < w_qkv.shape[2] and w_qkv.shape[1] <= 128
    return even and tiled and row_count == L and narrow


def layer(sizes, tokens, attn_gain, w_qkv, *rest):
    run = whole_layer if fits_whole(sizes, tokens, w_qkv) else body
    return run(sizes, tokens, attn_gain, w_qkv, *rest)


def solution(mesh):
    in_specs = (
        P(("dp", "tensor"), None),
        P("dp"),
        P(None, "dp", "tensor"),
        P("tensor", "dp"),
        P("dp"),
        P(None, "dp", "tensor"),
        P("tensor", "dp"),
        P(("dp", "tensor"), None),
    )
    out_specs = (
        P(("dp", "tensor"), None),
        P(("dp", "tensor"), None),
        P("dp"),
        P(None, "dp", "tensor"),
        P("tensor", "dp"),
        P("dp"),
        P(None, "dp", "tensor"),
        P("tensor", "dp"),
    )
    sizes = {axis: mesh.shape[axis] for axis in ("dp", "tensor")}
    return jax.shard_map(functools.partial(layer, sizes), mesh=mesh, in_specs=in_specs, out_specs=out_specs, check_vma=False)
```

```python
import functools

import jax
import jax.numpy as jnp
import numpy as np
from jax import lax
from jax.experimental import pallas as pl
from jax.experimental.pallas import tpu as pltpu
from jax.experimental.layout import Layout, with_layout_constraint
from jax.sharding import PartitionSpec as P

HD = 64
L = 512


NORM_EPS = 1e-05
ROPE_THETA = 160000.0
SQRT_HALF = 0.7071067811865476
GAUSS_NORM = 0.3989422804014327


def rope_tables(row_count):
    position = (jnp.arange(row_count) % L).astype(jnp.float32)
    halves = jnp.arange(HD // 2).astype(jnp.float32)
    inverse = ROPE_THETA ** (-2.0 * halves / HD)
    angles = position[:, None] * inverse[None, :]
    angles = jnp.concatenate([angles, angles], axis=1)
    return (jnp.cos(angles)[:, None, :], jnp.sin(angles)[:, None, :])


def rotate(field_rows, cos_table, sin_table):
    first_half = field_rows[..., : HD // 2]
    second_half = field_rows[..., HD // 2 :]
    turned = jnp.concatenate([-second_half, first_half], axis=-1)
    return field_rows * cos_table + turned * sin_table


def rotate_back(grad_field, cos_table, sin_table):
    scaled = grad_field * sin_table
    turned = jnp.concatenate([scaled[..., HD // 2 :], -scaled[..., : HD // 2]], axis=-1)
    return grad_field * cos_table + turned


def normalize(values):
    centred = values - jnp.mean(values, axis=-1, keepdims=True)
    inv_std = lax.rsqrt(jnp.mean(centred * centred, axis=-1, keepdims=True) + NORM_EPS)
    return (centred * inv_std, inv_std)


def normalize_back(grad_norm, normed, inv_std, gain_row):
    gain_part = jnp.sum(grad_norm * normed, axis=0)
    scaled = grad_norm * gain_row
    centred = scaled - jnp.mean(scaled, axis=-1, keepdims=True)
    grad_in = inv_std * (centred - normed * jnp.mean(scaled * normed, axis=-1, keepdims=True))
    return (grad_in, gain_part)


def gelu_pair(inputs):
    normal_cdf = 0.5 * (1.0 + lax.erf(inputs * SQRT_HALF))
    return (inputs * normal_cdf, normal_cdf + inputs * jnp.exp(-0.5 * inputs * inputs) * GAUSS_NORM)


def attend(queries, key_rows, value_rows):
    score_scale = HD ** (-0.5)
    scores = (
        jnp.einsum("qhd,khd->hqk", queries, key_rows, preferred_element_type=jnp.float32)
        * score_scale
    )
    row_max = jnp.max(scores, axis=-1, keepdims=True)
    log_total = row_max + jnp.log(jnp.sum(jnp.exp(scores - row_max), axis=-1, keepdims=True))
    weights = jnp.exp(scores - log_total).astype(jnp.bfloat16)
    attn_mix = jnp.einsum(
        "hqk,khd->qhd", weights, value_rows, preferred_element_type=jnp.float32
    ).astype(jnp.bfloat16)
    return (attn_mix, log_total)


def attend_back(queries, key_rows, value_rows, attn_mix, grad_mix, log_total):
    score_scale = HD ** (-0.5)
    scores = (
        jnp.einsum("qhd,khd->hqk", queries, key_rows, preferred_element_type=jnp.float32)
        * score_scale
    )
    probabilities = jnp.exp(scores - log_total)
    grad_probs = jnp.einsum(
        "qhd,khd->hqk", grad_mix, value_rows, preferred_element_type=jnp.float32
    )
    row_delta = jnp.sum(grad_mix.astype(jnp.float32) * attn_mix.astype(jnp.float32), axis=-1)
    grad_scores = (probabilities * (grad_probs - jnp.transpose(row_delta)[:, :, None])).astype(
        jnp.bfloat16
    )
    prob_rounded = probabilities.astype(jnp.bfloat16)
    grad_values = jnp.einsum(
        "hqk,qhd->khd", prob_rounded, grad_mix, preferred_element_type=jnp.float32
    )
    grad_queries = (
        jnp.einsum("hqk,khd->qhd", grad_scores, key_rows, preferred_element_type=jnp.float32)
        * score_scale
    )
    grad_keys = (
        jnp.einsum("hqk,qhd->khd", grad_scores, queries, preferred_element_type=jnp.float32)
        * score_scale
    )
    return (grad_queries, grad_keys, grad_values)


def exchange_kernel(plan, sizes, *refs):
    count = len(plan)
    sources, targets = refs[:count], refs[count : 2 * count]
    own_sem, send_sem, recv_sem = refs[2 * count :]
    axes = sorted({axis for _, axis, _ in plan})
    barrier = pltpu.get_barrier_semaphore()
    total = 0
    for axis in axes:
        me = lax.axis_index(axis)
        for shift in range(1, sizes[axis]):
            pl.semaphore_signal(
                barrier,
                inc=1,
                device_id={axis: lax.rem(me + shift, sizes[axis])},
                device_id_type=pl.DeviceIdType.MESH,
            )
            total += 1
    pl.semaphore_wait(barrier, total)
    slot = 0
    pending, relays, local = [], [], []

    def remote(source, target, axis, peer, index):
        return pltpu.make_async_remote_copy(
            src_ref=source,
            dst_ref=target,
            send_sem=send_sem.at[index],
            recv_sem=recv_sem.at[index],
            device_id={axis: peer},
            device_id_type=pl.DeviceIdType.MESH,
        )

    for which, (kind, axis, span) in enumerate(plan):
        size = sizes[axis]
        me = lax.axis_index(axis)
        source, target = sources[which], targets[which]
        outer = size // 2
        column = lax.rem(me, 2)
        row = me // 2
        partner = row * 2 + 1 - column
        if kind == "half":
            copy = remote(source.at[:, 1 - column, :, span], target, axis, partner, slot)
            copy.start()
            pending.append(copy)
            slot += 1
            continue
        if kind == "outer":
            for shift in range(1, outer):
                other = lax.rem(row + shift, outer)
                copy = remote(source.at[other], target.at[row], axis, other * 2 + column, slot)
                copy.start()
                pending.append(copy)
                slot += 1
            copy = pltpu.make_async_copy(source.at[row], target.at[row], own_sem.at[which])
            copy.start()
            local.append(copy)
            continue
        if kind == "relay":
            for shift in range(1, outer):
                peer = lax.rem(row + shift, outer) * 2 + column
                copy = remote(source, target.at[me], axis, peer, slot)
                copy.start()
                origin = lax.rem(row + outer - shift, outer) * 2 + column
                relays.append((copy, target, axis, origin, partner, slot + 1))
                slot += 2
            copy = remote(source, target.at[me], axis, partner, slot)
            copy.start()
            pending.append(copy)
            slot += 1
        else:
            for shift in range(1, size):
                peer = lax.rem(me + shift, size)
                piece = source if kind == "gather" else source.at[peer, :, span]
                copy = remote(piece, target.at[me], axis, peer, slot)
                copy.start()
                pending.append(copy)
                slot += 1
        piece = source if kind != "scatter" else source.at[me, :, span]
        copy = pltpu.make_async_copy(piece, target.at[me], own_sem.at[which])
        copy.start()
        local.append(copy)
    for copy, target, axis, origin, partner, index in relays:
        copy.wait_recv()
        onward = remote(target.at[origin], target.at[origin], axis, partner, index)
        onward.start()
        pending.append(onward)
    for copy, *_ in relays:
        copy.wait_send()
    for copy in pending + local:
        copy.wait()


def slots_of(kind, size):
    outer = size // 2
    return {"relay": 2 * outer - 1, "half": 1, "outer": outer - 1}.get(kind, size - 1)


def shape_of(kind, size, shape, wide):
    if kind == "half":
        return (shape[0], shape[2], wide)
    return {"scatter": shape[:-1] + (wide,), "outer": shape}.get(kind, (size,) + shape)


def exchange(sizes, number, *ops):
    arrays = [op[2] for op in ops]
    spans = [slice(*op[3]) if len(op) > 3 else slice(0, op[2].shape[-1]) for op in ops]
    plan = tuple((op[0], op[1], span) for op, span in zip(ops, spans))
    shapes = [
        jax.ShapeDtypeStruct(
            shape_of(kind, sizes[axis], array.shape, span.stop - span.start), array.dtype
        )
        for (kind, axis, span), array in zip(plan, arrays)
    ]
    slots = sum(slots_of(kind, sizes[axis]) for kind, axis, _ in plan)
    return pl.pallas_call(
        functools.partial(exchange_kernel, plan, sizes),
        out_shape=shapes,
        in_specs=[pl.BlockSpec(memory_space=pltpu.VMEM)] * len(arrays),
        out_specs=[pl.BlockSpec(memory_space=pltpu.VMEM)] * len(arrays),
        scratch_shapes=[
            pltpu.SemaphoreType.DMA((len(arrays),)),
            pltpu.SemaphoreType.DMA((slots,)),
            pltpu.SemaphoreType.DMA((slots,)),
        ],
        compiler_params=pltpu.CompilerParams(
            collective_id=number, has_side_effects=True, vmem_limit_bytes=48 << 20
        ),
    )(*arrays)


def pad_columns(array, multiple=128):
    extra = -array.shape[-1] % multiple
    return jnp.pad(array, [(0, 0)] * (array.ndim - 1) + [(0, extra)])


def total_of(pieces):
    return jnp.sum(pieces.astype(jnp.float32), axis=0)


def row_major(array):
    return with_layout_constraint(array, Layout(major_to_minor=(0, 1)))


def dot_f32(left, right, left_dim, right_dim):
    return lax.dot_general(
        left, right, (((left_dim,), (right_dim,)), ((), ())), preferred_element_type=jnp.float32
    )


def feed_forward_kernel(
    hidden, rows_ref, up_ref, gate_ref, down_ref, cot_ref, mlp_ref, back_ref, grads_ref
):
    bf16 = jnp.bfloat16
    rows, cot = rows_ref[...], cot_ref[...]
    inputs = dot_f32(rows, up_ref[...], 1, 0)
    gate_part = dot_f32(rows, gate_ref[...], 1, 0)
    activated, gelu_slope = gelu_pair(inputs)
    hidden_act = (activated * gate_part).astype(bf16)
    mlp_ref[...] = dot_f32(hidden_act, down_ref[...], 1, 1).astype(bf16)
    grad_act = dot_f32(cot, down_ref[...], 1, 0)
    grad_up = (grad_act * gate_part * gelu_slope).astype(bf16)
    grad_gate = (grad_act * activated).astype(bf16)
    back_ref[...] = (
        dot_f32(grad_up, up_ref[...], 1, 1) + dot_f32(grad_gate, gate_ref[...], 1, 1)
    ).astype(bf16)
    grads_ref[:, :hidden] = dot_f32(rows, grad_up, 0, 0).astype(bf16)
    grads_ref[:, hidden : 2 * hidden] = dot_f32(rows, grad_gate, 0, 0).astype(bf16)
    grads_ref[:, 2 * hidden : 3 * hidden] = dot_f32(cot, hidden_act, 0, 0).astype(bf16)
    spare = grads_ref.shape[1] - 3 * hidden
    if spare:
        grads_ref[:, 3 * hidden :] = jnp.zeros((grads_ref.shape[0], spare), bf16)


def feed_forward(hidden, rows, up, gate, down_t, cot):
    row_count, width = rows.shape
    padded = -(-3 * hidden // 128) * 128
    return pl.pallas_call(
        functools.partial(feed_forward_kernel, hidden),
        out_shape=[
            jax.ShapeDtypeStruct((row_count, width), jnp.bfloat16),
            jax.ShapeDtypeStruct((row_count, width), jnp.bfloat16),
            jax.ShapeDtypeStruct((width, padded), jnp.bfloat16),
        ],
        in_specs=[pl.BlockSpec(memory_space=pltpu.VMEM)] * 5,
        out_specs=[pl.BlockSpec(memory_space=pltpu.VMEM)] * 3,
        compiler_params=pltpu.CompilerParams(vmem_limit_bytes=48 << 20),
    )(rows, up, gate, down_t, cot)


def body(sizes, tokens, attn_gain, w_qkv, w_out, mlp_gain, w_in, w_down, cotangent):
    bf16, f32 = jnp.bfloat16, jnp.float32
    groups, members = sizes["dp"], sizes["tensor"]
    block = w_qkv.shape[1]
    width = block * groups
    heads_wide, hidden = w_qkv.shape[2], w_in.shape[2]
    own_rows = tokens.shape[0]
    packed = jnp.concatenate([w_qkv[0], w_qkv[1], w_qkv[2], w_out.T], axis=1)
    gain_tile = jnp.pad(jnp.stack([attn_gain, mlp_gain]), [(0, 14), (0, -block % 128)])
    weights, gain_tiles, token_rows, grad_rows = exchange(
        sizes,
        0,
        ("relay", "dp", packed),
        ("relay", "dp", gain_tile),
        ("relay", "tensor", tokens),
        ("relay", "tensor", cotangent),
    )
    weights = weights.reshape(width, -1)
    qkv_weight = weights[:, : 3 * heads_wide]
    out_weight_t = weights[:, 3 * heads_wide :]
    attn_full = gain_tiles[:, 0, :block].reshape(1, width).astype(f32)
    mlp_full = gain_tiles[:, 1, :block].reshape(1, width).astype(f32)
    outer = groups // 2
    column = lax.rem(lax.axis_index("dp"), 2)

    def quarter(array):
        return array.reshape(outer, 2, block, -1)

    def half_sum(array, received, low, high):
        own = lax.dynamic_index_in_dim(quarter(array)[..., low:high], column, 1, keepdims=False)
        return (own.astype(f32) + received.astype(f32)).astype(bf16)

    row_count = own_rows * members
    grad_rows = grad_rows.reshape(row_count, width)
    residual = tokens.astype(f32)
    normed_one, inv_one = normalize(residual)
    rows_one = (normalize(token_rows.reshape(row_count, width).astype(f32))[0] * attn_full).astype(bf16)
    head_count = heads_wide // HD
    head_shape = (row_count, head_count, HD)
    seq_shape = (row_count // L, L, head_count, HD)
    flat_shape = (row_count, heads_wide)
    cos_table, sin_table = rope_tables(row_count)
    projected = dot_f32(rows_one, qkv_weight, 1, 0)
    pieces = [projected[:, i * heads_wide : (i + 1) * heads_wide].reshape(head_shape) for i in range(3)]
    queries = rotate(pieces[0], cos_table, sin_table).astype(bf16).reshape(seq_shape)
    key_rows = rotate(pieces[1], cos_table, sin_table).astype(bf16).reshape(seq_shape)
    value_rows = pieces[2].astype(bf16).reshape(seq_shape)
    one_seq = row_count == L

    def over_sequences(function, arrays):
        if one_seq:
            results = function(*[array[0] for array in arrays])
            return tuple(result[None] for result in results)
        return lax.map(lambda seq_block: function(*seq_block), arrays)

    attn_mix, log_total = over_sequences(attend, (queries, key_rows, value_rows))
    mixed_rows = attn_mix.reshape(flat_shape)
    attn_part = dot_f32(mixed_rows, out_weight_t, 1, 1).astype(bf16)
    attn_parts, up_weight, down_weight_t = exchange(
        sizes,
        1,
        ("scatter", "tensor", attn_part.reshape(members, own_rows, width)),
        ("relay", "dp", w_in[0]),
        ("relay", "dp", w_down.T),
    )
    up_weight = up_weight.reshape(width, -1)
    down_weight_t = down_weight_t.reshape(width, -1)
    hidden_res = residual + total_of(attn_parts)
    normed_two, inv_two = normalize(hidden_res)
    ln_two = (normed_two * mlp_full).astype(bf16)
    rows_two, gate_weight = exchange(
        sizes, 2, ("relay", "tensor", ln_two), ("relay", "dp", w_in[1])
    )
    gate_weight = gate_weight.reshape(width, -1)
    rows_two = rows_two.reshape(row_count, width)
    mlp_part, ln_two_part, mlp_grads = feed_forward(
        hidden, rows_two, up_weight, gate_weight, down_weight_t, grad_rows
    )
    mlp_wide = mlp_grads.shape[-1]
    first = mlp_wide // 256 * 128
    ln_two_parts, mlp_grads_a = exchange(
        sizes,
        3,
        ("scatter", "tensor", ln_two_part.reshape(members, own_rows, width)),
        ("half", "dp", quarter(mlp_grads), (0, first)),
    )
    grad_res_two, mlp_gain_part = normalize_back(total_of(ln_two_parts), normed_two, inv_two, mlp_full)
    grad_hidden = cotangent.astype(f32) + grad_res_two
    grad_hidden_rows, mlp_grads_b, mlp_sums_a = exchange(
        sizes,
        4,
        ("relay", "tensor", grad_hidden.astype(bf16)),
        ("half", "dp", quarter(mlp_grads), (first, mlp_wide)),
        ("outer", "dp", half_sum(mlp_grads, mlp_grads_a, 0, first)),
    )
    grad_hidden_rows = grad_hidden_rows.reshape(row_count, width)
    grad_out_t = row_major(dot_f32(grad_hidden_rows, mixed_rows, 0, 0).astype(bf16))
    grad_mix = dot_f32(grad_hidden_rows, out_weight_t, 1, 0).astype(bf16).reshape(seq_shape)
    grad_q, grad_k, grad_v = over_sequences(
        attend_back, (queries, key_rows, value_rows, attn_mix, grad_mix, log_total)
    )
    grad_proj = jnp.concatenate(
        [
            rotate_back(grad_q.reshape(head_shape), cos_table, sin_table).reshape(flat_shape),
            rotate_back(grad_k.reshape(head_shape), cos_table, sin_table).reshape(flat_shape),
            grad_v.reshape(flat_shape),
        ],
        axis=1,
    ).astype(bf16)
    grad_qkv = row_major(dot_f32(rows_one, grad_proj, 0, 0).astype(bf16))
    ln_one_part = dot_f32(grad_proj, qkv_weight, 1, 1).astype(bf16)
    ln_one_parts, mlp_sums_b, grad_out_half, qkv_half = exchange(
        sizes,
        5,
        ("scatter", "tensor", ln_one_part.reshape(members, own_rows, width)),
        ("outer", "dp", half_sum(mlp_grads, mlp_grads_b, first, mlp_wide)),
        ("half", "dp", quarter(grad_out_t)),
        ("half", "dp", quarter(grad_qkv)),
    )
    grad_res_one, attn_gain_part = normalize_back(total_of(ln_one_parts), normed_one, inv_one, attn_full)
    input_grad = grad_hidden + grad_res_one
    gain_parts = jnp.stack([attn_gain_part, mlp_gain_part] + [jnp.zeros_like(attn_gain_part)] * 6)
    gain_parts = pad_columns(jnp.swapaxes(gain_parts.reshape(8, groups, block), 0, 1))
    late_parts, gain_parts, mlp_parts, grad_out_parts = exchange(
        sizes,
        6,
        ("outer", "dp", half_sum(grad_qkv, qkv_half, 0, 3 * heads_wide)),
        ("scatter", "dp", gain_parts),
        ("scatter", "tensor", mlp_part.reshape(members, own_rows, width)),
        ("outer", "dp", half_sum(grad_out_t, grad_out_half, 0, heads_wide)),
    )
    output = (hidden_res + total_of(mlp_parts)).astype(bf16)
    (gain_groups,) = exchange(sizes, 7, ("gather", "tensor", total_of(gain_parts)))
    gain_sum = total_of(gain_groups)
    late = total_of(late_parts)
    grad_w_qkv = jnp.stack([late[:, i * heads_wide : (i + 1) * heads_wide] for i in range(3)])
    grad_w_out = total_of(grad_out_parts).T
    mlp_sums = jnp.concatenate(
        [total_of(mlp_sums_a), total_of(mlp_sums_b)], axis=1
    )
    grad_w_in = jnp.stack([mlp_sums[:, :hidden], mlp_sums[:, hidden : 2 * hidden]])
    grad_w_down = mlp_sums[:, 2 * hidden : 3 * hidden].T
    return (
        output,
        input_grad,
        gain_sum[0, :block],
        grad_w_qkv,
        grad_w_out,
        gain_sum[1, :block],
        grad_w_in,
        grad_w_down,
    )


def lanes(shape, dim):
    return lax.broadcasted_iota(jnp.int32, shape, dim)


def spread_matrix(head_count, turned, sign):
    shape = (head_count * HD, head_count * 2 * HD)
    row, column = lanes(shape, 0), lanes(shape, 1)
    head = lax.shift_right_logical(column, 7)
    feature = lax.bitwise_and(column, HD - 1)
    upper = lax.bitwise_and(column, 2 * HD - 1) >= HD
    plain = row == head * HD + feature
    if not turned:
        return jnp.where(plain & jnp.logical_not(upper), 1.0, 0.0).astype(jnp.bfloat16)
    other = row == head * HD + lax.bitwise_and(feature + HD // 2, HD - 1)
    signed = jnp.where(feature < HD // 2, -sign, sign)
    return jnp.where(
        upper, jnp.where(other, signed, 0.0), jnp.where(plain, 1.0, 0.0)
    ).astype(jnp.bfloat16)


def paired_matrix():
    shape = (2 * HD, 2 * HD)
    row, column = lanes(shape, 0), lanes(shape, 1)
    feature = lax.bitwise_and(column, HD - 1)
    upper = column >= HD
    other = row == lax.bitwise_and(feature + HD // 2, HD - 1)
    signed = jnp.where(feature < HD // 2, 1.0, -1.0)
    return jnp.where(
        upper, jnp.where(other, signed, 0.0), jnp.where(row == column, 1.0, 0.0)
    ).astype(jnp.bfloat16)


def layer_kernel(sizes, dims, *refs):
    bf16, f32 = jnp.bfloat16, jnp.float32
    groups, members = sizes["dp"], sizes["tensor"]
    own_rows, width, block, heads_wide, hidden, pad_hidden = dims
    head_count = heads_wide // HD
    spread = 2 * heads_wide
    side = -3 * heads_wide % 128
    row_count = own_rows * members
    outer, rings = groups // 2, members // 2
    (
        tok_in, cot_in, qkv_in, out_in, up_in, down_in, attn_in, mlp_in, table_in,
        output_ref, input_grad_ref, gain_ref, qkv_grad_ref, out_grad_ref, mlp_grad_ref,
        tok_buf, cot_buf, qkv_raw, out_raw, up_raw, down_raw, attn_raw, mlp_raw, table,
        w_a, w_b, w_c, gain_buf, gain_rows, w_big, w_out_pad, up_w, gate_w, down_w,
        rows_one, probs, q_buf, k_buf, v_buf, mix_t, mix, mix_pack,
        part_one, recv_one, fwd_one, hidden_res, rows_two,
        act_buf, up_grad, gate_grad, part_two, recv_two, fwd_two,
        part_three, recv_three, fwd_three,
        mlp_grads, mlp_half, mlp_sum, mlp_parts,
        grad_hidden, grad_rows, out_grads, out_half, out_sum, out_parts,
        proj_grad, qk_grads, qk_half, qk_sum, qk_parts,
        vo_grads, vo_half, vo_sum, vo_parts,
        part_four, recv_four, fwd_four, gain_send, gain_recv, gain_group,
        load_sem, send_sem, recv_sem,
    ) = refs
    me_d, me_t = lax.axis_index("dp"), lax.axis_index("tensor")
    zrow, col = me_d // 2, lax.rem(me_d, 2)
    x_peer = zrow * 2 + 1 - col
    yrow, core = me_t // 2, lax.rem(me_t, 2)
    c_peer = yrow * 2 + 1 - core
    counter = [0]
    sent = []

    def make(source, target, axis, peer):
        index = counter[0]
        counter[0] += 1
        return pltpu.make_async_remote_copy(
            src_ref=source,
            dst_ref=target,
            send_sem=send_sem.at[index],
            recv_sem=recv_sem.at[index],
            device_id={axis: peer},
            device_id_type=pl.DeviceIdType.MESH,
        )

    def send(source, target, axis, peer):
        copy = make(source, target, axis, peer)
        copy.start()
        sent.append((copy, None))
        return copy

    def begin(copy, condition):
        pl.when(condition)(copy.start)
        sent.append((copy, condition))

    cuts = 2 if block % 32 == 0 else 1
    height = block // cuts

    class Chain:
        def __init__(self, buffer):
            self.buffer = buffer
            self.moves = {}
            last = outer - 1
            for step in range(1, outer):
                for way in (0, 1):
                    ahead = 1 if way == 0 else outer - 1
                    target = lax.rem(zrow + ahead, outer) * 2 + col
                    back = step - 1 if way else outer - step + 1
                    carried = lax.rem(zrow + back, outer) * 2 + col
                    origin = lax.rem(zrow + (step if way else outer - step), outer) * 2
                    lands = zrow + step <= last if way else zrow >= step
                    starts = (
                        (zrow >= 1) & (zrow + step - 1 <= last)
                        if way
                        else (zrow < last) & (zrow >= step - 1)
                    )
                    for cut in range(cuts):
                        self.moves[step, way, cut] = (
                            make(self.piece(carried, cut), self.piece(carried, cut), "dp", target),
                            make(
                                self.piece(origin + col, cut),
                                self.piece(origin + col, cut),
                                "dp",
                                x_peer,
                            ),
                            starts,
                            lands,
                            origin,
                        )

        def piece(self, index, cut):
            return self.buffer.at[index, cut * height : (cut + 1) * height]

        def start(self):
            for cut in range(cuts):
                for way in (0, 1):
                    move, _, starts, _, _ = self.moves[1, way, cut]
                    begin(move, starts)

        def start_pair(self):
            self.own = []
            for cut in range(cuts):
                piece = self.piece(me_d, cut)
                self.own.append(send(piece, piece, "dp", x_peer))

        def step(self, number):
            for cut in range(cuts):
                for way in (0, 1):
                    move, across, _, lands, _ = self.moves[number, way, cut]
                    pl.when(lands)(move.wait_recv)
                    if number + 1 < outer:
                        onward, _, starts, _, _ = self.moves[number + 1, way, cut]
                        begin(onward, starts)
                    begin(across, lands)

        def paired(self, number, then=None):
            for way in (0, 1):
                lands, origin = self.moves[number, way, 0][3:]

                @pl.when(lands)
                def _():
                    for cut in range(cuts):
                        self.moves[number, way, cut][1].wait_recv()
                    if then is not None:
                        then(origin + 1 - col)

    loads = [
        pltpu.make_async_copy(source, target, load_sem.at[index])
        for index, (source, target) in enumerate(
            [
                (qkv_in, qkv_raw), (out_in, out_raw), (attn_in, attn_raw), (mlp_in, mlp_raw),
                (tok_in, tok_buf.at[me_t]), (cot_in, cot_buf.at[me_t]),
                (up_in, up_raw), (down_in, down_raw), (table_in, table),
            ]
        )
    ]
    for load in loads:
        load.start()
    barrier = pltpu.get_barrier_semaphore()
    for axis, me in (("dp", me_d), ("tensor", me_t)):
        for shift in range(1, sizes[axis]):
            pl.semaphore_signal(
                barrier,
                inc=1,
                device_id={axis: lax.rem(me + shift, sizes[axis])},
                device_id_type=pl.DeviceIdType.MESH,
            )
    eye_heads = jnp.where(
        lanes((heads_wide, heads_wide), 0) == lanes((heads_wide, heads_wide), 1), 1.0, 0.0
    ).astype(bf16)
    for load in loads[:4]:
        load.wait()
    gain_buf[me_d] = jnp.zeros(gain_buf.shape[1:], bf16)
    gain_buf[me_d, 0:1, :block] = attn_raw[...]
    gain_buf[me_d, 8:9, :block] = mlp_raw[...]
    for which in range(3):
        w_a[me_d, :, which * heads_wide : (which + 1) * heads_wide] = qkv_raw[which]
    out_turned = dot_f32(out_raw[...], eye_heads, 0, 0).astype(bf16)
    if side:
        w_a[me_d, :, 3 * heads_wide :] = out_turned[:, :side]
    w_c[me_d] = out_turned[:, side:]
    pl.semaphore_wait(barrier, groups + members - 2)

    def dp_spread(buffer):
        copies = []
        for shift in range(1, outer):
            peer = lax.rem(zrow + shift, outer) * 2 + col
            origin = lax.rem(zrow + outer - shift, outer) * 2 + col
            copies.append((send(buffer.at[me_d], buffer.at[me_d], "dp", peer), origin))
        return copies

    def dp_pair(buffer, origin):
        mirrored = origin // 2 * 2 + 1 - col
        return (send(buffer.at[origin], buffer.at[origin], "dp", x_peer), mirrored)

    def tensor_spread(buffer, span=slice(0, own_rows)):
        copies = []
        own = buffer.at[me_t, span]
        for shift in range(1, rings):
            peer = lax.rem(yrow + shift, rings) * 2 + core
            origin = lax.rem(yrow + rings - shift, rings) * 2 + core
            copies.append((send(own, own, "tensor", peer), origin))
        near = send(own, own, "tensor", c_peer)
        return copies, near

    def tensor_relay(buffer, copies, span=slice(0, own_rows)):
        onward = []
        for copy, origin in copies:
            copy.wait_recv()
            piece = buffer.at[origin, span]
            onward.append(send(piece, piece, "tensor", c_peer))
        return onward

    gain_z = dp_spread(gain_buf)
    gain_x = [dp_pair(gain_buf, me_d)]
    chain_a = Chain(w_a)
    chain_a.start()
    chain_a.start_pair()
    for load in loads[4:6]:
        load.wait()
    tok_y, tok_near = tensor_spread(tok_buf)
    cot_y, cot_near = tensor_spread(cot_buf)
    for load in loads[6:]:
        load.wait()
    eye_hidden = jnp.where(
        lanes((hidden, hidden), 0) == lanes((hidden, hidden), 1), 1.0, 0.0
    ).astype(bf16)
    for which in range(2):
        w_b[me_d, :, which * hidden : (which + 1) * hidden] = up_raw[which]
    w_b[me_d, :, 2 * hidden : 3 * hidden] = dot_f32(down_raw[...], eye_hidden, 0, 0).astype(bf16)
    if pad_hidden > 3 * hidden:
        w_b[me_d, :, 3 * hidden :] = jnp.zeros((block, pad_hidden - 3 * hidden), bf16)
    chain_b = Chain(w_b)

    turn = spread_matrix(head_count, True, 1.0)
    plain = spread_matrix(head_count, False, 1.0)

    def expand(index):
        for which, matrix in ((0, turn), (1, turn), (2, plain)):
            piece = w_a[index, :, which * heads_wide : (which + 1) * heads_wide]
            w_big[index, :, which * spread : (which + 1) * spread] = dot_f32(
                piece, matrix, 1, 0
            ).astype(bf16)

    def expand_out():
        value = dot_f32(
            w_c[...].reshape(width, heads_wide - side), plain[side:], 1, 0
        )
        if side:
            head_piece = w_a[:, :, 3 * heads_wide :].reshape(width, side)
            value = value + dot_f32(head_piece, plain[:side], 1, 0)
        w_out_pad[...] = value.astype(bf16).reshape(groups, block, spread)

    expand(me_d)
    chain_a.step(1)
    for copy, origin in gain_z:
        copy.wait_recv()
        gain_x.append(dp_pair(gain_buf, origin))
    tok_far = tensor_relay(tok_buf, tok_y)
    for number in range(2, outer - 1):
        chain_a.step(number)
    c_z = dp_spread(w_c)
    chain_b.start()
    for copy, _ in gain_x:
        copy.wait_recv()
    for index in range(groups):
        tile = gain_buf[index].astype(f32)
        gain_rows[0:1, index * block : (index + 1) * block] = tile[0:1, :block]
        gain_rows[8:9, index * block : (index + 1) * block] = tile[8:9, :block]
    attn_gain, mlp_gain = gain_rows[0:1, :], gain_rows[8:9, :]
    tok_near.wait_recv()
    for copy in tok_far:
        copy.wait_recv()
    all_rows = tok_buf[...].reshape(row_count, width).astype(f32)
    rows_one[...] = (normalize(all_rows)[0] * attn_gain).astype(bf16)
    if outer > 2:
        chain_a.step(outer - 1)
    c_x = [dp_pair(w_c, me_d)]
    cot_far = tensor_relay(cot_buf, cot_y)
    for shift in range(1, outer):
        expand(lax.rem(zrow + shift, outer) * 2 + col)
    for copy, origin in c_z:
        copy.wait_recv()
        c_x.append(dp_pair(w_c, origin))
    chain_b.start_pair()
    for copy in chain_a.own:
        copy.wait_recv()
    expand(x_peer)
    for number in range(1, outer):
        chain_a.paired(number, expand)

    chain_b.step(1)
    paired = paired_matrix()
    rotary = table[...]
    for which in range(3):
        weight = w_big[:, :, which * spread : (which + 1) * spread].reshape(width, spread)
        projected = dot_f32(rows_one[...], weight, 1, 0)
        for head in range(head_count):
            piece = projected[:, head * 128 : (head + 1) * 128]
            if which == 2:
                v_buf[head] = piece.astype(bf16)
                continue
            turned = piece * rotary
            turned = (turned + pltpu.roll(turned, 64, 1)).astype(bf16)
            (q_buf, k_buf)[which][head] = turned
    for head in range(head_count):
        scores = dot_f32(k_buf[head], q_buf[head], 1, 1) * (0.5 * HD ** (-0.5))
        peak = jnp.max(scores, axis=0, keepdims=True)
        powers = jnp.exp(scores - peak)
        share = powers * (1.0 / jnp.sum(powers, axis=0, keepdims=True))
        probs[head] = share
        mixed_t = dot_f32(v_buf[head], share.astype(bf16), 0, 0).astype(bf16)
        mix_t[head] = mixed_t
        mixed = jnp.transpose(mixed_t.astype(f32)).astype(bf16)
        mix[:, :, head * 128 : (head + 1) * 128] = mixed.reshape(members, own_rows, 128)
        mix_pack[:, head * HD : (head + 1) * HD] = mixed[:, :HD]

    every = slice(0, own_rows)
    if own_rows % 32 == 0:
        spans = (slice(0, own_rows // 2), slice(own_rows // 2, own_rows))
    else:
        spans = (every,)

    def reduce_far(part, recv, span=every):
        first = []
        for shift in range(1, rings):
            far = lax.rem(yrow + shift, rings)
            first.append(
                send(part.at[far * 2 + 1 - core, span], recv.at[shift, span], "tensor", c_peer)
            )
        return first

    def reduce_near(part, recv, span=every):
        return send(part.at[c_peer, span], recv.at[0, span], "tensor", c_peer)

    def reduce_middle(part, recv, fwd, first, span=every):
        second = []
        for shift in range(1, rings):
            far = lax.rem(yrow + shift, rings)
            first[shift - 1].wait_recv()
            fwd[shift, span] = (
                part[far * 2 + core, span].astype(f32) + recv[shift, span].astype(f32)
            ).astype(bf16)
            second.append(
                send(
                    fwd.at[shift, span],
                    recv.at[rings + shift, span],
                    "tensor",
                    far * 2 + core,
                )
            )
        return second

    def reduce_finish(part, recv, near, second, span=every):
        near.wait_recv()
        total = part[me_t, span].astype(f32) + recv[0, span].astype(f32)
        for shift in range(1, rings):
            second[shift - 1].wait_recv()
            total = total + recv[rings + shift, span].astype(f32)
        return total

    def project(part, ring, left, right):
        part[pl.ds(2 * ring, 2)] = (
            dot_f32(left, right, 1, 1).astype(bf16).reshape(2, own_rows, width)
        )

    for copy, _ in c_x:
        copy.wait_recv()
    expand_out()
    out_weight = w_out_pad[...].reshape(width, spread)

    def mixed_ring(ring):
        return mix[pl.ds(2 * ring, 2)].reshape(2 * own_rows, spread)

    for shift in range(1, rings):
        far = lax.rem(yrow + shift, rings)
        project(part_one, far, mixed_ring(far), out_weight)
    first_one = [reduce_far(part_one, recv_one, span) for span in spans]
    for number in range(2, outer - 1):
        chain_b.step(number)
    project(part_one, yrow, mixed_ring(yrow), out_weight)
    near_one = [reduce_near(part_one, recv_one, span) for span in spans]
    second_one = [
        reduce_middle(part_one, recv_one, fwd_one, first, span)
        for first, span in zip(first_one, spans)
    ]
    for head in range(head_count):
        q_buf[head] = dot_f32(q_buf[head], paired, 1, 0).astype(bf16)
        k_buf[head] = dot_f32(k_buf[head], paired, 1, 0).astype(bf16)
    if outer > 2:
        chain_b.step(outer - 1)
    rows_y, rows_near = [], []
    for index, span in enumerate(spans):
        residual = tok_buf[me_t, span].astype(f32)
        hidden_res[span] = residual + reduce_finish(
            part_one, recv_one, near_one[index], second_one[index], span
        )
        normed_two = normalize(hidden_res[span])[0]
        rows_two[me_t, span] = (normed_two * mlp_gain).astype(bf16)
        far_copies, near_copy = tensor_spread(rows_two, span)
        rows_y.append(far_copies)
        rows_near.append(near_copy)
    cot_near.wait_recv()
    for copy in cot_far:
        copy.wait_recv()
    for copy in chain_b.own:
        copy.wait_recv()
    for number in range(1, outer):
        chain_b.paired(number)
    up_w[...] = w_b[:, :, :hidden].reshape(width, hidden)
    gate_w[...] = w_b[:, :, hidden : 2 * hidden].reshape(width, hidden)
    down_w[...] = w_b[:, :, 2 * hidden : 3 * hidden].reshape(width, hidden)

    def feed(ring):
        base = 2 * ring
        count = 2 * own_rows
        rows = rows_two[pl.ds(base, 2)].reshape(count, width)
        cot = cot_buf[pl.ds(base, 2)].reshape(count, width)
        inputs = dot_f32(rows, up_w[...], 1, 0)
        gate_part = dot_f32(rows, gate_w[...], 1, 0)
        grad_act = dot_f32(cot, down_w[...], 1, 0)
        activated, slope = gelu_pair(inputs)
        act_buf[ring] = (activated * gate_part).astype(bf16)
        grad_up = (grad_act * gate_part * slope).astype(bf16)
        grad_gate = (grad_act * activated).astype(bf16)
        up_grad[ring] = grad_up
        gate_grad[ring] = grad_gate
        part_two[pl.ds(base, 2)] = (
            (dot_f32(grad_up, up_w[...], 1, 1) + dot_f32(grad_gate, gate_w[...], 1, 1))
            .astype(bf16)
            .reshape(2, own_rows, width)
        )

    for copy in rows_near:
        copy.wait_recv()
    feed(yrow)
    rows_far = []
    for copies, span in zip(rows_y, spans):
        rows_far += tensor_relay(rows_two, copies, span)
    for copy in rows_far:
        copy.wait_recv()
    for shift in range(1, rings):
        feed(lax.rem(yrow + shift, rings))
    first_two = reduce_far(part_two, recv_two)
    near_two = reduce_near(part_two, recv_two)

    staged = outer == 4
    beside = zrow // 2 * 2 + 1 - lax.rem(zrow, 2)
    if staged:
        across_z = lax.rem(zrow + 2, outer)
        targets = [lax.rem(beside + 2, outer), across_z, beside, zrow]
    else:
        targets = [lax.rem(zrow + shift, outer) for shift in range(1, outer + 1)]

    def pair_start(grads, half):
        return [
            (send(grads.at[row * 2 + 1 - col], half.at[row], "dp", x_peer), row)
            for row in targets
        ]

    def pair_step(state, number):
        grads, half, sums, parts, copies, moved = state
        copy, row = copies[number]
        copy.wait_recv()
        value = grads[row * 2 + col].astype(f32) + half[row].astype(f32)
        if number == outer - 1:
            for copy in moved[1:] if staged else moved:
                copy.wait_recv()
            if not staged:
                parts[zrow] = jnp.zeros(parts.shape[1:], bf16)
            arrived = parts[1 : outer - 1] if staged else parts[...]
            return value + jnp.sum(arrived.astype(f32), axis=0)
        if not staged:
            sums[row] = value.astype(bf16)
            moved.append(send(sums.at[row], parts.at[zrow], "dp", row * 2 + col))
            return None
        if number == 1:
            moved[0].wait_recv()
            value = value + parts[0].astype(f32)
        sums[number] = value.astype(bf16)
        target, place = ((beside, 0), (across_z, 1), (beside, 2))[number]
        moved.append(send(sums.at[number], parts.at[place], "dp", target * 2 + col))
        return None

    full_rows = rows_two[...].reshape(row_count, width)
    full_cot = cot_buf[...].reshape(row_count, width)
    for which, grad in ((0, up_grad), (1, gate_grad)):
        mlp_grads[:, :, which * hidden : (which + 1) * hidden] = (
            dot_f32(full_rows, grad[...].reshape(row_count, hidden), 0, 0)
            .astype(bf16)
            .reshape(groups, block, hidden)
        )
    full_act = act_buf[...].reshape(row_count, hidden)
    mlp_grads[:, :, 2 * hidden : 3 * hidden] = (
        dot_f32(full_cot, full_act, 0, 0).astype(bf16).reshape(groups, block, hidden)
    )
    if pad_hidden > 3 * hidden:
        mlp_grads[:, :, 3 * hidden :] = jnp.zeros(
            (groups, block, pad_hidden - 3 * hidden), bf16
        )
    mlp_pairs = pair_start(mlp_grads, mlp_half)
    second_two = reduce_middle(part_two, recv_two, fwd_two, first_two)
    part_three[...] = (
        dot_f32(full_act, down_w[...], 1, 1).astype(bf16).reshape(members, own_rows, width)
    )
    normed_two, inv_two = normalize(hidden_res[...])
    mlp_state = (mlp_grads, mlp_half, mlp_sum, mlp_parts, mlp_pairs, [])
    pair_step(mlp_state, 0)
    back_two = reduce_finish(part_two, recv_two, near_two, second_two)
    grad_res, mlp_gain_part = normalize_back(back_two, normed_two, inv_two, mlp_gain)
    grad_hidden[...] = cot_buf[me_t].astype(f32) + grad_res
    grad_rows[me_t] = grad_hidden[...].astype(bf16)
    grad_y, grad_near = tensor_spread(grad_rows)
    first_three = reduce_far(part_three, recv_three)
    near_three = reduce_near(part_three, recv_three)
    for number in range(1, min(2, outer - 1)):
        pair_step(mlp_state, number)
    grad_far = tensor_relay(grad_rows, grad_y)
    second_three = reduce_middle(part_three, recv_three, fwd_three, first_three)
    grad_near.wait_recv()
    for copy in grad_far:
        copy.wait_recv()
    full_grad = grad_rows[...].reshape(row_count, width)
    grad_mix = dot_f32(full_grad, out_weight, 1, 0).astype(bf16)
    out_product = dot_f32(full_grad, mix_pack[...], 0, 0).astype(bf16)
    if side:
        vo_grads[:, :, heads_wide:] = out_product[:, :side].reshape(groups, block, side)
    out_grads[...] = out_product[:, side:].reshape(groups, block, heads_wide - side)
    out_pairs = pair_start(out_grads, out_half)
    for number in range(2, outer - 1):
        pair_step(mlp_state, number)
    scale = HD ** (-0.5)
    for head in range(head_count):
        grad_head = grad_mix[:, head * 128 : (head + 1) * 128]
        grad_head_t = jnp.transpose(grad_head.astype(f32))
        delta = jnp.sum(grad_head_t * mix_t[head].astype(f32), axis=0, keepdims=True)
        grad_probs = dot_f32(v_buf[head], grad_head, 1, 1)
        share = probs[head]
        grad_scores = (share * (grad_probs - delta)).astype(bf16)
        grad_v = dot_f32(share.astype(bf16), grad_head, 1, 0)
        grad_k = dot_f32(grad_scores, q_buf[head], 1, 0) * (rotary * scale)
        grad_k = grad_k + pltpu.roll(grad_k, 64, 1)
        grad_q = jnp.transpose(dot_f32(k_buf[head], grad_scores, 0, 0)) * (rotary * scale)
        grad_q = grad_q + pltpu.roll(grad_q, 64, 1)
        for which, value in enumerate((grad_q, grad_k, grad_v)):
            start = which * heads_wide + head * HD
            proj_grad[:, start : start + HD] = value[:, :HD].astype(bf16)
    qk_grads[...] = (
        dot_f32(rows_one[...], proj_grad[:, : 2 * heads_wide], 0, 0)
        .astype(bf16)
        .reshape(groups, block, 2 * heads_wide)
    )
    qk_pairs = pair_start(qk_grads, qk_half)
    vo_grads[:, :, :heads_wide] = (
        dot_f32(rows_one[...], proj_grad[:, 2 * heads_wide :], 0, 0)
        .astype(bf16)
        .reshape(groups, block, heads_wide)
    )
    vo_pairs = pair_start(vo_grads, vo_half)
    out_state = (out_grads, out_half, out_sum, out_parts, out_pairs, [])
    pair_step(out_state, 0)
    qkv_weight = w_a[:, :, : 3 * heads_wide].reshape(width, 3 * heads_wide)

    def grad_ring(ring):
        return proj_grad[pl.ds(pl.multiple_of(ring * 2 * own_rows, 2 * own_rows), 2 * own_rows)]

    for shift in range(1, rings):
        far = lax.rem(yrow + shift, rings)
        project(part_four, far, grad_ring(far), qkv_weight)
    first_four = reduce_far(part_four, recv_four)
    project(part_four, yrow, grad_ring(yrow), qkv_weight)
    near_four = reduce_near(part_four, recv_four)
    second_four = reduce_middle(part_four, recv_four, fwd_four, first_four)

    def total(parts, across):
        for copy in across:
            copy.wait_recv()
        return jnp.sum(parts[...].astype(f32), axis=0)

    qk_state = (qk_grads, qk_half, qk_sum, qk_parts, qk_pairs, [])
    vo_state = (vo_grads, vo_half, vo_sum, vo_parts, vo_pairs, [])
    pair_step(qk_state, 0)
    for number in range(1, outer - 1):
        pair_step(out_state, number)
    mlp_out = reduce_finish(part_three, recv_three, near_three, second_three)
    output_ref[...] = (hidden_res[...] + mlp_out).astype(bf16)
    mlp_grad_ref[...] = pair_step(mlp_state, outer - 1)
    for number in range(1, min(2, outer - 1)):
        pair_step(qk_state, number)
    residual = tok_buf[me_t].astype(f32)
    normed_one, inv_one = normalize(residual)
    back_one = reduce_finish(part_four, recv_four, near_four, second_four)
    grad_res, attn_gain_part = normalize_back(back_one, normed_one, inv_one, attn_gain)
    input_grad_ref[...] = grad_hidden[...] + grad_res
    gain_send[...] = jnp.zeros(gain_send.shape, f32)
    attn_row = attn_gain_part.reshape(1, width)
    mlp_row = mlp_gain_part.reshape(1, width)
    for index in range(groups):
        gain_send[index, 0:1, :block] = attn_row[:, index * block : (index + 1) * block]
        gain_send[index, 1:2, :block] = mlp_row[:, index * block : (index + 1) * block]
    gain_recv[me_d] = gain_send[me_d]
    gain_copies = []
    for shift in range(1, groups):
        peer = lax.rem(me_d + shift, groups)
        gain_copies.append(send(gain_send.at[peer], gain_recv.at[me_d], "dp", peer))
    for number in range(2, outer - 1):
        pair_step(qk_state, number)
    for number in range(outer - 1):
        pair_step(vo_state, number)
    gain_group[me_t] = total(gain_recv, gain_copies)
    gain_copies = []
    for shift in range(1, members):
        peer = lax.rem(me_t + shift, members)
        gain_copies.append(send(gain_group.at[me_t], gain_group.at[me_t], "tensor", peer))
    out_grad_ref[...] = pair_step(out_state, outer - 1)
    qkv_grad_ref[:, : 2 * heads_wide] = pair_step(qk_state, outer - 1)
    qkv_grad_ref[:, 2 * heads_wide :] = pair_step(vo_state, outer - 1)
    gain_ref[...] = total(gain_group, gain_copies)
    for copy, condition in sent:
        if condition is None:
            copy.wait_send()
        else:
            pl.when(condition)(copy.wait_send)


def rotary_table(row_count):
    position = (np.arange(row_count) % L).astype(np.float32)
    halves = np.arange(HD // 2).astype(np.float32)
    inverse = np.float32(ROPE_THETA) ** (np.float32(-2.0) * halves / np.float32(HD))
    angles = position[:, None] * inverse[None, :]
    return np.concatenate([np.cos(angles)] * 2 + [np.sin(angles)] * 2, axis=1).astype(np.float32)


def whole_layer(sizes, tokens, attn_gain, w_qkv, w_out, mlp_gain, w_in, w_down, cotangent):
    bf16, f32 = jnp.bfloat16, jnp.float32
    groups, members = sizes["dp"], sizes["tensor"]
    own_rows, width = tokens.shape
    block, heads_wide, hidden = w_qkv.shape[1], w_qkv.shape[2], w_in.shape[2]
    pad_hidden = -(-3 * hidden // 128) * 128
    row_count = own_rows * members
    head_count, spread = heads_wide // HD, 2 * heads_wide
    side = -3 * heads_wide % 128
    outer, rings = groups // 2, members // 2
    vmem = pltpu.VMEM
    parts = vmem((members, own_rows, width), bf16)
    arrived = vmem((2 * rings, own_rows, width), bf16)
    passed = vmem((rings, own_rows, width), bf16)
    heads = vmem((head_count, row_count, 128), bf16)
    ringed = vmem((rings, 2 * own_rows, hidden), bf16)

    def exchanged(wide):
        quarter = vmem((outer, block, wide), bf16)
        return [vmem((groups, block, wide), bf16), quarter, quarter, quarter]

    scratch = [
        parts, parts,
        vmem(w_qkv.shape, bf16), vmem(w_out.shape, bf16),
        vmem(w_in.shape, bf16), vmem(w_down.shape, bf16),
        vmem((1, block), bf16), vmem((1, block), bf16), vmem((row_count, 2 * HD), f32),
        vmem((groups, block, 3 * heads_wide + side), bf16),
        vmem((groups, block, pad_hidden), bf16),
        vmem((groups, block, heads_wide - side), bf16),
        vmem((groups, 16, 128), bf16),
        vmem((16, width), f32),
        vmem((groups, block, 3 * spread), bf16),
        vmem((groups, block, spread), bf16),
        vmem((width, hidden), bf16), vmem((width, hidden), bf16), vmem((width, hidden), bf16),
        vmem((row_count, width), bf16),
        vmem((head_count, row_count, row_count), f32),
        heads, heads, heads,
        vmem((head_count, 128, row_count), bf16),
        vmem((members, own_rows, spread), bf16),
        vmem((row_count, heads_wide), bf16),
        parts, arrived, passed,
        vmem((own_rows, width), f32),
        parts,
        ringed, ringed, ringed,
        parts, arrived, passed,
        parts, arrived, passed,
        *exchanged(pad_hidden),
        vmem((own_rows, width), f32),
        parts,
        *exchanged(heads_wide - side),
        vmem((row_count, 3 * heads_wide), bf16),
        *exchanged(2 * heads_wide),
        *exchanged(heads_wide + side),
        parts, arrived, passed,
        vmem((groups, 8, 128), f32), vmem((groups, 8, 128), f32), vmem((members, 8, 128), f32),
    ]
    cuts = 2 if block % 32 == 0 else 1
    chains = 2 * cuts * (4 * (outer - 1) + 1)
    halves = 2 if own_rows % 32 == 0 else 1
    gathers = 2 * (2 * outer - 1) + chains + (3 + halves) * (2 * rings - 1)
    reduces = (3 + halves) * (2 * rings - 1) + 4 * (2 * outer - 1)
    slots = gathers + reduces + groups + members - 2
    dims = (own_rows, width, block, heads_wide, hidden, pad_hidden)
    output, input_grad, gains, qkv_sum, out_sum, mlp_sums = pl.pallas_call(
        functools.partial(layer_kernel, sizes, dims),
        out_shape=[
            jax.ShapeDtypeStruct((own_rows, width), bf16),
            jax.ShapeDtypeStruct((own_rows, width), f32),
            jax.ShapeDtypeStruct((8, 128), f32),
            jax.ShapeDtypeStruct((block, 3 * heads_wide + side), f32),
            jax.ShapeDtypeStruct((block, heads_wide - side), f32),
            jax.ShapeDtypeStruct((block, pad_hidden), f32),
        ],
        in_specs=[pl.BlockSpec(memory_space=pltpu.HBM)] * 9,
        out_specs=[pl.BlockSpec(memory_space=pltpu.VMEM)] * 6,
        scratch_shapes=scratch
        + [
            pltpu.SemaphoreType.DMA((9,)),
            pltpu.SemaphoreType.DMA((slots,)),
            pltpu.SemaphoreType.DMA((slots,)),
        ],
        compiler_params=pltpu.CompilerParams(
            collective_id=0, has_side_effects=True, vmem_limit_bytes=44 << 20
        ),
    )(
        *[
            pltpu.with_memory_space_constraint(array, pltpu.HBM)
            for array in (
                tokens, cotangent, w_qkv, w_out, w_in, w_down,
                attn_gain.reshape(1, block), mlp_gain.reshape(1, block),
                jnp.asarray(rotary_table(row_count)),
            )
        ]
    )
    results = pl.pallas_call(
        functools.partial(finish_kernel, hidden),
        out_shape=[
            jax.ShapeDtypeStruct(output.shape, bf16),
            jax.ShapeDtypeStruct(input_grad.shape, f32),
            jax.ShapeDtypeStruct(w_qkv.shape, f32),
            jax.ShapeDtypeStruct(w_out.shape, f32),
            jax.ShapeDtypeStruct(w_in.shape, f32),
            jax.ShapeDtypeStruct(w_down.shape, f32),
            jax.ShapeDtypeStruct((1, block), f32),
            jax.ShapeDtypeStruct((1, block), f32),
        ],
        in_specs=[pl.BlockSpec(memory_space=pltpu.VMEM)] * 6,
        out_specs=[pl.BlockSpec(memory_space=pltpu.HBM)] * 8,
        scratch_shapes=[
            vmem(w_qkv.shape, f32),
            vmem(w_out.shape, f32),
            vmem(w_in.shape, f32),
            vmem(w_down.shape, f32),
            vmem((1, block), f32),
            vmem((1, block), f32),
            pltpu.SemaphoreType.DMA((8,)),
        ],
        compiler_params=pltpu.CompilerParams(vmem_limit_bytes=16 << 20),
    )(output, input_grad, qkv_sum, out_sum, mlp_sums, gains)
    output, input_grad, grad_w_qkv, grad_w_out, grad_w_in, grad_w_down = results[:6]
    return (
        output,
        input_grad,
        results[6].reshape(block),
        grad_w_qkv,
        grad_w_out,
        results[7].reshape(block),
        grad_w_in,
        grad_w_down,
    )


def finish_kernel(hidden, *refs):
    (
        output, input_grad, qkv_sum, out_sum, mlp_sums, gains,
        output_to, input_grad_to, qkv_to, out_to, up_to, down_to, attn_to, mlp_to,
        qkv_buf, out_buf, up_buf, down_buf, attn_buf, mlp_buf, sems,
    ) = refs
    started = []

    def put(source, target):
        copy = pltpu.make_async_copy(source, target, sems.at[len(started)])
        copy.start()
        started.append(copy)

    put(output, output_to)
    put(input_grad, input_grad_to)
    attn_buf[...] = gains[0:1, : attn_buf.shape[1]]
    put(attn_buf, attn_to)
    mlp_buf[...] = gains[1:2, : mlp_buf.shape[1]]
    put(mlp_buf, mlp_to)
    heads_wide = out_buf.shape[0]
    side = heads_wide - out_sum.shape[1]
    for which in range(3):
        qkv_buf[which] = qkv_sum[:, which * heads_wide : (which + 1) * heads_wide]
    put(qkv_buf, qkv_to)
    for which in range(2):
        up_buf[which] = mlp_sums[:, which * hidden : (which + 1) * hidden]
    put(up_buf, up_to)
    if side:
        out_buf[:side] = jnp.transpose(qkv_sum[:, 3 * heads_wide :])
    out_buf[side:] = jnp.transpose(out_sum[...])
    put(out_buf, out_to)
    down_buf[...] = jnp.transpose(mlp_sums[:, 2 * hidden : 3 * hidden])
    put(down_buf, down_to)
    for copy in started:
        copy.wait()


def fits_whole(sizes, tokens, w_qkv):
    row_count = tokens.shape[0] * sizes["tensor"]
    even = sizes["dp"] % 2 == 0 and sizes["tensor"] % 2 == 0
    tiled = w_qkv.shape[1] % 16 == 0 and tokens.shape[0] % 16 == 0
    narrow = -3 * w_qkv.shape[2] % 128 < w_qkv.shape[2] and w_qkv.shape[1] <= 128
    return even and tiled and row_count == L and narrow


def layer(sizes, tokens, attn_gain, w_qkv, *rest):
    run = whole_layer if fits_whole(sizes, tokens, w_qkv) else body
    return run(sizes, tokens, attn_gain, w_qkv, *rest)


def solution(mesh):
    in_specs = (
        P(("dp", "tensor"), None),
        P("dp"),
        P(None, "dp", "tensor"),
        P("tensor", "dp"),
        P("dp"),
        P(None, "dp", "tensor"),
        P("tensor", "dp"),
        P(("dp", "tensor"), None),
    )
    out_specs = (
        P(("dp", "tensor"), None),
        P(("dp", "tensor"), None),
        P("dp"),
        P(None, "dp", "tensor"),
        P("tensor", "dp"),
        P("dp"),
        P(None, "dp", "tensor"),
        P("tensor", "dp"),
    )
    sizes = {axis: mesh.shape[axis] for axis in ("dp", "tensor")}
    return jax.shard_map(functools.partial(layer, sizes), mesh=mesh, in_specs=in_specs, out_specs=out_specs, check_vma=False)
```
